32 devices in a mesh: dp: 8 (over y, x, core), tensor: 4 (over z).
Axes of the slice: x: 2, y: 2, z: 4, core: 2. Of those that a mesh axis runs over, the one named last changes fastest.
Arguments:
- activations: bfloat16 [16, 1024, 1024], P('dp', 'tensor'), may hold values from -6 to 6
- cotangent: bfloat16 [16, 1024, 1024], P('dp', 'tensor'), may hold values from -6 to 6
- attn_gain: float32 [1024], replicated, may hold values from 0.5 to 1.5
- attn_shift: float32 [1024], replicated, may hold values from -2 to 2
- qkv_weight: bfloat16 [1024, 3072], P('dp', 'tensor'), may hold values from -0.1875 to 0.1875
- qkv_bias: float32 [3072], P('tensor'), may hold values from -3 to 3
- out_weight: bfloat16 [1024, 1024], P('dp', 'tensor'), may hold values from -3.5 to 3.5
- out_bias: float32 [1024], replicated, may hold values from -2 to 2
- mlp_gain: float32 [1024], replicated, may hold values from 0.5 to 1.5
- mlp_shift: float32 [1024], replicated, may hold values from -2 to 2
- fc1_weight: bfloat16 [1024, 4096], P('dp', 'tensor'), may hold values from -0.1875 to 0.1875
- fc1_bias: float32 [4096], P('tensor'), may hold values from -3 to 3
- fc2_weight: bfloat16 [1024, 4096], P('dp', 'tensor'), may hold values from -0.09375 to 0.09375
- fc2_bias: float32 [1024], replicated, may hold values from -2 to 2
Outputs:
- output: bfloat16 [16, 1024, 1024], P('dp', 'tensor')
- input_grad: float32 [16, 1024, 1024], P('dp', 'tensor')
- grad_attn_gain: float32 [1024], replicated
- grad_attn_shift: float32 [1024], replicated
- grad_qkv_weight: float32 [1024, 3072], P('dp', 'tensor')
- grad_qkv_bias: float32 [3072], P('tensor')
- grad_out_weight: float32 [1024, 1024], P('dp', 'tensor')
- grad_out_bias: float32 [1024], replicated
- grad_mlp_gain: float32 [1024], replicated
- grad_mlp_shift: float32 [1024], replicated
- grad_fc1_weight: float32 [1024, 4096], P('dp', 'tensor')
- grad_fc1_bias: float32 [4096], P('tensor')
- grad_fc2_weight: float32 [1024, 4096], P('dp', 'tensor')
- grad_fc2_bias: float32 [1024], replicated
The draws below stay inside these ranges and needn't reach their ends.
All inputs are finite; a program needn't handle non-finite values.
Results may differ from the reference program's by a relative error of at most 0.02.
Values may be sent and summed in bfloat16 or wider, within the bound.
No kernel may reach another device: no remote copies, remote signals or barrier semaphores. Data moves between devices by JAX's collectives and lax.ppermute only.
A program may use at most 192 MiB of HBM per device.

```python
import math
import jax
import jax.numpy as jnp
from jax import lax

D = 1024
H = 16
HD = 64
FF = 4096
GRID = 16
LEN = 1024
CLIPS = 16
QBLK = 512


def shard_levels(rng, extent, cuts, least, largest):
    loudness, own = 1.0, jax.random.fold_in(rng, 6)
    for dim, parts in cuts:
        heights = jnp.exp(jax.random.uniform(jax.random.fold_in(own, dim), (parts,), jnp.float32, least / len(cuts), largest / len(cuts)))
        loudness = loudness * jnp.repeat(heights, extent[dim] // parts).reshape([-1 if axis == dim else 1 for axis in range(len(extent))])
    return loudness


def scatter_about(own_key, shape, spread, limit, split=(), held_as=jnp.bfloat16):
    values = jax.random.normal(own_key, shape, jnp.float32) * spread
    if len(split) > 0:
        values = shard_levels(own_key, shape, split, -0.22, 0.18) * values
    return jnp.clip(values, min=-limit, max=limit).astype(held_as)


def setup_inputs(seed: int = 0) -> dict:
    keys = jax.random.split(jax.random.key(seed), 15)
    activations = scatter_about(keys[0], (CLIPS, LEN, D), 1.0, 6.0, ((0, 8), (1, 4)))
    cotangent = scatter_about(keys[1], (CLIPS, LEN, D), 1.0, 6.0, ((0, 8), (1, 4)))
    attn_gain = jnp.clip(1.0 + 0.1 * jax.random.normal(keys[2], (D,), jnp.float32), 0.5, 1.5)
    attn_shift = scatter_about(keys[3], (D,), 0.3, 2.0, (), jnp.float32)
    qkv_weight = scatter_about(keys[4], (D, 3 * D), D ** -0.5, 0.1875, ((0, 8), (1, 4)))
    qkv_bias = scatter_about(keys[5], (3 * D,), 0.5, 3.0, ((0, 4),), jnp.float32)
    out_weight = scatter_about(keys[6], (D, D), (max(1, 3 * D // LEN)) ** -0.5, 3.5, ((0, 8), (1, 4)))
    out_bias = scatter_about(keys[7], (D,), 0.3, 2.0, (), jnp.float32)
    mlp_gain = jnp.clip(1.0 + 0.1 * jax.random.normal(keys[8], (D,), jnp.float32), 0.5, 1.5)
    mlp_shift = scatter_about(keys[9], (D,), 0.3, 2.0, (), jnp.float32)
    fc1_weight = scatter_about(keys[10], (D, FF), D ** -0.5, 0.1875, ((0, 8), (1, 4)))
    fc1_bias = scatter_about(keys[11], (FF,), 0.5, 3.0, ((0, 4),), jnp.float32)
    fc2_weight = scatter_about(keys[12], (D, FF), FF ** -0.5, 0.09375, ((0, 8), (1, 4)))
    fc2_bias = scatter_about(keys[13], (D,), 0.3, 2.0, (), jnp.float32)
    return dict(activations=activations, cotangent=cotangent, attn_gain=attn_gain, attn_shift=attn_shift, qkv_weight=qkv_weight, qkv_bias=qkv_bias, out_weight=out_weight, out_bias=out_bias, mlp_gain=mlp_gain, mlp_shift=mlp_shift, fc1_weight=fc1_weight, fc1_bias=fc1_bias, fc2_weight=fc2_weight, fc2_bias=fc2_bias)


@jax.custom_vjp
def low(v):
    return lax.optimization_barrier(v.astype(jnp.bfloat16)).astype(jnp.float32)

@jax.custom_vjp
def low_back(v):
    return v

def low_keep(v):
    return (low(v), None)

def low_pass(kept, grad):
    return (grad,)

def back_keep(v):
    return (v, None)

def back_low(kept, grad):
    return (low(grad),)
low.defvjp(low_keep, low_pass)
low_back.defvjp(back_keep, back_low)

def norm_rows(values, gain_vec, shift_vec):
    row_mean = lax.optimization_barrier(jnp.mean(values, axis=-1, keepdims=True))
    centred = values - row_mean
    variance = lax.optimization_barrier(jnp.mean(centred * centred, axis=-1, keepdims=True))
    return centred * lax.rsqrt(variance + 1e-06) * gain_vec + shift_vec

def rotary_tables(length):
    section = 2 * (HD // 3 // 2)
    half = section // 2
    position = jnp.arange(length)
    frame = (position // (GRID * GRID)).astype(jnp.float32)
    row_pos = (position // GRID % GRID).astype(jnp.float32)
    col_pos = (position % GRID).astype(jnp.float32)
    omega = 1.0 / 10000.0 ** (jnp.arange(half).astype(jnp.float32) / half)
    pieces = [jnp.repeat(coordinate[:, None] * omega[None, :], 2, axis=1) for coordinate in (frame, row_pos, col_pos)]
    pieces.append(jnp.zeros((length, HD - 3 * section), jnp.float32))
    angles = jnp.concatenate(pieces, axis=1)
    parity = jnp.where(jnp.arange(HD) % 2 == 0, -1.0, 1.0).astype(jnp.float32)
    return (jnp.cos(angles), jnp.sin(angles) * parity)

def pair_swap(values):
    shape = values.shape
    paired = values.reshape(shape[:-1] + (shape[-1] // 2, 2))
    return paired[..., ::-1].reshape(shape)

def rotate(values, cosine, sine):
    return values * cosine + pair_swap(values) * sine

def layer(inputs, params):
    attn_gain, attn_shift, qkv_weight, qkv_bias, out_weight, out_bias, mlp_gain, mlp_shift, fc1_weight, fc1_bias, fc2_weight, fc2_bias = params
    highest = lax.Precision.HIGHEST
    cosine, sine = rotary_tables(LEN)
    cosine = cosine[:, None, :]
    sine = sine[:, None, :]
    first = low(norm_rows(inputs, attn_gain, attn_shift))
    packed = low_back(jnp.dot(first, qkv_weight, precision=highest) + qkv_bias).reshape(LEN, H, 3, HD)
    query = low(rotate(packed[:, :, 0], cosine, sine))
    key_all = low(rotate(packed[:, :, 1], cosine, sine))
    value_all = low(packed[:, :, 2])
    factor = 1.0 / math.sqrt(HD)

    def block_attend(query_block):
        scores = low_back(jnp.einsum('qhd,khd->hqk', query_block, key_all, precision=highest) * factor)
        probs = jax.nn.softmax(scores, axis=-1)
        return jnp.einsum('hqk,khd->qhd', low(probs), value_all, precision=highest)
    heads_out = lax.map(jax.checkpoint(block_attend), query.reshape(LEN // QBLK, QBLK, H, HD))
    heads_out = low(low_back(heads_out.reshape(LEN, D)))
    attended = low_back(jnp.dot(heads_out, out_weight.T, precision=highest))
    resid = inputs + attended + out_bias
    second = low(norm_rows(resid, mlp_gain, mlp_shift))
    hidden = low_back(jnp.dot(second, fc1_weight, precision=highest) + fc1_bias)
    act = low(jax.nn.gelu(hidden, approximate=False))
    branch = low_back(jnp.dot(act, fc2_weight.T, precision=highest))
    return resid + branch + fc2_bias

def reference(activations, cotangent, attn_gain, attn_shift, qkv_weight, qkv_bias, out_weight, out_bias, mlp_gain, mlp_shift, fc1_weight, fc1_bias, fc2_weight, fc2_bias):
    params = tuple((item.astype(jnp.float32) for item in (attn_gain, attn_shift, qkv_weight, qkv_bias, out_weight, out_bias, mlp_gain, mlp_shift, fc1_weight, fc1_bias, fc2_weight, fc2_bias)))

    def per_clip(totals, inputs_pair):
        clip_in, clip_grad = inputs_pair
        result, pull = jax.vjp(layer, clip_in.astype(jnp.float32), params)
        grad_in, grad_params = pull(clip_grad.astype(jnp.float32))
        totals = tuple((left + right for left, right in zip(totals, grad_params)))
        return (totals, (result.astype(jnp.bfloat16), grad_in))
    start_totals = tuple((jnp.zeros_like(item) for item in params))
    grads, (output, input_grad) = lax.scan(per_clip, start_totals, (activations, cotangent))
    return (output, input_grad, grads[0], grads[1], grads[2], grads[3], grads[4], grads[5], grads[6], grads[7], grads[8], grads[9], grads[10], grads[11])
```

```python
import math

import jax
import jax.numpy as jnp
from jax import lax
from jax.sharding import PartitionSpec as P

HD = 64
GRID = 16


def norm_rows(values, gain_vec, shift_vec):
    row_mean = jnp.mean(values, axis=-1, keepdims=True)
    centred = values - row_mean
    variance = jnp.mean(centred * centred, axis=-1, keepdims=True)
    return centred * lax.rsqrt(variance + 1e-06) * gain_vec + shift_vec


def rotary_tables(length):
    section = 2 * (HD // 3 // 2)
    half = section // 2
    position = jnp.arange(length)
    frame = (position // (GRID * GRID)).astype(jnp.float32)
    row_pos = (position // GRID % GRID).astype(jnp.float32)
    col_pos = (position % GRID).astype(jnp.float32)
    omega = 1.0 / 10000.0 ** (jnp.arange(half).astype(jnp.float32) / half)
    pieces = [
        jnp.repeat(coordinate[:, None] * omega[None, :], 2, axis=1)
        for coordinate in (frame, row_pos, col_pos)
    ]
    pieces.append(jnp.zeros((length, HD - 3 * section), jnp.float32))
    angles = jnp.concatenate(pieces, axis=1)
    parity = jnp.where(jnp.arange(HD) % 2 == 0, -1.0, 1.0).astype(jnp.float32)
    return (jnp.cos(angles), jnp.sin(angles) * parity)


def pair_swap(values):
    shape = values.shape
    paired = values.reshape(shape[:-1] + (shape[-1] // 2, 2))
    return paired[..., ::-1].reshape(shape)


def contract(left, right, left_dim, right_dim):
    return lax.dot_general(
        left, right, (((left_dim,), (right_dim,)), ((), ())), preferred_element_type=jnp.float32
    )


def exact_gelu(values):
    return jax.nn.gelu(values, approximate=False)


def body(
    activations,
    cotangent,
    attn_gain,
    attn_shift,
    qkv_weight,
    qkv_bias,
    out_weight,
    out_bias,
    mlp_gain,
    mlp_shift,
    fc1_weight,
    fc1_bias,
    fc2_weight,
    fc2_bias,
):
    tensor_size = lax.axis_size("tensor")
    tensor_rank = lax.axis_index("tensor")
    row_count = activations.shape[1]
    width = activations.shape[2]
    length = row_count * tensor_size
    block_rows = min(512, length)
    block_count = length // block_rows
    local_heads = qkv_weight.shape[1] // (3 * HD)
    packed_cols = qkv_weight.shape[1]
    unit_cols = fc1_weight.shape[1]
    factor = 1.0 / math.sqrt(HD)
    cosine, sine = rotary_tables(length)
    cosine = cosine[:, None, :]
    sine = sine[:, None, :]

    def rotate(values):
        return values * cosine + pair_swap(values) * sine

    def rotate_back(values):
        return values * cosine + pair_swap(values * sine)

    def fetch():
        gathered = (
            lax.all_gather(qkv_weight, "dp", axis=0, tiled=True),
            lax.all_gather(out_weight, "dp", axis=0, tiled=True),
            lax.all_gather(fc1_weight, "dp", axis=0, tiled=True),
            lax.all_gather(fc2_weight, "dp", axis=0, tiled=True),
        )
        return (gathered, gathered)

    def seq_gather(values):
        return lax.all_gather(values, "tensor", axis=0, tiled=True)

    def part_sum(values):
        return lax.psum_scatter(
            values.astype(jnp.bfloat16), "tensor", scatter_dimension=0, tiled=True
        ).astype(jnp.float32)

    def grad_gather(values):
        return lax.all_gather(values, "tensor", axis=0, tiled=True)

    def grad_sum(values):
        return lax.psum_scatter(
            values.astype(jnp.bfloat16), "tensor", scatter_dimension=0, tiled=True
        ).astype(jnp.float32)

    def forward(inputs, weights):
        (weight_qkv, weight_out, weight_up, weight_down), (
            whole_qkv,
            whole_out,
            whole_up,
            whole_down,
        ) = weights
        first_all = seq_gather(norm_rows(inputs, attn_gain, attn_shift).astype(jnp.bfloat16))
        packed = (
            jnp.dot(first_all, weight_qkv, preferred_element_type=jnp.float32) + qkv_bias
        ).reshape(length, local_heads, 3, HD)
        query = rotate(packed[:, :, 0]).astype(jnp.bfloat16)
        key_all = rotate(packed[:, :, 1]).astype(jnp.bfloat16)
        value_all = packed[:, :, 2].astype(jnp.bfloat16)
        outputs = []
        log_sums = []
        for block in range(block_count):
            query_block = query[block * block_rows : (block + 1) * block_rows]
            scores = (
                jnp.einsum("qhd,khd->hqk", query_block, key_all, preferred_element_type=jnp.float32)
                * factor
            )
            row_max = jnp.max(scores, axis=-1, keepdims=True)
            expo = jnp.exp(scores - row_max)
            row_total = jnp.sum(expo, axis=-1, keepdims=True)
            weights_low = (expo / row_total).astype(jnp.bfloat16)
            outputs.append(
                jnp.einsum(
                    "hqk,khd->qhd", weights_low, value_all, preferred_element_type=jnp.float32
                )
            )
            log_sums.append(row_max + jnp.log(row_total))
        heads_out = (
            jnp.concatenate(outputs, axis=0).reshape(length, local_heads * HD).astype(jnp.bfloat16)
        )
        log_total = jnp.concatenate(log_sums, axis=1)
        attended = part_sum(contract(heads_out, weight_out, 1, 1))
        resid = inputs + attended + out_bias
        second_all = seq_gather(norm_rows(resid, mlp_gain, mlp_shift).astype(jnp.bfloat16))
        hidden = jnp.dot(second_all, weight_up, preferred_element_type=jnp.float32) + fc1_bias
        act = exact_gelu(hidden).astype(jnp.bfloat16)
        branch = part_sum(contract(act, weight_down, 1, 1))
        result = resid + branch + fc2_bias
        kept = (
            first_all,
            query,
            key_all,
            value_all,
            log_total,
            heads_out,
            heads_out,
            resid,
            second_all,
            hidden,
            act,
        )
        return (result, kept)

    def backward(inputs, grad_low, kept, weights):
        (weight_qkv, weight_out, weight_up, weight_down), (
            whole_qkv,
            whole_out,
            whole_up,
            whole_down,
        ) = weights
        (
            first_all,
            query,
            key_all,
            value_all,
            log_total,
            heads_out,
            heads_rows,
            resid,
            second_all,
            hidden,
            act,
        ) = kept
        grad_top = grad_low.astype(jnp.float32)
        grad_fc2_bias = jnp.sum(grad_top, axis=0)
        grad_all = grad_gather(grad_low)
        grad_fc2_weight = contract(grad_all, act, 0, 0)
        grad_act = jnp.dot(grad_all, weight_down, preferred_element_type=jnp.float32)
        gelu_pull = jax.vjp(exact_gelu, hidden)[1]
        grad_hidden = gelu_pull(grad_act)[0].astype(jnp.bfloat16)
        grad_fc1_bias = jnp.sum(grad_hidden, axis=0, dtype=jnp.float32)
        grad_fc1_weight = contract(second_all, grad_hidden, 0, 0)
        grad_second = grad_sum(contract(grad_hidden, weight_up, 1, 1))
        second_pull = jax.vjp(norm_rows, resid, mlp_gain, mlp_shift)[1]
        grad_resid_norm, grad_mlp_gain, grad_mlp_shift = second_pull(grad_second)
        grad_resid = grad_top + grad_resid_norm
        grad_out_bias = jnp.sum(grad_resid, axis=0)
        resid_low = grad_resid.astype(jnp.bfloat16)
        resid_all = grad_gather(resid_low)
        grad_out_weight = contract(resid_all, heads_out, 0, 0)
        grad_heads = jnp.dot(resid_all, weight_out, preferred_element_type=jnp.float32).astype(
            jnp.bfloat16
        )
        grad_heads = grad_heads.reshape(length, local_heads, HD)
        grad_key = jnp.zeros((length, local_heads, HD), jnp.float32)
        grad_value = jnp.zeros((length, local_heads, HD), jnp.float32)
        query_grads = []
        for block in range(block_count):
            lower = block * block_rows
            upper = lower + block_rows
            query_block = query[lower:upper]
            grad_block = grad_heads[lower:upper]
            scores = (
                jnp.einsum("qhd,khd->hqk", query_block, key_all, preferred_element_type=jnp.float32)
                * factor
            )
            probs = jnp.exp(scores - log_total[:, lower:upper])
            grad_value = grad_value + jnp.einsum(
                "hqk,qhd->khd",
                probs.astype(jnp.bfloat16),
                grad_block,
                preferred_element_type=jnp.float32,
            )
            grad_probs = jnp.einsum(
                "qhd,khd->hqk", grad_block, value_all, preferred_element_type=jnp.float32
            )
            grad_scores = (
                probs * (grad_probs - jnp.sum(probs * grad_probs, axis=-1, keepdims=True))
            ).astype(jnp.bfloat16)
            query_grads.append(
                jnp.einsum("hqk,khd->qhd", grad_scores, key_all, preferred_element_type=jnp.float32)
                * factor
            )
            grad_key = (
                grad_key
                + jnp.einsum(
                    "hqk,qhd->khd", grad_scores, query_block, preferred_element_type=jnp.float32
                )
                * factor
            )
        grad_query = jnp.concatenate(query_grads, axis=0)
        grad_packed = jnp.stack(
            [rotate_back(grad_query), rotate_back(grad_key), grad_value], axis=2
        )
        grad_packed = grad_packed.reshape(length, packed_cols).astype(jnp.bfloat16)
        grad_qkv_bias = jnp.sum(grad_packed, axis=0, dtype=jnp.float32)
        grad_qkv_weight = contract(first_all, grad_packed, 0, 0)
        grad_first = grad_sum(contract(grad_packed, weight_qkv, 1, 1))
        first_pull = jax.vjp(norm_rows, inputs, attn_gain, attn_shift)[1]
        grad_input_norm, grad_attn_gain, grad_attn_shift = first_pull(grad_first)
        input_grad = grad_resid + grad_input_norm
        grads = (
            grad_attn_gain,
            grad_attn_shift,
            grad_qkv_weight,
            grad_qkv_bias,
            grad_out_weight,
            grad_out_bias,
            grad_mlp_gain,
            grad_mlp_shift,
            grad_fc1_weight,
            grad_fc1_bias,
            grad_fc2_weight,
            grad_fc2_bias,
        )
        return (input_grad, grads)

    def per_clip(totals, inputs_pair):
        clip_in, clip_grad = inputs_pair
        forward_weights = fetch()
        result, kept = forward(clip_in.astype(jnp.float32), forward_weights)
        backward_weights = fetch()
        input_grad, grads = backward(clip_in.astype(jnp.float32), clip_grad, kept, backward_weights)
        totals = tuple((left + right for left, right in zip(totals, grads)))
        return (totals, (result.astype(jnp.bfloat16), input_grad))

    out_cols = local_heads * HD
    start_totals = (
        jnp.zeros((width,), jnp.float32),
        jnp.zeros((width,), jnp.float32),
        jnp.zeros((width, packed_cols), jnp.float32),
        jnp.zeros((packed_cols,), jnp.float32),
        jnp.zeros((width, out_cols), jnp.float32),
        jnp.zeros((width,), jnp.float32),
        jnp.zeros((width,), jnp.float32),
        jnp.zeros((width,), jnp.float32),
        jnp.zeros((width, unit_cols), jnp.float32),
        jnp.zeros((unit_cols,), jnp.float32),
        jnp.zeros((width, unit_cols), jnp.float32),
        jnp.zeros((width,), jnp.float32),
    )
    totals, (output, input_grad) = lax.scan(per_clip, start_totals, (activations, cotangent))
    out_grad = totals[4]
    weight_sums = (
        lax.psum_scatter(
            totals[2].astype(jnp.bfloat16), "dp", scatter_dimension=0, tiled=True
        ).astype(jnp.float32),
        lax.psum_scatter(
            out_grad.astype(jnp.bfloat16), "dp", scatter_dimension=0, tiled=True
        ).astype(jnp.float32),
        lax.psum_scatter(
            totals[8].astype(jnp.bfloat16), "dp", scatter_dimension=0, tiled=True
        ).astype(jnp.float32),
        lax.psum_scatter(
            totals[10].astype(jnp.bfloat16), "dp", scatter_dimension=0, tiled=True
        ).astype(jnp.float32),
    )
    qkv_place = lax.dynamic_update_slice_in_dim(
        jnp.zeros((packed_cols * tensor_size,), jnp.float32),
        totals[3],
        tensor_rank * packed_cols,
        0,
    )
    unit_place = lax.dynamic_update_slice_in_dim(
        jnp.zeros((unit_cols * tensor_size,), jnp.float32), totals[9], tensor_rank * unit_cols, 0
    )
    summed = lax.psum(
        (totals[0], totals[1], qkv_place, totals[5], totals[6], totals[7], unit_place, totals[11]),
        ("dp", "tensor"),
    )
    grad_qkv_bias = lax.dynamic_slice_in_dim(summed[2], tensor_rank * packed_cols, packed_cols, 0)
    grad_fc1_bias = lax.dynamic_slice_in_dim(summed[6], tensor_rank * unit_cols, unit_cols, 0)
    return (
        output,
        input_grad,
        summed[0],
        summed[1],
        weight_sums[0],
        grad_qkv_bias,
        weight_sums[1],
        summed[3],
        summed[4],
        summed[5],
        weight_sums[2],
        grad_fc1_bias,
        weight_sums[3],
        summed[7],
    )


SWAP_CORE, SWAP_X, SWAP_Y = 1, 2, 4


def one_clip_per_chip(mesh):
    return mesh.shape["dp"] == 8 and mesh.shape["tensor"] == 4


def swap(values, bit):
    return lax.ppermute(values, "dp", [(i, i ^ bit) for i in range(8)])


def shift(values, step):
    return lax.ppermute(values, "tensor", [(i, (i + step) % 4) for i in range(4)])


def clip_routes(back):
    routes = []
    for turn in range(2):
        pairs = []
        for column in range(4):
            for core in range(2):
                for place in range(4):
                    source = (2 * column + core) * 4 + place
                    target = (2 * column + place // 2) * 4 + 2 * core + (turn ^ (place % 2))
                    pairs.append((target, source) if back else (source, target))
        routes.append(pairs)
    return routes


def pick(flag, first, second):
    return jnp.where(flag, second, first)


def to_clips(values):
    odd = lax.axis_index("tensor") % 2 == 1
    arrived = []
    for turn, pairs in enumerate(clip_routes(False)):
        sent = pick(odd, values[turn], values[1 - turn])
        arrived.append(lax.ppermute(sent, ("dp", "tensor"), pairs))
    return jnp.concatenate(
        [pick(odd, arrived[0], arrived[1]), pick(odd, arrived[1], arrived[0])], axis=0
    )


def from_clips(values):
    odd = lax.axis_index("tensor") % 2 == 1
    rows = values.shape[0] // 2
    arrived = []
    for turn, pairs in enumerate(clip_routes(True)):
        sent = pick(odd, values[turn * rows : (turn + 1) * rows], values[(1 - turn) * rows : (2 - turn) * rows])
        arrived.append(lax.ppermute(sent, ("dp", "tensor"), pairs))
    return jnp.stack([pick(odd, arrived[0], arrived[1]), pick(odd, arrived[1], arrived[0])])


def three_parts(values):
    high = lax.reduce_precision(values, 8, 7)
    rest = values - high
    middle = lax.reduce_precision(rest, 8, 7)
    low = rest - middle
    return jnp.stack([high, middle, low]).astype(jnp.bfloat16)


def clip_body(
    activations,
    cotangent,
    attn_gain,
    attn_shift,
    qkv_weight,
    qkv_bias,
    out_weight,
    out_bias,
    mlp_gain,
    mlp_shift,
    fc1_weight,
    fc1_bias,
    fc2_weight,
    fc2_bias,
):
    index = lax.axis_index("dp")
    core = index % 2
    at_x = index // 2 % 2
    at_y = index // 4
    width = activations.shape[2]
    length = activations.shape[1] * 4
    half_rows = length // 2
    own_rows = qkv_weight.shape[0]
    heads_here = qkv_weight.shape[1] // (3 * HD)
    half_heads = heads_here // 2
    heads = 4 * half_heads
    qkv_cols = half_heads * 3 * HD
    out_cols = out_weight.shape[1] // 2
    unit_cols = fc1_weight.shape[1] // 2
    factor = 1.0 / math.sqrt(HD)
    low = jnp.bfloat16

    def first_half(values):
        return lax.slice_in_dim(values, 0, values.shape[-1] // 2, axis=values.ndim - 1)

    def second_half(values):
        return lax.slice_in_dim(values, values.shape[-1] // 2, values.shape[-1], axis=values.ndim - 1)

    def own_half(values):
        return pick(core == 1, first_half(values), second_half(values))

    def other_half(values):
        return pick(core == 1, second_half(values), first_half(values))

    def by_kind(values):
        lead = values.shape[:-1]
        split = values.reshape(lead + (2, half_heads, 3, HD))
        return jnp.swapaxes(split, -3, -2).reshape(values.shape)

    def by_head(values):
        lead = values.shape[:-1]
        split = values.reshape(lead + (2, 3, half_heads, HD))
        return jnp.swapaxes(split, -3, -2).reshape(values.shape)

    tokens = to_clips(activations).astype(jnp.float32)

    columns = (by_kind(qkv_weight), out_weight, fc1_weight, fc2_weight)
    biases = (by_kind(qkv_bias), None, fc1_bias, None)
    mine = jnp.concatenate([own_half(item) for item in columns], axis=1)
    theirs = swap(jnp.concatenate([other_half(item) for item in columns], axis=1), SWAP_CORE)
    rows = jnp.stack([pick(core == 1, mine, theirs), pick(core == 1, theirs, mine)])

    def along_z(values):
        return jnp.stack([values] + [shift(values, step) for step in (1, 2, 3)], axis=values.ndim - 1)

    def over_plane(values):
        even, odd = values[0], values[1]
        even_x = swap(even, SWAP_X)
        odd_y = swap(odd, SWAP_Y)
        even = jnp.stack([pick(at_x == 1, even, even_x), pick(at_x == 1, even_x, even)])
        odd = jnp.stack([pick(at_y == 1, odd, odd_y), pick(at_y == 1, odd_y, odd)])
        even_y = swap(even, SWAP_Y)
        odd_x = swap(odd, SWAP_X)
        even = jnp.stack([pick(at_y == 1, even, even_y), pick(at_y == 1, even_y, even)])
        odd = jnp.stack([pick(at_x == 1, odd, odd_x), pick(at_x == 1, odd_x, odd)], axis=1)
        whole = jnp.stack([even, odd], axis=2)
        return whole.reshape((4 * 2 * own_rows, -1))

    bounds = [0, qkv_cols, qkv_cols + out_cols, qkv_cols + out_cols + unit_cols, qkv_cols + out_cols + 2 * unit_cols]

    def widened(part, bias):
        lines = jnp.zeros((16, part.shape[-1]), low)
        lines = lines.at[:3].set(three_parts(own_half(bias)))
        return jnp.concatenate([part.reshape(-1, part.shape[-1]), lines], axis=0)

    def parted(values, cols):
        body_rows, lines = values[: 2 * own_rows], values[2 * own_rows :]
        bias = jnp.sum(lines[:3].astype(jnp.float32), axis=0).reshape(-1)
        return body_rows.reshape(2, own_rows, 4, cols), bias

    qkv_z, bias_qkv = parted(along_z(widened(rows[:, :, : bounds[1]], biases[0])), qkv_cols)
    weight_qkv = over_plane(qkv_z)
    out_z = along_z(rows[:, :, bounds[1] : bounds[2]])
    weight_out = over_plane(out_z)
    up_z, bias_up = parted(along_z(widened(rows[:, :, bounds[2] : bounds[3]], biases[2])), unit_cols)
    weight_up = over_plane(up_z)
    down_z = along_z(rows[:, :, bounds[3] :])
    weight_down = over_plane(down_z)

    def both_halves(values):
        other = swap(values, SWAP_CORE)
        return jnp.concatenate([pick(core == 1, values, other), pick(core == 1, other, values)], axis=0)

    def part_sum(values):
        halves = values.reshape((2, half_rows) + values.shape[1:])
        sent = pick(core == 1, halves[1], halves[0]).astype(low)
        return pick(core == 1, halves[0], halves[1]) + swap(sent, SWAP_CORE).astype(jnp.float32)

    cosine, sine = rotary_tables(length)
    cosine = cosine[:, None, :]
    sine = sine[:, None, :]

    def rotate(values):
        return values * cosine + pair_swap(values) * sine

    def rotate_back(values):
        return values * cosine + pair_swap(values * sine)

    first_all = both_halves(norm_rows(tokens, attn_gain, attn_shift).astype(low))
    packed = jnp.dot(first_all, weight_qkv, preferred_element_type=jnp.float32) + bias_qkv
    packed = packed.reshape(length, 4, 3, half_heads, HD)
    query = rotate(packed[:, :, 0].reshape(length, heads, HD)).astype(low)
    key = rotate(packed[:, :, 1].reshape(length, heads, HD)).astype(low)
    value = packed[:, :, 2].reshape(length, heads, HD).astype(low)
    scores = jnp.einsum("qhd,khd->hqk", query, key, preferred_element_type=jnp.float32) * factor
    row_max = jnp.max(scores, axis=-1, keepdims=True)
    expo = jnp.exp(scores - row_max)
    row_total = jnp.sum(expo, axis=-1, keepdims=True)
    weights_low = (expo / row_total).astype(low)
    heads_out = jnp.einsum("hqk,khd->qhd", weights_low, value, preferred_element_type=jnp.float32)
    heads_out = heads_out.reshape(length, heads * HD).astype(low)
    log_total = row_max + jnp.log(row_total)
    resid = tokens + part_sum(contract(heads_out, weight_out, 1, 1)) + out_bias
    second_all = both_halves(norm_rows(resid, mlp_gain, mlp_shift).astype(low))
    hidden = jnp.dot(second_all, weight_up, preferred_element_type=jnp.float32) + bias_up
    act = exact_gelu(hidden).astype(low)
    result = resid + part_sum(contract(act, weight_down, 1, 1)) + fc2_bias
    output = from_clips(result.astype(low))

    def to_owner(grad, cols):
        parts = grad.astype(low).reshape(2, 2, 2, own_rows, 4 * cols)
        even, odd = parts[:, :, 0], parts[:, :, 1]
        even = pick(at_y == 1, even[0], even[1]) + swap(pick(at_y == 1, even[1], even[0]), SWAP_Y)
        odd = pick(at_x == 1, odd[:, 0], odd[:, 1]) + swap(pick(at_x == 1, odd[:, 1], odd[:, 0]), SWAP_X)
        even = pick(at_x == 1, even[0], even[1]) + swap(pick(at_x == 1, even[1], even[0]), SWAP_X)
        odd = pick(at_y == 1, odd[0], odd[1]) + swap(pick(at_y == 1, odd[1], odd[0]), SWAP_Y)
        both = jnp.stack([even, odd]).reshape(2, own_rows, 4, cols)
        total = both[:, :, 0].astype(jnp.float32)
        for step in (1, 2, 3):
            total = total + shift(both[:, :, step], 4 - step).astype(jnp.float32)
        total = total.astype(low)
        kept = pick(core == 1, total[0], total[1])
        came = swap(pick(core == 1, total[1], total[0]), SWAP_CORE)
        return jnp.concatenate(
            [pick(core == 1, kept, came), pick(core == 1, came, kept)], axis=-1
        ).astype(jnp.float32)

    grad_own = to_clips(cotangent)
    grad_top = grad_own.astype(jnp.float32)
    grad_all = both_halves(grad_own)
    sum_fc2_bias = jnp.sum(grad_top, axis=0)
    grad_fc2_weight = to_owner(contract(grad_all, act, 0, 0), unit_cols)
    grad_act = jnp.dot(grad_all, weight_down, preferred_element_type=jnp.float32)
    grad_hidden = jax.vjp(exact_gelu, hidden)[1](grad_act)[0].astype(low)
    sum_fc1_bias = jnp.sum(grad_hidden, axis=0, dtype=jnp.float32)
    grad_fc1_weight = to_owner(contract(second_all, grad_hidden, 0, 0), unit_cols)
    grad_second = part_sum(contract(grad_hidden, weight_up, 1, 1))
    second_pull = jax.vjp(norm_rows, resid, mlp_gain, mlp_shift)[1]
    grad_resid_norm, sum_mlp_gain, sum_mlp_shift = second_pull(grad_second)
    grad_resid = grad_top + grad_resid_norm
    sum_out_bias = jnp.sum(grad_resid, axis=0)
    resid_all = both_halves(grad_resid.astype(low))
    grad_out_weight = to_owner(contract(resid_all, heads_out, 0, 0), out_cols)
    grad_heads = jnp.dot(resid_all, weight_out, preferred_element_type=jnp.float32).astype(low)
    grad_heads = grad_heads.reshape(length, heads, HD)
    scores = jnp.einsum("qhd,khd->hqk", query, key, preferred_element_type=jnp.float32) * factor
    probs = jnp.exp(scores - log_total)
    grad_value = jnp.einsum(
        "hqk,qhd->khd", probs.astype(low), grad_heads, preferred_element_type=jnp.float32
    )
    grad_probs = jnp.einsum("qhd,khd->hqk", grad_heads, value, preferred_element_type=jnp.float32)
    grad_scores = (
        probs * (grad_probs - jnp.sum(probs * grad_probs, axis=-1, keepdims=True))
    ).astype(low)
    grad_query = factor * jnp.einsum("hqk,khd->qhd", grad_scores, key, preferred_element_type=jnp.float32)
    grad_key = factor * jnp.einsum("hqk,qhd->khd", grad_scores, query, preferred_element_type=jnp.float32)
    kinds = [
        item.reshape(length, 4, 1, half_heads, HD)
        for item in (rotate_back(grad_query), rotate_back(grad_key), grad_value)
    ]
    grad_packed = jnp.concatenate(kinds, axis=2).reshape(length, 4 * qkv_cols).astype(low)
    sum_qkv_bias = jnp.sum(grad_packed, axis=0, dtype=jnp.float32)
    grad_qkv_weight = by_head(to_owner(contract(first_all, grad_packed, 0, 0), qkv_cols))
    grad_first = part_sum(contract(grad_packed, weight_qkv, 1, 1))
    first_pull = jax.vjp(norm_rows, tokens, attn_gain, attn_shift)[1]
    grad_input_norm, sum_attn_gain, sum_attn_shift = first_pull(grad_first)
    input_grad = from_clips((grad_resid + grad_input_norm).astype(low)).astype(jnp.float32)

    def plane_total(values):
        values = values + swap(values, SWAP_X)
        return values + swap(values, SWAP_Y)

    def whole_total(values):
        values = plane_total(values)
        values = values + swap(values, SWAP_CORE)
        for bit in (1, 2):
            values = values + lax.ppermute(values, "tensor", [(i, i ^ bit) for i in range(4)])
        return values

    def bias_total(values, cols):
        blocks = plane_total(values).reshape(4, cols)
        total = blocks[0]
        for step in (1, 2, 3):
            total = total + shift(blocks[step], 4 - step)
        other = swap(total, SWAP_CORE)
        return jnp.concatenate([pick(core == 1, total, other), pick(core == 1, other, total)])

    early = whole_total(jnp.stack([sum_fc2_bias, sum_mlp_gain, sum_mlp_shift, sum_out_bias]))
    late = whole_total(jnp.stack([sum_attn_gain, sum_attn_shift]))
    return (
        output,
        input_grad,
        late[0],
        late[1],
        grad_qkv_weight,
        by_head(bias_total(sum_qkv_bias, qkv_cols)),
        grad_out_weight,
        early[3],
        early[1],
        early[2],
        grad_fc1_weight,
        bias_total(sum_fc1_bias, unit_cols),
        grad_fc2_weight,
        early[0],
    )


def solution(mesh):
    in_specs = (
        P("dp", "tensor", None),
        P("dp", "tensor", None),
        P(),
        P(),
        P("dp", "tensor"),
        P("tensor"),
        P("dp", "tensor"),
        P(),
        P(),
        P(),
        P("dp", "tensor"),
        P("tensor"),
        P("dp", "tensor"),
        P(),
    )
    out_specs = (
        P("dp", "tensor", None),
        P("dp", "tensor", None),
        P(),
        P(),
        P("dp", "tensor"),
        P("tensor"),
        P("dp", "tensor"),
        P(),
        P(),
        P(),
        P("dp", "tensor"),
        P("tensor"),
        P("dp", "tensor"),
        P(),
    )
    plan = clip_body if one_clip_per_chip(mesh) else body
    return jax.shard_map(plan, mesh=mesh, in_specs=in_specs, out_specs=out_specs, check_vma=False)
```

```python
import math

import jax
import jax.numpy as jnp
from jax import lax
from jax.experimental import pallas as pl
from jax.experimental.pallas import tpu as pltpu
from jax.sharding import PartitionSpec as P

HD = 64
GRID = 16


def norm_rows(values, gain_vec, shift_vec):
    row_mean = jnp.mean(values, axis=-1, keepdims=True)
    centred = values - row_mean
    variance = jnp.mean(centred * centred, axis=-1, keepdims=True)
    return centred * lax.rsqrt(variance + 1e-06) * gain_vec + shift_vec


def rotary_tables(length):
    section = 2 * (HD // 3 // 2)
    half = section // 2
    position = jnp.arange(length)
    frame = (position // (GRID * GRID)).astype(jnp.float32)
    row_pos = (position // GRID % GRID).astype(jnp.float32)
    col_pos = (position % GRID).astype(jnp.float32)
    omega = 1.0 / 10000.0 ** (jnp.arange(half).astype(jnp.float32) / half)
    pieces = [
        jnp.repeat(coordinate[:, None] * omega[None, :], 2, axis=1)
        for coordinate in (frame, row_pos, col_pos)
    ]
    pieces.append(jnp.zeros((length, HD - 3 * section), jnp.float32))
    angles = jnp.concatenate(pieces, axis=1)
    parity = jnp.where(jnp.arange(HD) % 2 == 0, -1.0, 1.0).astype(jnp.float32)
    return (jnp.cos(angles), jnp.sin(angles) * parity)


def pair_swap(values):
    shape = values.shape
    paired = values.reshape(shape[:-1] + (shape[-1] // 2, 2))
    return paired[..., ::-1].reshape(shape)


def contract(left, right, left_dim, right_dim):
    return lax.dot_general(
        left, right, (((left_dim,), (right_dim,)), ((), ())), preferred_element_type=jnp.float32
    )


def exact_gelu(values):
    return jax.nn.gelu(values, approximate=False)


def body(
    activations,
    cotangent,
    attn_gain,
    attn_shift,
    qkv_weight,
    qkv_bias,
    out_weight,
    out_bias,
    mlp_gain,
    mlp_shift,
    fc1_weight,
    fc1_bias,
    fc2_weight,
    fc2_bias,
):
    tensor_size = lax.axis_size("tensor")
    tensor_rank = lax.axis_index("tensor")
    row_count = activations.shape[1]
    width = activations.shape[2]
    length = row_count * tensor_size
    block_rows = min(512, length)
    block_count = length // block_rows
    local_heads = qkv_weight.shape[1] // (3 * HD)
    packed_cols = qkv_weight.shape[1]
    unit_cols = fc1_weight.shape[1]
    factor = 1.0 / math.sqrt(HD)
    cosine, sine = rotary_tables(length)
    cosine = cosine[:, None, :]
    sine = sine[:, None, :]

    def rotate(values):
        return values * cosine + pair_swap(values) * sine

    def rotate_back(values):
        return values * cosine + pair_swap(values * sine)

    def fetch():
        gathered = (
            lax.all_gather(qkv_weight, "dp", axis=0, tiled=True),
            lax.all_gather(out_weight, "dp", axis=0, tiled=True),
            lax.all_gather(fc1_weight, "dp", axis=0, tiled=True),
            lax.all_gather(fc2_weight, "dp", axis=0, tiled=True),
        )
        return (gathered, gathered)

    def seq_gather(values):
        return lax.all_gather(values, "tensor", axis=0, tiled=True)

    def part_sum(values):
        return lax.psum_scatter(
            values.astype(jnp.bfloat16), "tensor", scatter_dimension=0, tiled=True
        ).astype(jnp.float32)

    def grad_gather(values):
        return lax.all_gather(values, "tensor", axis=0, tiled=True)

    def grad_sum(values):
        return lax.psum_scatter(
            values.astype(jnp.bfloat16), "tensor", scatter_dimension=0, tiled=True
        ).astype(jnp.float32)

    def forward(inputs, weights):
        (weight_qkv, weight_out, weight_up, weight_down), (
            whole_qkv,
            whole_out,
            whole_up,
            whole_down,
        ) = weights
        first_all = seq_gather(norm_rows(inputs, attn_gain, attn_shift).astype(jnp.bfloat16))
        packed = (
            jnp.dot(first_all, weight_qkv, preferred_element_type=jnp.float32) + qkv_bias
        ).reshape(length, local_heads, 3, HD)
        query = rotate(packed[:, :, 0]).astype(jnp.bfloat16)
        key_all = rotate(packed[:, :, 1]).astype(jnp.bfloat16)
        value_all = packed[:, :, 2].astype(jnp.bfloat16)
        outputs = []
        log_sums = []
        for block in range(block_count):
            query_block = query[block * block_rows : (block + 1) * block_rows]
            scores = (
                jnp.einsum("qhd,khd->hqk", query_block, key_all, preferred_element_type=jnp.float32)
                * factor
            )
            row_max = jnp.max(scores, axis=-1, keepdims=True)
            expo = jnp.exp(scores - row_max)
            row_total = jnp.sum(expo, axis=-1, keepdims=True)
            weights_low = (expo / row_total).astype(jnp.bfloat16)
            outputs.append(
                jnp.einsum(
                    "hqk,khd->qhd", weights_low, value_all, preferred_element_type=jnp.float32
                )
            )
            log_sums.append(row_max + jnp.log(row_total))
        heads_out = (
            jnp.concatenate(outputs, axis=0).reshape(length, local_heads * HD).astype(jnp.bfloat16)
        )
        log_total = jnp.concatenate(log_sums, axis=1)
        attended = part_sum(contract(heads_out, weight_out, 1, 1))
        resid = inputs + attended + out_bias
        second_all = seq_gather(norm_rows(resid, mlp_gain, mlp_shift).astype(jnp.bfloat16))
        hidden = jnp.dot(second_all, weight_up, preferred_element_type=jnp.float32) + fc1_bias
        act = exact_gelu(hidden).astype(jnp.bfloat16)
        branch = part_sum(contract(act, weight_down, 1, 1))
        result = resid + branch + fc2_bias
        kept = (
            first_all,
            query,
            key_all,
            value_all,
            log_total,
            heads_out,
            heads_out,
            resid,
            second_all,
            hidden,
            act,
        )
        return (result, kept)

    def backward(inputs, grad_low, kept, weights):
        (weight_qkv, weight_out, weight_up, weight_down), (
            whole_qkv,
            whole_out,
            whole_up,
            whole_down,
        ) = weights
        (
            first_all,
            query,
            key_all,
            value_all,
            log_total,
            heads_out,
            heads_rows,
            resid,
            second_all,
            hidden,
            act,
        ) = kept
        grad_top = grad_low.astype(jnp.float32)
        grad_fc2_bias = jnp.sum(grad_top, axis=0)
        grad_all = grad_gather(grad_low)
        grad_fc2_weight = contract(grad_all, act, 0, 0)
        grad_act = jnp.dot(grad_all, weight_down, preferred_element_type=jnp.float32)
        gelu_pull = jax.vjp(exact_gelu, hidden)[1]
        grad_hidden = gelu_pull(grad_act)[0].astype(jnp.bfloat16)
        grad_fc1_bias = jnp.sum(grad_hidden, axis=0, dtype=jnp.float32)
        grad_fc1_weight = contract(second_all, grad_hidden, 0, 0)
        grad_second = grad_sum(contract(grad_hidden, weight_up, 1, 1))
        second_pull = jax.vjp(norm_rows, resid, mlp_gain, mlp_shift)[1]
        grad_resid_norm, grad_mlp_gain, grad_mlp_shift = second_pull(grad_second)
        grad_resid = grad_top + grad_resid_norm
        grad_out_bias = jnp.sum(grad_resid, axis=0)
        resid_low = grad_resid.astype(jnp.bfloat16)
        resid_all = grad_gather(resid_low)
        grad_out_weight = contract(resid_all, heads_out, 0, 0)
        grad_heads = jnp.dot(resid_all, weight_out, preferred_element_type=jnp.float32).astype(
            jnp.bfloat16
        )
        grad_heads = grad_heads.reshape(length, local_heads, HD)
        grad_key = jnp.zeros((length, local_heads, HD), jnp.float32)
        grad_value = jnp.zeros((length, local_heads, HD), jnp.float32)
        query_grads = []
        for block in range(block_count):
            lower = block * block_rows
            upper = lower + block_rows
            query_block = query[lower:upper]
            grad_block = grad_heads[lower:upper]
            scores = (
                jnp.einsum("qhd,khd->hqk", query_block, key_all, preferred_element_type=jnp.float32)
                * factor
            )
            probs = jnp.exp(scores - log_total[:, lower:upper])
            grad_value = grad_value + jnp.einsum(
                "hqk,qhd->khd",
                probs.astype(jnp.bfloat16),
                grad_block,
                preferred_element_type=jnp.float32,
            )
            grad_probs = jnp.einsum(
                "qhd,khd->hqk", grad_block, value_all, preferred_element_type=jnp.float32
            )
            grad_scores = (
                probs * (grad_probs - jnp.sum(probs * grad_probs, axis=-1, keepdims=True))
            ).astype(jnp.bfloat16)
            query_grads.append(
                jnp.einsum("hqk,khd->qhd", grad_scores, key_all, preferred_element_type=jnp.float32)
                * factor
            )
            grad_key = (
                grad_key
                + jnp.einsum(
                    "hqk,qhd->khd", grad_scores, query_block, preferred_element_type=jnp.float32
                )
                * factor
            )
        grad_query = jnp.concatenate(query_grads, axis=0)
        grad_packed = jnp.stack(
            [rotate_back(grad_query), rotate_back(grad_key), grad_value], axis=2
        )
        grad_packed = grad_packed.reshape(length, packed_cols).astype(jnp.bfloat16)
        grad_qkv_bias = jnp.sum(grad_packed, axis=0, dtype=jnp.float32)
        grad_qkv_weight = contract(first_all, grad_packed, 0, 0)
        grad_first = grad_sum(contract(grad_packed, weight_qkv, 1, 1))
        first_pull = jax.vjp(norm_rows, inputs, attn_gain, attn_shift)[1]
        grad_input_norm, grad_attn_gain, grad_attn_shift = first_pull(grad_first)
        input_grad = grad_resid + grad_input_norm
        grads = (
            grad_attn_gain,
            grad_attn_shift,
            grad_qkv_weight,
            grad_qkv_bias,
            grad_out_weight,
            grad_out_bias,
            grad_mlp_gain,
            grad_mlp_shift,
            grad_fc1_weight,
            grad_fc1_bias,
            grad_fc2_weight,
            grad_fc2_bias,
        )
        return (input_grad, grads)

    def per_clip(totals, inputs_pair):
        clip_in, clip_grad = inputs_pair
        forward_weights = fetch()
        result, kept = forward(clip_in.astype(jnp.float32), forward_weights)
        backward_weights = fetch()
        input_grad, grads = backward(clip_in.astype(jnp.float32), clip_grad, kept, backward_weights)
        totals = tuple((left + right for left, right in zip(totals, grads)))
        return (totals, (result.astype(jnp.bfloat16), input_grad))

    out_cols = local_heads * HD
    start_totals = (
        jnp.zeros((width,), jnp.float32),
        jnp.zeros((width,), jnp.float32),
        jnp.zeros((width, packed_cols), jnp.float32),
        jnp.zeros((packed_cols,), jnp.float32),
        jnp.zeros((width, out_cols), jnp.float32),
        jnp.zeros((width,), jnp.float32),
        jnp.zeros((width,), jnp.float32),
        jnp.zeros((width,), jnp.float32),
        jnp.zeros((width, unit_cols), jnp.float32),
        jnp.zeros((unit_cols,), jnp.float32),
        jnp.zeros((width, unit_cols), jnp.float32),
        jnp.zeros((width,), jnp.float32),
    )
    totals, (output, input_grad) = lax.scan(per_clip, start_totals, (activations, cotangent))
    out_grad = totals[4]
    weight_sums = (
        lax.psum_scatter(
            totals[2].astype(jnp.bfloat16), "dp", scatter_dimension=0, tiled=True
        ).astype(jnp.float32),
        lax.psum_scatter(
            out_grad.astype(jnp.bfloat16), "dp", scatter_dimension=0, tiled=True
        ).astype(jnp.float32),
        lax.psum_scatter(
            totals[8].astype(jnp.bfloat16), "dp", scatter_dimension=0, tiled=True
        ).astype(jnp.float32),
        lax.psum_scatter(
            totals[10].astype(jnp.bfloat16), "dp", scatter_dimension=0, tiled=True
        ).astype(jnp.float32),
    )
    qkv_place = lax.dynamic_update_slice_in_dim(
        jnp.zeros((packed_cols * tensor_size,), jnp.float32),
        totals[3],
        tensor_rank * packed_cols,
        0,
    )
    unit_place = lax.dynamic_update_slice_in_dim(
        jnp.zeros((unit_cols * tensor_size,), jnp.float32), totals[9], tensor_rank * unit_cols, 0
    )
    summed = lax.psum(
        (totals[0], totals[1], qkv_place, totals[5], totals[6], totals[7], unit_place, totals[11]),
        ("dp", "tensor"),
    )
    grad_qkv_bias = lax.dynamic_slice_in_dim(summed[2], tensor_rank * packed_cols, packed_cols, 0)
    grad_fc1_bias = lax.dynamic_slice_in_dim(summed[6], tensor_rank * unit_cols, unit_cols, 0)
    return (
        output,
        input_grad,
        summed[0],
        summed[1],
        weight_sums[0],
        grad_qkv_bias,
        weight_sums[1],
        summed[3],
        summed[4],
        summed[5],
        weight_sums[2],
        grad_fc1_bias,
        weight_sums[3],
        summed[7],
    )


def lane_swap(values):
    even = lax.broadcasted_iota(jnp.int32, values.shape, 1) % 2 == 0
    return jnp.where(even, pltpu.roll(values, 127, 1), pltpu.roll(values, 1, 1))


def attend_kernel(first_ref, weight_ref, bias_ref, cos_ref, sin_ref, qkv_ref, heads_ref, turned_ref, log_ref):
    low = jnp.bfloat16
    packed = jnp.dot(first_ref[...], weight_ref[...], preferred_element_type=jnp.float32) + bias_ref[...]
    cosine, sine = cos_ref[...], sin_ref[...]

    def rotate(values):
        return values * cosine + lane_swap(values) * sine

    query = (rotate(packed[:, :128]).astype(low).astype(jnp.float32) * 0.125).astype(low)
    key = rotate(packed[:, 128:256]).astype(low)
    value = packed[:, 256:]
    qkv_ref[:, :128] = query
    qkv_ref[:, 128:256] = key
    qkv_ref[:, 256:] = value.astype(low)
    value = jnp.transpose(value).astype(low)
    first_head = lax.broadcasted_iota(jnp.int32, key.shape, 1) < HD
    for head in range(2):
        mine = slice(head * HD, (head + 1) * HD)
        key_here = jnp.where(first_head == (head == 0), key, jnp.zeros_like(key))
        scores = contract(key_here, query, 1, 1)
        top = jnp.max(scores, axis=0, keepdims=True)
        expo = jnp.exp(scores - top)
        total = jnp.sum(expo, axis=0, keepdims=True)
        summed = jnp.dot(value[mine], expo.astype(low), preferred_element_type=jnp.float32)
        turned_ref[0, mine] = summed / total
        log_ref[0, head : head + 1] = top + jnp.log(total)
    heads_ref[...] = jnp.transpose(turned_ref[0]).astype(low)


def attend(first, weight, bias, cosine, sine):
    length, width = first.shape
    pairs = weight.shape[1] // 384
    return pl.pallas_call(
        attend_kernel,
        grid=(pairs,),
        in_specs=[
            pl.BlockSpec((length, width), lambda i: (0, 0)),
            pl.BlockSpec((width, 384), lambda i: (0, i)),
            pl.BlockSpec((1, 384), lambda i: (0, i)),
            pl.BlockSpec((length, 128), lambda i: (0, 0)),
            pl.BlockSpec((length, 128), lambda i: (0, 0)),
        ],
        out_specs=[
            pl.BlockSpec((length, 384), lambda i: (0, i)),
            pl.BlockSpec((length, 128), lambda i: (0, i)),
            pl.BlockSpec((1, 128, length), lambda i: (i, 0, 0)),
            pl.BlockSpec((1, 2, length), lambda i: (i, 0, 0)),
        ],
        out_shape=[
            jax.ShapeDtypeStruct((length, 384 * pairs), jnp.bfloat16),
            jax.ShapeDtypeStruct((length, 128 * pairs), jnp.bfloat16),
            jax.ShapeDtypeStruct((pairs, 128, length), jnp.float32),
            jax.ShapeDtypeStruct((pairs, 2, length), jnp.float32),
        ],
        name="attend",
    )(first, weight, bias.reshape(1, -1), cosine, sine)


def attend_back_kernel(qkv_ref, grad_ref, turned_ref, log_ref, cos_ref, sin_ref, out_ref, bias_ref):
    low = jnp.bfloat16
    query = qkv_ref[:, :128]
    key = qkv_ref[:, 128:256]
    value = qkv_ref[:, 256:]
    grad = grad_ref[...]
    key_turned = jnp.transpose(key.astype(jnp.float32)).astype(low)
    product = jnp.transpose(grad.astype(jnp.float32)) * turned_ref[0]
    first_head = lax.broadcasted_iota(jnp.int32, key.shape, 1) < HD
    zero = jnp.zeros_like(key)
    query_grads, key_grads, value_grads = [], [], []
    for head in range(2):
        mine = slice(head * HD, (head + 1) * HD)
        here = first_head == (head == 0)
        delta = jnp.sum(product[mine], axis=0, keepdims=True)
        scores = contract(jnp.where(here, key, zero), query, 1, 1)
        probs = jnp.exp(scores - log_ref[0, head : head + 1])
        grad_probs = contract(jnp.where(here, value, zero), grad, 1, 1)
        grad_scores = (probs * (grad_probs - delta)).astype(low)
        value_grads.append(jnp.dot(probs.astype(low), grad, preferred_element_type=jnp.float32))
        key_grads.append(jnp.dot(grad_scores, query, preferred_element_type=jnp.float32))
        query_grads.append(jnp.dot(key_turned[mine], grad_scores, preferred_element_type=jnp.float32))
    cosine, sine = cos_ref[...], sin_ref[...]

    def rotate_back(values):
        return values * cosine + lane_swap(values * sine)

    parts = [
        rotate_back(jnp.transpose(jnp.concatenate(query_grads, axis=0)) * 0.125),
        rotate_back(jnp.where(first_head, key_grads[0], key_grads[1])),
        jnp.where(first_head, value_grads[0], value_grads[1]),
    ]
    for at, part in enumerate(parts):
        part = part.astype(low)
        out_ref[:, at * 128 : (at + 1) * 128] = part
        bias_ref[:, at * 128 : (at + 1) * 128] = jnp.sum(part.astype(jnp.float32), axis=0, keepdims=True)


def attend_back(qkv, grad, turned, logs, cosine, sine):
    length = qkv.shape[0]
    pairs = qkv.shape[1] // 384
    return pl.pallas_call(
        attend_back_kernel,
        grid=(pairs,),
        in_specs=[
            pl.BlockSpec((length, 384), lambda i: (0, i)),
            pl.BlockSpec((length, 128), lambda i: (0, i)),
            pl.BlockSpec((1, 128, length), lambda i: (i, 0, 0)),
            pl.BlockSpec((1, 2, length), lambda i: (i, 0, 0)),
            pl.BlockSpec((length, 128), lambda i: (0, 0)),
            pl.BlockSpec((length, 128), lambda i: (0, 0)),
        ],
        out_specs=[
            pl.BlockSpec((length, 384), lambda i: (0, i)),
            pl.BlockSpec((1, 384), lambda i: (0, i)),
        ],
        out_shape=[
            jax.ShapeDtypeStruct((length, 384 * pairs), jnp.bfloat16),
            jax.ShapeDtypeStruct((1, 384 * pairs), jnp.float32),
        ],
        name="attend_back",
    )(qkv, grad, turned, logs, cosine, sine)


SWAP_CORE, SWAP_X, SWAP_Y = 1, 2, 4


def one_clip_per_chip(mesh):
    return mesh.shape["dp"] == 8 and mesh.shape["tensor"] == 4


def swap(values, bit):
    return lax.ppermute(values, "dp", [(i, i ^ bit) for i in range(8)])


def shift(values, step):
    return lax.ppermute(values, "tensor", [(i, (i + step) % 4) for i in range(4)])


def clip_routes(back):
    routes = []
    for turn in range(2):
        pairs = []
        for column in range(4):
            for core in range(2):
                for place in range(4):
                    source = (2 * column + core) * 4 + place
                    target = (2 * column + place // 2) * 4 + 2 * core + (turn ^ (place % 2))
                    pairs.append((target, source) if back else (source, target))
        routes.append(pairs)
    return routes


def pick(flag, first, second):
    return jnp.where(flag, second, first)


def to_clips(values):
    odd = lax.axis_index("tensor") % 2 == 1
    arrived = []
    for turn, pairs in enumerate(clip_routes(False)):
        sent = pick(odd, values[turn], values[1 - turn])
        arrived.append(lax.ppermute(sent, ("dp", "tensor"), pairs))
    return jnp.concatenate(
        [pick(odd, arrived[0], arrived[1]), pick(odd, arrived[1], arrived[0])], axis=0
    )


def from_clips(values):
    odd = lax.axis_index("tensor") % 2 == 1
    rows = values.shape[0] // 2
    arrived = []
    for turn, pairs in enumerate(clip_routes(True)):
        sent = pick(odd, values[turn * rows : (turn + 1) * rows], values[(1 - turn) * rows : (2 - turn) * rows])
        arrived.append(lax.ppermute(sent, ("dp", "tensor"), pairs))
    return jnp.stack([pick(odd, arrived[0], arrived[1]), pick(odd, arrived[1], arrived[0])])


def three_parts(values):
    high = lax.reduce_precision(values, 8, 7)
    rest = values - high
    middle = lax.reduce_precision(rest, 8, 7)
    low = rest - middle
    return jnp.stack([high, middle, low]).astype(jnp.bfloat16)


def clip_body(
    activations,
    cotangent,
    attn_gain,
    attn_shift,
    qkv_weight,
    qkv_bias,
    out_weight,
    out_bias,
    mlp_gain,
    mlp_shift,
    fc1_weight,
    fc1_bias,
    fc2_weight,
    fc2_bias,
):
    index = lax.axis_index("dp")
    core = index % 2
    at_x = index // 2 % 2
    at_y = index // 4
    width = activations.shape[2]
    length = activations.shape[1] * 4
    half_rows = length // 2
    own_rows = qkv_weight.shape[0]
    heads_here = qkv_weight.shape[1] // (3 * HD)
    half_heads = heads_here // 2
    qkv_cols = half_heads * 3 * HD
    out_cols = out_weight.shape[1] // 2
    unit_cols = fc1_weight.shape[1] // 2
    low = jnp.bfloat16

    def first_half(values):
        return lax.slice_in_dim(values, 0, values.shape[-1] // 2, axis=values.ndim - 1)

    def second_half(values):
        return lax.slice_in_dim(values, values.shape[-1] // 2, values.shape[-1], axis=values.ndim - 1)

    def own_half(values):
        return pick(core == 1, first_half(values), second_half(values))

    def other_half(values):
        return pick(core == 1, second_half(values), first_half(values))

    def by_kind(values):
        lead = values.shape[:-1]
        split = values.reshape(lead + (2, half_heads, 3, HD))
        return jnp.swapaxes(split, -3, -2).reshape(values.shape)

    def by_head(values):
        lead = values.shape[:-1]
        split = values.reshape(lead + (2, 3, half_heads, HD))
        return jnp.swapaxes(split, -3, -2).reshape(values.shape)

    tokens = to_clips(activations).astype(jnp.float32)

    columns = (by_kind(qkv_weight), out_weight, fc1_weight, fc2_weight)
    biases = (by_kind(qkv_bias), None, fc1_bias, None)
    mine = jnp.concatenate([own_half(item) for item in columns], axis=1)
    theirs = swap(jnp.concatenate([other_half(item) for item in columns], axis=1), SWAP_CORE)
    rows = jnp.stack([pick(core == 1, mine, theirs), pick(core == 1, theirs, mine)])

    def along_z(values):
        return jnp.stack([values] + [shift(values, step) for step in (1, 2, 3)], axis=values.ndim - 1)

    def over_plane(values):
        even, odd = values[0], values[1]
        even_x = swap(even, SWAP_X)
        odd_y = swap(odd, SWAP_Y)
        even = jnp.stack([pick(at_x == 1, even, even_x), pick(at_x == 1, even_x, even)])
        odd = jnp.stack([pick(at_y == 1, odd, odd_y), pick(at_y == 1, odd_y, odd)])
        even_y = swap(even, SWAP_Y)
        odd_x = swap(odd, SWAP_X)
        even = jnp.stack([pick(at_y == 1, even, even_y), pick(at_y == 1, even_y, even)])
        odd = jnp.stack([pick(at_x == 1, odd, odd_x), pick(at_x == 1, odd_x, odd)], axis=1)
        whole = jnp.stack([even, odd], axis=2)
        return whole.reshape((4 * 2 * own_rows, -1))

    bounds = [0, qkv_cols, qkv_cols + out_cols, qkv_cols + out_cols + unit_cols, qkv_cols + out_cols + 2 * unit_cols]

    def widened(part, bias):
        lines = jnp.zeros((16, part.shape[-1]), low)
        lines = lines.at[:3].set(three_parts(own_half(bias)))
        return jnp.concatenate([part.reshape(-1, part.shape[-1]), lines], axis=0)

    def parted(values, cols):
        body_rows, lines = values[: 2 * own_rows], values[2 * own_rows :]
        bias = jnp.sum(lines[:3].astype(jnp.float32), axis=0).reshape(-1)
        return body_rows.reshape(2, own_rows, 4, cols), bias

    qkv_z, bias_qkv = parted(along_z(widened(rows[:, :, : bounds[1]], biases[0])), qkv_cols)
    weight_qkv = over_plane(qkv_z)
    out_z = along_z(rows[:, :, bounds[1] : bounds[2]])
    weight_out = over_plane(out_z)
    up_z, bias_up = parted(along_z(widened(rows[:, :, bounds[2] : bounds[3]], biases[2])), unit_cols)
    weight_up = over_plane(up_z)
    down_z = along_z(rows[:, :, bounds[3] :])
    weight_down = over_plane(down_z)

    def both_halves(values):
        other = swap(values, SWAP_CORE)
        return jnp.concatenate([pick(core == 1, values, other), pick(core == 1, other, values)], axis=0)

    def part_sum(values):
        halves = values.reshape((2, half_rows) + values.shape[1:])
        sent = pick(core == 1, halves[1], halves[0]).astype(low)
        return pick(core == 1, halves[0], halves[1]) + swap(sent, SWAP_CORE).astype(jnp.float32)

    cosine, sine = (jnp.concatenate([item, item], axis=1) for item in rotary_tables(length))

    first_all = both_halves(norm_rows(tokens, attn_gain, attn_shift).astype(low))
    qkv, heads_out, turned, log_total = attend(first_all, weight_qkv, bias_qkv, cosine, sine)
    resid = tokens + part_sum(contract(heads_out, weight_out, 1, 1)) + out_bias
    second_all = both_halves(norm_rows(resid, mlp_gain, mlp_shift).astype(low))
    hidden = jnp.dot(second_all, weight_up, preferred_element_type=jnp.float32) + bias_up
    act = exact_gelu(hidden).astype(low)
    result = resid + part_sum(contract(act, weight_down, 1, 1)) + fc2_bias
    output = from_clips(result.astype(low))

    def to_owner(grad, cols):
        parts = grad.astype(low).reshape(2, 2, 2, own_rows, 4 * cols)
        even, odd = parts[:, :, 0], parts[:, :, 1]
        even = pick(at_y == 1, even[0], even[1]) + swap(pick(at_y == 1, even[1], even[0]), SWAP_Y)
        odd = pick(at_x == 1, odd[:, 0], odd[:, 1]) + swap(pick(at_x == 1, odd[:, 1], odd[:, 0]), SWAP_X)
        even = pick(at_x == 1, even[0], even[1]) + swap(pick(at_x == 1, even[1], even[0]), SWAP_X)
        odd = pick(at_y == 1, odd[0], odd[1]) + swap(pick(at_y == 1, odd[1], odd[0]), SWAP_Y)
        both = jnp.stack([even, odd]).reshape(2, own_rows, 4, cols)
        total = both[:, :, 0].astype(jnp.float32)
        for step in (1, 2, 3):
            total = total + shift(both[:, :, step], 4 - step).astype(jnp.float32)
        total = total.astype(low)
        kept = pick(core == 1, total[0], total[1])
        came = swap(pick(core == 1, total[1], total[0]), SWAP_CORE)
        return jnp.concatenate(
            [pick(core == 1, kept, came), pick(core == 1, came, kept)], axis=-1
        ).astype(jnp.float32)

    grad_own = to_clips(cotangent)
    grad_top = grad_own.astype(jnp.float32)
    grad_all = both_halves(grad_own)
    sum_fc2_bias = jnp.sum(grad_top, axis=0)
    grad_fc2_weight = to_owner(contract(grad_all, act, 0, 0), unit_cols)
    grad_act = jnp.dot(grad_all, weight_down, preferred_element_type=jnp.float32)
    grad_hidden = jax.vjp(exact_gelu, hidden)[1](grad_act)[0].astype(low)
    sum_fc1_bias = jnp.sum(grad_hidden, axis=0, dtype=jnp.float32)
    grad_fc1_weight = to_owner(contract(second_all, grad_hidden, 0, 0), unit_cols)
    grad_second = part_sum(contract(grad_hidden, weight_up, 1, 1))
    second_pull = jax.vjp(norm_rows, resid, mlp_gain, mlp_shift)[1]
    grad_resid_norm, sum_mlp_gain, sum_mlp_shift = second_pull(grad_second)
    grad_resid = grad_top + grad_resid_norm
    sum_out_bias = jnp.sum(grad_resid, axis=0)
    resid_all = both_halves(grad_resid.astype(low))
    grad_out_weight = to_owner(contract(resid_all, heads_out, 0, 0), out_cols)
    grad_heads = jnp.dot(resid_all, weight_out, preferred_element_type=jnp.float32).astype(low)
    grad_packed, sum_qkv_bias = attend_back(qkv, grad_heads, turned, log_total, cosine, sine)
    sum_qkv_bias = sum_qkv_bias.reshape(-1)
    grad_qkv_weight = by_head(to_owner(contract(first_all, grad_packed, 0, 0), qkv_cols))
    grad_first = part_sum(contract(grad_packed, weight_qkv, 1, 1))
    first_pull = jax.vjp(norm_rows, tokens, attn_gain, attn_shift)[1]
    grad_input_norm, sum_attn_gain, sum_attn_shift = first_pull(grad_first)
    input_grad = from_clips((grad_resid + grad_input_norm).astype(low)).astype(jnp.float32)

    def plane_total(values):
        values = values + swap(values, SWAP_X)
        return values + swap(values, SWAP_Y)

    def whole_total(values):
        values = plane_total(values)
        values = values + swap(values, SWAP_CORE)
        for bit in (1, 2):
            values = values + lax.ppermute(values, "tensor", [(i, i ^ bit) for i in range(4)])
        return values

    def bias_total(values, cols):
        blocks = plane_total(values).reshape(4, cols)
        total = blocks[0]
        for step in (1, 2, 3):
            total = total + shift(blocks[step], 4 - step)
        other = swap(total, SWAP_CORE)
        return jnp.concatenate([pick(core == 1, total, other), pick(core == 1, other, total)])

    early = whole_total(jnp.stack([sum_fc2_bias, sum_mlp_gain, sum_mlp_shift, sum_out_bias]))
    late = whole_total(jnp.stack([sum_attn_gain, sum_attn_shift]))
    return (
        output,
        input_grad,
        late[0],
        late[1],
        grad_qkv_weight,
        by_head(bias_total(sum_qkv_bias, qkv_cols)),
        grad_out_weight,
        early[3],
        early[1],
        early[2],
        grad_fc1_weight,
        bias_total(sum_fc1_bias, unit_cols),
        grad_fc2_weight,
        early[0],
    )


def solution(mesh):
    in_specs = (
        P("dp", "tensor", None),
        P("dp", "tensor", None),
        P(),
        P(),
        P("dp", "tensor"),
        P("tensor"),
        P("dp", "tensor"),
        P(),
        P(),
        P(),
        P("dp", "tensor"),
        P("tensor"),
        P("dp", "tensor"),
        P(),
    )
    out_specs = (
        P("dp", "tensor", None),
        P("dp", "tensor", None),
        P(),
        P(),
        P("dp", "tensor"),
        P("tensor"),
        P("dp", "tensor"),
        P(),
        P(),
        P(),
        P("dp", "tensor"),
        P("tensor"),
        P("dp", "tensor"),
        P(),
    )
    plan = clip_body if one_clip_per_chip(mesh) else body
    return jax.shard_map(plan, mesh=mesh, in_specs=in_specs, out_specs=out_specs, check_vma=False)
```

```python
import math

import jax
import jax.numpy as jnp
from jax import lax
from jax.experimental import pallas as pl
from jax.experimental.pallas import tpu as pltpu
from jax.sharding import PartitionSpec as P

HD = 64
GRID = 16


def norm_rows(values, gain_vec, shift_vec):
    row_mean = jnp.mean(values, axis=-1, keepdims=True)
    centred = values - row_mean
    variance = jnp.mean(centred * centred, axis=-1, keepdims=True)
    return centred * lax.rsqrt(variance + 1e-06) * gain_vec + shift_vec


def rotary_tables(length):
    section = 2 * (HD // 3 // 2)
    half = section // 2
    position = jnp.arange(length)
    frame = (position // (GRID * GRID)).astype(jnp.float32)
    row_pos = (position // GRID % GRID).astype(jnp.float32)
    col_pos = (position % GRID).astype(jnp.float32)
    omega = 1.0 / 10000.0 ** (jnp.arange(half).astype(jnp.float32) / half)
    pieces = [
        jnp.repeat(coordinate[:, None] * omega[None, :], 2, axis=1)
        for coordinate in (frame, row_pos, col_pos)
    ]
    pieces.append(jnp.zeros((length, HD - 3 * section), jnp.float32))
    angles = jnp.concatenate(pieces, axis=1)
    parity = jnp.where(jnp.arange(HD) % 2 == 0, -1.0, 1.0).astype(jnp.float32)
    return (jnp.cos(angles), jnp.sin(angles) * parity)


def pair_swap(values):
    shape = values.shape
    paired = values.reshape(shape[:-1] + (shape[-1] // 2, 2))
    return paired[..., ::-1].reshape(shape)


def contract(left, right, left_dim, right_dim):
    return lax.dot_general(
        left, right, (((left_dim,), (right_dim,)), ((), ())), preferred_element_type=jnp.float32
    )


def exact_gelu(values):
    return jax.nn.gelu(values, approximate=False)


def body(
    activations,
    cotangent,
    attn_gain,
    attn_shift,
    qkv_weight,
    qkv_bias,
    out_weight,
    out_bias,
    mlp_gain,
    mlp_shift,
    fc1_weight,
    fc1_bias,
    fc2_weight,
    fc2_bias,
):
    tensor_size = lax.axis_size("tensor")
    tensor_rank = lax.axis_index("tensor")
    row_count = activations.shape[1]
    width = activations.shape[2]
    length = row_count * tensor_size
    block_rows = min(512, length)
    block_count = length // block_rows
    local_heads = qkv_weight.shape[1] // (3 * HD)
    packed_cols = qkv_weight.shape[1]
    unit_cols = fc1_weight.shape[1]
    factor = 1.0 / math.sqrt(HD)
    cosine, sine = rotary_tables(length)
    cosine = cosine[:, None, :]
    sine = sine[:, None, :]

    def rotate(values):
        return values * cosine + pair_swap(values) * sine

    def rotate_back(values):
        return values * cosine + pair_swap(values * sine)

    def fetch():
        gathered = (
            lax.all_gather(qkv_weight, "dp", axis=0, tiled=True),
            lax.all_gather(out_weight, "dp", axis=0, tiled=True),
            lax.all_gather(fc1_weight, "dp", axis=0, tiled=True),
            lax.all_gather(fc2_weight, "dp", axis=0, tiled=True),
        )
        return (gathered, gathered)

    def seq_gather(values):
        return lax.all_gather(values, "tensor", axis=0, tiled=True)

    def part_sum(values):
        return lax.psum_scatter(
            values.astype(jnp.bfloat16), "tensor", scatter_dimension=0, tiled=True
        ).astype(jnp.float32)

    def grad_gather(values):
        return lax.all_gather(values, "tensor", axis=0, tiled=True)

    def grad_sum(values):
        return lax.psum_scatter(
            values.astype(jnp.bfloat16), "tensor", scatter_dimension=0, tiled=True
        ).astype(jnp.float32)

    def forward(inputs, weights):
        (weight_qkv, weight_out, weight_up, weight_down), (
            whole_qkv,
            whole_out,
            whole_up,
            whole_down,
        ) = weights
        first_all = seq_gather(norm_rows(inputs, attn_gain, attn_shift).astype(jnp.bfloat16))
        packed = (
            jnp.dot(first_all, weight_qkv, preferred_element_type=jnp.float32) + qkv_bias
        ).reshape(length, local_heads, 3, HD)
        query = rotate(packed[:, :, 0]).astype(jnp.bfloat16)
        key_all = rotate(packed[:, :, 1]).astype(jnp.bfloat16)
        value_all = packed[:, :, 2].astype(jnp.bfloat16)
        outputs = []
        log_sums = []
        for block in range(block_count):
            query_block = query[block * block_rows : (block + 1) * block_rows]
            scores = (
                jnp.einsum("qhd,khd->hqk", query_block, key_all, preferred_element_type=jnp.float32)
                * factor
            )
            row_max = jnp.max(scores, axis=-1, keepdims=True)
            expo = jnp.exp(scores - row_max)
            row_total = jnp.sum(expo, axis=-1, keepdims=True)
            weights_low = (expo / row_total).astype(jnp.bfloat16)
            outputs.append(
                jnp.einsum(
                    "hqk,khd->qhd", weights_low, value_all, preferred_element_type=jnp.float32
                )
            )
            log_sums.append(row_max + jnp.log(row_total))
        heads_out = (
            jnp.concatenate(outputs, axis=0).reshape(length, local_heads * HD).astype(jnp.bfloat16)
        )
        log_total = jnp.concatenate(log_sums, axis=1)
        attended = part_sum(contract(heads_out, weight_out, 1, 1))
        resid = inputs + attended + out_bias
        second_all = seq_gather(norm_rows(resid, mlp_gain, mlp_shift).astype(jnp.bfloat16))
        hidden = jnp.dot(second_all, weight_up, preferred_element_type=jnp.float32) + fc1_bias
        act = exact_gelu(hidden).astype(jnp.bfloat16)
        branch = part_sum(contract(act, weight_down, 1, 1))
        result = resid + branch + fc2_bias
        kept = (
            first_all,
            query,
            key_all,
            value_all,
            log_total,
            heads_out,
            heads_out,
            resid,
            second_all,
            hidden,
            act,
        )
        return (result, kept)

    def backward(inputs, grad_low, kept, weights):
        (weight_qkv, weight_out, weight_up, weight_down), (
            whole_qkv,
            whole_out,
            whole_up,
            whole_down,
        ) = weights
        (
            first_all,
            query,
            key_all,
            value_all,
            log_total,
            heads_out,
            heads_rows,
            resid,
            second_all,
            hidden,
            act,
        ) = kept
        grad_top = grad_low.astype(jnp.float32)
        grad_fc2_bias = jnp.sum(grad_top, axis=0)
        grad_all = grad_gather(grad_low)
        grad_fc2_weight = contract(grad_all, act, 0, 0)
        grad_act = jnp.dot(grad_all, weight_down, preferred_element_type=jnp.float32)
        gelu_pull = jax.vjp(exact_gelu, hidden)[1]
        grad_hidden = gelu_pull(grad_act)[0].astype(jnp.bfloat16)
        grad_fc1_bias = jnp.sum(grad_hidden, axis=0, dtype=jnp.float32)
        grad_fc1_weight = contract(second_all, grad_hidden, 0, 0)
        grad_second = grad_sum(contract(grad_hidden, weight_up, 1, 1))
        second_pull = jax.vjp(norm_rows, resid, mlp_gain, mlp_shift)[1]
        grad_resid_norm, grad_mlp_gain, grad_mlp_shift = second_pull(grad_second)
        grad_resid = grad_top + grad_resid_norm
        grad_out_bias = jnp.sum(grad_resid, axis=0)
        resid_low = grad_resid.astype(jnp.bfloat16)
        resid_all = grad_gather(resid_low)
        grad_out_weight = contract(resid_all, heads_out, 0, 0)
        grad_heads = jnp.dot(resid_all, weight_out, preferred_element_type=jnp.float32).astype(
            jnp.bfloat16
        )
        grad_heads = grad_heads.reshape(length, local_heads, HD)
        grad_key = jnp.zeros((length, local_heads, HD), jnp.float32)
        grad_value = jnp.zeros((length, local_heads, HD), jnp.float32)
        query_grads = []
        for block in range(block_count):
            lower = block * block_rows
            upper = lower + block_rows
            query_block = query[lower:upper]
            grad_block = grad_heads[lower:upper]
            scores = (
                jnp.einsum("qhd,khd->hqk", query_block, key_all, preferred_element_type=jnp.float32)
                * factor
            )
            probs = jnp.exp(scores - log_total[:, lower:upper])
            grad_value = grad_value + jnp.einsum(
                "hqk,qhd->khd",
                probs.astype(jnp.bfloat16),
                grad_block,
                preferred_element_type=jnp.float32,
            )
            grad_probs = jnp.einsum(
                "qhd,khd->hqk", grad_block, value_all, preferred_element_type=jnp.float32
            )
            grad_scores = (
                probs * (grad_probs - jnp.sum(probs * grad_probs, axis=-1, keepdims=True))
            ).astype(jnp.bfloat16)
            query_grads.append(
                jnp.einsum("hqk,khd->qhd", grad_scores, key_all, preferred_element_type=jnp.float32)
                * factor
            )
            grad_key = (
                grad_key
                + jnp.einsum(
                    "hqk,qhd->khd", grad_scores, query_block, preferred_element_type=jnp.float32
                )
                * factor
            )
        grad_query = jnp.concatenate(query_grads, axis=0)
        grad_packed = jnp.stack(
            [rotate_back(grad_query), rotate_back(grad_key), grad_value], axis=2
        )
        grad_packed = grad_packed.reshape(length, packed_cols).astype(jnp.bfloat16)
        grad_qkv_bias = jnp.sum(grad_packed, axis=0, dtype=jnp.float32)
        grad_qkv_weight = contract(first_all, grad_packed, 0, 0)
        grad_first = grad_sum(contract(grad_packed, weight_qkv, 1, 1))
        first_pull = jax.vjp(norm_rows, inputs, attn_gain, attn_shift)[1]
        grad_input_norm, grad_attn_gain, grad_attn_shift = first_pull(grad_first)
        input_grad = grad_resid + grad_input_norm
        grads = (
            grad_attn_gain,
            grad_attn_shift,
            grad_qkv_weight,
            grad_qkv_bias,
            grad_out_weight,
            grad_out_bias,
            grad_mlp_gain,
            grad_mlp_shift,
            grad_fc1_weight,
            grad_fc1_bias,
            grad_fc2_weight,
            grad_fc2_bias,
        )
        return (input_grad, grads)

    def per_clip(totals, inputs_pair):
        clip_in, clip_grad = inputs_pair
        forward_weights = fetch()
        result, kept = forward(clip_in.astype(jnp.float32), forward_weights)
        backward_weights = fetch()
        input_grad, grads = backward(clip_in.astype(jnp.float32), clip_grad, kept, backward_weights)
        totals = tuple((left + right for left, right in zip(totals, grads)))
        return (totals, (result.astype(jnp.bfloat16), input_grad))

    out_cols = local_heads * HD
    start_totals = (
        jnp.zeros((width,), jnp.float32),
        jnp.zeros((width,), jnp.float32),
        jnp.zeros((width, packed_cols), jnp.float32),
        jnp.zeros((packed_cols,), jnp.float32),
        jnp.zeros((width, out_cols), jnp.float32),
        jnp.zeros((width,), jnp.float32),
        jnp.zeros((width,), jnp.float32),
        jnp.zeros((width,), jnp.float32),
        jnp.zeros((width, unit_cols), jnp.float32),
        jnp.zeros((unit_cols,), jnp.float32),
        jnp.zeros((width, unit_cols), jnp.float32),
        jnp.zeros((width,), jnp.float32),
    )
    totals, (output, input_grad) = lax.scan(per_clip, start_totals, (activations, cotangent))
    out_grad = totals[4]
    weight_sums = (
        lax.psum_scatter(
            totals[2].astype(jnp.bfloat16), "dp", scatter_dimension=0, tiled=True
        ).astype(jnp.float32),
        lax.psum_scatter(
            out_grad.astype(jnp.bfloat16), "dp", scatter_dimension=0, tiled=True
        ).astype(jnp.float32),
        lax.psum_scatter(
            totals[8].astype(jnp.bfloat16), "dp", scatter_dimension=0, tiled=True
        ).astype(jnp.float32),
        lax.psum_scatter(
            totals[10].astype(jnp.bfloat16), "dp", scatter_dimension=0, tiled=True
        ).astype(jnp.float32),
    )
    qkv_place = lax.dynamic_update_slice_in_dim(
        jnp.zeros((packed_cols * tensor_size,), jnp.float32),
        totals[3],
        tensor_rank * packed_cols,
        0,
    )
    unit_place = lax.dynamic_update_slice_in_dim(
        jnp.zeros((unit_cols * tensor_size,), jnp.float32), totals[9], tensor_rank * unit_cols, 0
    )
    summed = lax.psum(
        (totals[0], totals[1], qkv_place, totals[5], totals[6], totals[7], unit_place, totals[11]),
        ("dp", "tensor"),
    )
    grad_qkv_bias = lax.dynamic_slice_in_dim(summed[2], tensor_rank * packed_cols, packed_cols, 0)
    grad_fc1_bias = lax.dynamic_slice_in_dim(summed[6], tensor_rank * unit_cols, unit_cols, 0)
    return (
        output,
        input_grad,
        summed[0],
        summed[1],
        weight_sums[0],
        grad_qkv_bias,
        weight_sums[1],
        summed[3],
        summed[4],
        summed[5],
        weight_sums[2],
        grad_fc1_bias,
        weight_sums[3],
        summed[7],
    )


def lane_swap(values):
    even = lax.broadcasted_iota(jnp.int32, values.shape, 1) % 2 == 0
    return jnp.where(even, pltpu.roll(values, 127, 1), pltpu.roll(values, 1, 1))


def attend_kernel(
    place_ref, first_ref, even_ref, odd_ref, bias_ref, cos_ref, sin_ref, qkv_ref, heads_ref, turned_ref, log_ref, weight_ref
):
    low = jnp.bfloat16
    rows = even_ref.shape[2]
    for at in range(4):
        weight_ref[2 * at * rows : (2 * at + 1) * rows] = even_ref[at ^ place_ref[0], 0]
        weight_ref[(2 * at + 1) * rows : (2 * at + 2) * rows] = odd_ref[at ^ place_ref[0], 0]
    packed = jnp.dot(first_ref[...], weight_ref[...], preferred_element_type=jnp.float32) + bias_ref[0]
    cosine, sine = cos_ref[...], sin_ref[...]

    def rotate(values):
        return values * cosine + lane_swap(values) * sine

    query = (rotate(packed[:, :128]).astype(low).astype(jnp.float32) * 0.125).astype(low)
    key = rotate(packed[:, 128:256]).astype(low)
    value = packed[:, 256:]
    qkv_ref[:, :128] = query
    qkv_ref[:, 128:256] = key
    qkv_ref[:, 256:] = value.astype(low)
    value = jnp.transpose(value).astype(low)
    first_head = lax.broadcasted_iota(jnp.int32, key.shape, 1) < HD
    for head in range(2):
        mine = slice(head * HD, (head + 1) * HD)
        key_here = jnp.where(first_head == (head == 0), key, jnp.zeros_like(key))
        scores = contract(key_here, query, 1, 1)
        top = jnp.max(scores, axis=0, keepdims=True)
        expo = jnp.exp(scores - top)
        total = jnp.sum(expo, axis=0, keepdims=True)
        summed = jnp.dot(value[mine], expo.astype(low), preferred_element_type=jnp.float32)
        turned_ref[0, mine] = summed / total
        log_ref[0, head : head + 1] = top + jnp.log(total)
    heads_ref[...] = jnp.transpose(turned_ref[0]).astype(low)


def attend(place, first, even, odd, bias, cosine, sine):
    length, width = first.shape
    rows = even.shape[2]
    pairs = even.shape[1]
    return pl.pallas_call(
        attend_kernel,
        grid_spec=pltpu.PrefetchScalarGridSpec(
            num_scalar_prefetch=1,
            grid=(pairs,),
            in_specs=[
                pl.BlockSpec((length, width), lambda i, place: (0, 0)),
                pl.BlockSpec((4, 1, rows, 384), lambda i, place: (0, i, 0, 0)),
                pl.BlockSpec((4, 1, rows, 384), lambda i, place: (0, i, 0, 0)),
                pl.BlockSpec((1, 1, 384), lambda i, place: (i, 0, 0)),
                pl.BlockSpec((length, 128), lambda i, place: (0, 0)),
                pl.BlockSpec((length, 128), lambda i, place: (0, 0)),
            ],
            out_specs=[
                pl.BlockSpec((length, 384), lambda i, place: (0, i)),
                pl.BlockSpec((length, 128), lambda i, place: (0, i ^ place[1])),
                pl.BlockSpec((1, 128, length), lambda i, place: (i, 0, 0)),
                pl.BlockSpec((1, 2, length), lambda i, place: (i, 0, 0)),
                pl.BlockSpec((width, 384), lambda i, place: (0, i)),
            ],
        ),
        out_shape=[
            jax.ShapeDtypeStruct((length, 384 * pairs), jnp.bfloat16),
            jax.ShapeDtypeStruct((length, 128 * pairs), jnp.bfloat16),
            jax.ShapeDtypeStruct((pairs, 128, length), jnp.float32),
            jax.ShapeDtypeStruct((pairs, 2, length), jnp.float32),
            jax.ShapeDtypeStruct((width, 384 * pairs), jnp.bfloat16),
        ],
        name="attend",
    )(place, first, even, odd, bias.reshape(pairs, 1, 384), cosine, sine)


def attend_back_kernel(place_ref, qkv_ref, grad_ref, turned_ref, log_ref, cos_ref, sin_ref, out_ref, bias_ref):
    low = jnp.bfloat16
    query = qkv_ref[:, :128]
    key = qkv_ref[:, 128:256]
    value = qkv_ref[:, 256:]
    grad = grad_ref[...]
    key_turned = jnp.transpose(key.astype(jnp.float32)).astype(low)
    product = jnp.transpose(grad.astype(jnp.float32)) * turned_ref[0]
    first_head = lax.broadcasted_iota(jnp.int32, key.shape, 1) < HD
    zero = jnp.zeros_like(key)
    query_grads, key_grads, value_grads = [], [], []
    for head in range(2):
        mine = slice(head * HD, (head + 1) * HD)
        here = first_head == (head == 0)
        delta = jnp.sum(product[mine], axis=0, keepdims=True)
        scores = contract(jnp.where(here, key, zero), query, 1, 1)
        probs = jnp.exp(scores - log_ref[0, head : head + 1])
        grad_probs = contract(jnp.where(here, value, zero), grad, 1, 1)
        grad_scores = (probs * (grad_probs - delta)).astype(low)
        value_grads.append(jnp.dot(probs.astype(low), grad, preferred_element_type=jnp.float32))
        key_grads.append(jnp.dot(grad_scores, query, preferred_element_type=jnp.float32))
        query_grads.append(jnp.dot(key_turned[mine], grad_scores, preferred_element_type=jnp.float32))
    cosine, sine = cos_ref[...], sin_ref[...]

    def rotate_back(values):
        return values * cosine + lane_swap(values * sine)

    parts = [
        rotate_back(jnp.transpose(jnp.concatenate(query_grads, axis=0)) * 0.125),
        rotate_back(jnp.where(first_head, key_grads[0], key_grads[1])),
        jnp.where(first_head, value_grads[0], value_grads[1]),
    ]
    for at, part in enumerate(parts):
        part = part.astype(low)
        out_ref[:, at * 128 : (at + 1) * 128] = part
        bias_ref[0, :, at * 128 : (at + 1) * 128] = jnp.sum(part.astype(jnp.float32), axis=0, keepdims=True)


def attend_back(place, qkv, grad, turned, logs, cosine, sine):
    length = qkv.shape[0]
    pairs = qkv.shape[1] // 384
    return pl.pallas_call(
        attend_back_kernel,
        grid_spec=pltpu.PrefetchScalarGridSpec(
            num_scalar_prefetch=1,
            grid=(pairs,),
            in_specs=[
                pl.BlockSpec((length, 384), lambda i, place: (0, i)),
                pl.BlockSpec((length, 128), lambda i, place: (0, i ^ place[1])),
                pl.BlockSpec((1, 128, length), lambda i, place: (i, 0, 0)),
                pl.BlockSpec((1, 2, length), lambda i, place: (i, 0, 0)),
                pl.BlockSpec((length, 128), lambda i, place: (0, 0)),
                pl.BlockSpec((length, 128), lambda i, place: (0, 0)),
            ],
            out_specs=[
                pl.BlockSpec((length, 384), lambda i, place: (0, i)),
                pl.BlockSpec((1, 1, 384), lambda i, place: (i ^ place[1], 0, 0)),
            ],
        ),
        out_shape=[
            jax.ShapeDtypeStruct((length, 384 * pairs), jnp.bfloat16),
            jax.ShapeDtypeStruct((pairs, 1, 384), jnp.float32),
        ],
        name="attend_back",
    )(place, qkv, grad, turned, logs, cosine, sine)


PLANE = ("y", "x", "tensor")
EVERY = ("y", "x", "core", "tensor")


def one_clip_per_chip(mesh):
    return mesh.shape["dp"] == 8 and mesh.shape["tensor"] == 4


def swap(values, axis, bit=1):
    return lax.ppermute(values, axis, [(i, i ^ bit) for i in range(4 if axis == "tensor" else 2)])


def clip_routes(back):
    routes = []
    for turn in range(2):
        pairs = []
        for column in range(4):
            for core in range(2):
                for place in range(4):
                    source = (2 * column + core) * 4 + place
                    target = (2 * column + place // 2) * 4 + 2 * core + (turn ^ (place % 2))
                    pairs.append((target, source) if back else (source, target))
        routes.append(pairs)
    return routes


def pick(flag, first, second):
    return jnp.where(flag, second, first)


def to_clips(values):
    odd = lax.axis_index("tensor") % 2 == 1
    arrived = []
    for turn, pairs in enumerate(clip_routes(False)):
        sent = pick(odd, values[turn], values[1 - turn])
        arrived.append(lax.ppermute(sent, EVERY, pairs))
    return jnp.concatenate(
        [pick(odd, arrived[0], arrived[1]), pick(odd, arrived[1], arrived[0])], axis=0
    )


def from_clips(values):
    odd = lax.axis_index("tensor") % 2 == 1
    rows = values.shape[0] // 2
    arrived = []
    for turn, pairs in enumerate(clip_routes(True)):
        sent = pick(odd, values[turn * rows : (turn + 1) * rows], values[(1 - turn) * rows : (2 - turn) * rows])
        arrived.append(lax.ppermute(sent, EVERY, pairs))
    return jnp.stack([pick(odd, arrived[0], arrived[1]), pick(odd, arrived[1], arrived[0])])


def three_parts(values):
    high = lax.reduce_precision(values, 8, 7)
    rest = values - high
    middle = lax.reduce_precision(rest, 8, 7)
    low = rest - middle
    return jnp.stack([high, middle, low]).astype(jnp.bfloat16)


def clip_body(
    activations,
    cotangent,
    attn_gain,
    attn_shift,
    qkv_weight,
    qkv_bias,
    out_weight,
    out_bias,
    mlp_gain,
    mlp_shift,
    fc1_weight,
    fc1_bias,
    fc2_weight,
    fc2_bias,
):
    core, at_x, at_y, at_z = (lax.axis_index(name) for name in ("core", "x", "y", "tensor"))
    place = jnp.stack([2 * at_y + at_x, at_z]).astype(jnp.int32)
    width = activations.shape[2]
    length = activations.shape[1] * 4
    half_rows = length // 2
    own_rows = qkv_weight.shape[0]
    half_heads = qkv_weight.shape[1] // (6 * HD)
    qkv_cols = half_heads * 3 * HD
    out_cols = out_weight.shape[1] // 2
    unit_cols = fc1_weight.shape[1] // 2
    low = jnp.bfloat16

    def first_half(values):
        return lax.slice_in_dim(values, 0, values.shape[-1] // 2, axis=values.ndim - 1)

    def second_half(values):
        return lax.slice_in_dim(values, values.shape[-1] // 2, values.shape[-1], axis=values.ndim - 1)

    def own_half(values):
        return pick(core == 1, first_half(values), second_half(values))

    def other_half(values):
        return pick(core == 1, second_half(values), first_half(values))

    def by_kind(values):
        lead = values.shape[:-1]
        split = values.reshape(lead + (2, half_heads, 3, HD))
        return jnp.swapaxes(split, -3, -2).reshape(values.shape)

    def by_head(values):
        lead = values.shape[:-1]
        split = values.reshape(lead + (2, 3, half_heads, HD))
        return jnp.swapaxes(split, -3, -2).reshape(values.shape)

    tokens = to_clips(activations).astype(jnp.float32)

    columns = (by_kind(qkv_weight), out_weight, fc1_weight, fc2_weight)
    mine = jnp.concatenate([own_half(item) for item in columns], axis=1)
    theirs = swap(jnp.concatenate([other_half(item) for item in columns], axis=1), "core")
    held = jnp.concatenate([pick(core == 1, mine, theirs), pick(core == 1, theirs, mine)], axis=0)

    lines = jnp.concatenate([own_half(by_kind(qkv_bias)), own_half(fc1_bias)])
    lines = jnp.pad(three_parts(lines), ((0, 0), (0, 3 * qkv_cols - lines.shape[0]))).reshape(9, qkv_cols)
    near = jnp.concatenate([held[:, :qkv_cols], lines, jnp.zeros((7, qkv_cols), low)], axis=0)[None]
    near = jnp.concatenate([near, swap(near, "tensor", 1)])
    near = jnp.concatenate([near, swap(near, "tensor", 2)])
    lines = near[:, 2 * own_rows : 2 * own_rows + 9].astype(jnp.float32).reshape(4, 3, 3 * qkv_cols).sum(axis=1)
    bias_qkv = lines[:, :qkv_cols]
    bias_up = lines[:, qkv_cols : qkv_cols + unit_cols]
    bias_up = pick(at_z % 2 == 1, bias_up, bias_up[jnp.array([1, 0, 3, 2])])
    bias_up = pick(at_z // 2 == 1, bias_up, bias_up[jnp.array([2, 3, 0, 1])]).reshape(-1)
    even = near[None, :, :own_rows]
    odd = near[None, :, own_rows : 2 * own_rows]
    even = jnp.concatenate([even, swap(even, "x")])
    odd = jnp.concatenate([odd, swap(odd, "y")])
    even = jnp.concatenate([even, swap(even, "y")])
    odd_x = swap(odd, "x")
    odd = jnp.stack([odd[0], odd_x[0], odd[1], odd_x[1]])

    others = lax.all_gather(held[:, qkv_cols:], PLANE, axis=0, tiled=True).reshape(4, 4, 2 * own_rows, -1)

    def whole(lower, upper):
        return jnp.swapaxes(others[..., lower:upper], 1, 2).reshape(8 * own_rows, -1)

    weight_out = whole(0, out_cols)
    weight_up = whole(out_cols, out_cols + unit_cols)
    weight_down = whole(out_cols + unit_cols, out_cols + 2 * unit_cols)

    def both_halves(values):
        other = swap(values, "core")
        return jnp.concatenate([pick(core == 1, values, other), pick(core == 1, other, values)], axis=0)

    def part_sum(values):
        halves = values.reshape((2, half_rows) + values.shape[1:])
        sent = pick(core == 1, halves[1], halves[0]).astype(low)
        return pick(core == 1, halves[0], halves[1]) + swap(sent, "core").astype(jnp.float32)

    cosine, sine = (jnp.concatenate([item, item], axis=1) for item in rotary_tables(length))

    first_all = both_halves(norm_rows(tokens, attn_gain, attn_shift).astype(low))
    qkv, heads_out, turned, log_total, weight_qkv = attend(place, first_all, even, odd, bias_qkv, cosine, sine)
    resid = tokens + part_sum(contract(heads_out, weight_out, 1, 1)) + out_bias
    second_all = both_halves(norm_rows(resid, mlp_gain, mlp_shift).astype(low))
    hidden = jnp.dot(second_all, weight_up, preferred_element_type=jnp.float32) + bias_up
    act = exact_gelu(hidden).astype(low)
    result = resid + part_sum(contract(act, weight_down, 1, 1)) + fc2_bias
    output = from_clips(result.astype(low))

    def to_core(total):
        kept = pick(core == 1, total[0], total[1])
        came = swap(pick(core == 1, total[1], total[0]), "core")
        return jnp.concatenate(
            [pick(core == 1, kept, came), pick(core == 1, came, kept)], axis=-1
        ).astype(jnp.float32)

    def to_owner(grad, cols, relative):
        parts = grad.astype(low).reshape(2, 2, 2, own_rows, 4, cols)
        even, odd = parts[:, :, 0], parts[:, :, 1]
        even = pick(at_y == 1, even[0], even[1]) + swap(pick(at_y == 1, even[1], even[0]), "y")
        odd = pick(at_x == 1, odd[:, 0], odd[:, 1]) + swap(pick(at_x == 1, odd[:, 1], odd[:, 0]), "x")
        even = pick(at_x == 1, even[0], even[1]) + swap(pick(at_x == 1, even[1], even[0]), "x")
        odd = pick(at_y == 1, odd[0], odd[1]) + swap(pick(at_y == 1, odd[1], odd[0]), "y")
        both = jnp.stack([even, odd])
        if relative:
            both = both[:, :, :2] + swap(both[:, :, 2:], "tensor", 2)
            both = both[:, :, 0] + swap(both[:, :, 1], "tensor", 1)
        else:
            high = at_z // 2 == 1
            both = pick(high, both[:, :, :2], both[:, :, 2:]) + swap(pick(high, both[:, :, 2:], both[:, :, :2]), "tensor", 2)
            one = at_z % 2 == 1
            both = pick(one, both[:, :, 0], both[:, :, 1]) + swap(pick(one, both[:, :, 1], both[:, :, 0]), "tensor", 1)
        return to_core(both)

    def scattered(grad, cols):
        parts = jnp.swapaxes(grad.astype(low).reshape(4, 2 * own_rows, 4, cols), 1, 2)
        total = lax.psum_scatter(parts.reshape(-1, cols), PLANE, scatter_dimension=0, tiled=True)
        return to_core(total.reshape(2, own_rows, cols))

    grad_own = to_clips(cotangent)
    grad_top = grad_own.astype(jnp.float32)
    grad_all = both_halves(grad_own)
    sum_fc2_bias = jnp.sum(grad_top, axis=0)
    grad_fc2_weight = scattered(contract(grad_all, act, 0, 0), unit_cols)
    grad_act = jnp.dot(grad_all, weight_down, preferred_element_type=jnp.float32)
    grad_hidden = jax.vjp(exact_gelu, hidden)[1](grad_act)[0].astype(low)
    sum_fc1_bias = jnp.sum(grad_hidden, axis=0, dtype=jnp.float32)
    grad_fc1_weight = to_owner(contract(second_all, grad_hidden, 0, 0), unit_cols, False)
    grad_second = part_sum(contract(grad_hidden, weight_up, 1, 1))
    second_pull = jax.vjp(norm_rows, resid, mlp_gain, mlp_shift)[1]
    grad_resid_norm, sum_mlp_gain, sum_mlp_shift = second_pull(grad_second)
    grad_resid = grad_top + grad_resid_norm
    sum_out_bias = jnp.sum(grad_resid, axis=0)
    resid_all = both_halves(grad_resid.astype(low))
    grad_out_weight = to_owner(contract(resid_all, heads_out, 0, 0), out_cols, False)
    grad_heads = jnp.dot(resid_all, weight_out, preferred_element_type=jnp.float32).astype(low)
    grad_packed, sum_qkv_bias = attend_back(place, qkv, grad_heads, turned, log_total, cosine, sine)
    grad_qkv_weight = by_head(to_owner(contract(first_all, grad_packed, 0, 0), qkv_cols, True))
    grad_first = part_sum(contract(grad_packed, weight_qkv, 1, 1))
    first_pull = jax.vjp(norm_rows, tokens, attn_gain, attn_shift)[1]
    grad_input_norm, sum_attn_gain, sum_attn_shift = first_pull(grad_first)
    input_grad = from_clips((grad_resid + grad_input_norm).astype(low)).astype(jnp.float32)

    def by_core(values):
        none = jnp.zeros_like(values)
        return [pick(core == 1, values, none), pick(core == 1, none, values)]

    sums = [sum_attn_gain, sum_attn_shift, sum_out_bias, sum_mlp_gain, sum_mlp_shift, sum_fc2_bias]
    sums = jnp.concatenate(sums + by_core(sum_qkv_bias.reshape(-1)) + by_core(sum_fc1_bias))
    for axis, bit in (("core", 1), ("x", 1), ("y", 1), ("tensor", 1), ("tensor", 2)):
        sums = sums + swap(sums, axis, bit)
    vectors = sums[: 6 * width].reshape(6, width)
    qkv_sums = sums[6 * width : 6 * width + 8 * qkv_cols].reshape(2, 4, qkv_cols)
    unit_sums = sums[6 * width + 8 * qkv_cols :].reshape(2, 4, unit_cols)

    def own_place(values):
        return lax.dynamic_index_in_dim(values, at_z, 1, keepdims=False).reshape(-1)

    return (
        output,
        input_grad,
        vectors[0],
        vectors[1],
        grad_qkv_weight,
        by_head(own_place(qkv_sums)),
        grad_out_weight,
        vectors[2],
        vectors[3],
        vectors[4],
        grad_fc1_weight,
        own_place(unit_sums),
        grad_fc2_weight,
        vectors[5],
    )


def solution(mesh):
    if one_clip_per_chip(mesh):
        plan, rows = clip_body, ("y", "x", "core")
        mesh = jax.sharding.Mesh(mesh.devices.reshape(2, 2, 2, 4), EVERY)
    else:
        plan, rows = body, "dp"
    tokens, matrix, columns = P(rows, "tensor", None), P(rows, "tensor"), P("tensor")
    params = (P(), P(), matrix, columns, matrix, P(), P(), P(), matrix, columns, matrix, P())
    both = (tokens, tokens) + params
    return jax.shard_map(plan, mesh=mesh, in_specs=both, out_specs=both, check_vma=False)
```

```python
import math

import jax
import jax.numpy as jnp
from jax import lax
from jax.experimental import pallas as pl
from jax.experimental.pallas import tpu as pltpu
from jax.sharding import PartitionSpec as P

HD = 64
GRID = 16


def norm_rows(values, gain_vec, shift_vec):
    row_mean = jnp.mean(values, axis=-1, keepdims=True)
    centred = values - row_mean
    variance = jnp.mean(centred * centred, axis=-1, keepdims=True)
    return centred * lax.rsqrt(variance + 1e-06) * gain_vec + shift_vec


def rotary_tables(length):
    section = 2 * (HD // 3 // 2)
    half = section // 2
    position = jnp.arange(length)
    frame = (position // (GRID * GRID)).astype(jnp.float32)
    row_pos = (position // GRID % GRID).astype(jnp.float32)
    col_pos = (position % GRID).astype(jnp.float32)
    omega = 1.0 / 10000.0 ** (jnp.arange(half).astype(jnp.float32) / half)
    pieces = [
        jnp.repeat(coordinate[:, None] * omega[None, :], 2, axis=1)
        for coordinate in (frame, row_pos, col_pos)
    ]
    pieces.append(jnp.zeros((length, HD - 3 * section), jnp.float32))
    angles = jnp.concatenate(pieces, axis=1)
    parity = jnp.where(jnp.arange(HD) % 2 == 0, -1.0, 1.0).astype(jnp.float32)
    return (jnp.cos(angles), jnp.sin(angles) * parity)


def pair_swap(values):
    shape = values.shape
    paired = values.reshape(shape[:-1] + (shape[-1] // 2, 2))
    return paired[..., ::-1].reshape(shape)


def contract(left, right, left_dim, right_dim):
    return lax.dot_general(
        left, right, (((left_dim,), (right_dim,)), ((), ())), preferred_element_type=jnp.float32
    )


def exact_gelu(values):
    return jax.nn.gelu(values, approximate=False)


def body(
    activations,
    cotangent,
    attn_gain,
    attn_shift,
    qkv_weight,
    qkv_bias,
    out_weight,
    out_bias,
    mlp_gain,
    mlp_shift,
    fc1_weight,
    fc1_bias,
    fc2_weight,
    fc2_bias,
):
    tensor_size = lax.axis_size("tensor")
    tensor_rank = lax.axis_index("tensor")
    row_count = activations.shape[1]
    width = activations.shape[2]
    length = row_count * tensor_size
    block_rows = min(512, length)
    block_count = length // block_rows
    local_heads = qkv_weight.shape[1] // (3 * HD)
    packed_cols = qkv_weight.shape[1]
    unit_cols = fc1_weight.shape[1]
    factor = 1.0 / math.sqrt(HD)
    cosine, sine = rotary_tables(length)
    cosine = cosine[:, None, :]
    sine = sine[:, None, :]

    def rotate(values):
        return values * cosine + pair_swap(values) * sine

    def rotate_back(values):
        return values * cosine + pair_swap(values * sine)

    def fetch():
        gathered = (
            lax.all_gather(qkv_weight, "dp", axis=0, tiled=True),
            lax.all_gather(out_weight, "dp", axis=0, tiled=True),
            lax.all_gather(fc1_weight, "dp", axis=0, tiled=True),
            lax.all_gather(fc2_weight, "dp", axis=0, tiled=True),
        )
        return (gathered, gathered)

    def seq_gather(values):
        return lax.all_gather(values, "tensor", axis=0, tiled=True)

    def part_sum(values):
        return lax.psum_scatter(
            values.astype(jnp.bfloat16), "tensor", scatter_dimension=0, tiled=True
        ).astype(jnp.float32)

    def grad_gather(values):
        return lax.all_gather(values, "tensor", axis=0, tiled=True)

    def grad_sum(values):
        return lax.psum_scatter(
            values.astype(jnp.bfloat16), "tensor", scatter_dimension=0, tiled=True
        ).astype(jnp.float32)

    def forward(inputs, weights):
        (weight_qkv, weight_out, weight_up, weight_down), (
            whole_qkv,
            whole_out,
            whole_up,
            whole_down,
        ) = weights
        first_all = seq_gather(norm_rows(inputs, attn_gain, attn_shift).astype(jnp.bfloat16))
        packed = (
            jnp.dot(first_all, weight_qkv, preferred_element_type=jnp.float32) + qkv_bias
        ).reshape(length, local_heads, 3, HD)
        query = rotate(packed[:, :, 0]).astype(jnp.bfloat16)
        key_all = rotate(packed[:, :, 1]).astype(jnp.bfloat16)
        value_all = packed[:, :, 2].astype(jnp.bfloat16)
        outputs = []
        log_sums = []
        for block in range(block_count):
            query_block = query[block * block_rows : (block + 1) * block_rows]
            scores = (
                jnp.einsum("qhd,khd->hqk", query_block, key_all, preferred_element_type=jnp.float32)
                * factor
            )
            row_max = jnp.max(scores, axis=-1, keepdims=True)
            expo = jnp.exp(scores - row_max)
            row_total = jnp.sum(expo, axis=-1, keepdims=True)
            weights_low = (expo / row_total).astype(jnp.bfloat16)
            outputs.append(
                jnp.einsum(
                    "hqk,khd->qhd", weights_low, value_all, preferred_element_type=jnp.float32
                )
            )
            log_sums.append(row_max + jnp.log(row_total))
        heads_out = (
            jnp.concatenate(outputs, axis=0).reshape(length, local_heads * HD).astype(jnp.bfloat16)
        )
        log_total = jnp.concatenate(log_sums, axis=1)
        attended = part_sum(contract(heads_out, weight_out, 1, 1))
        resid = inputs + attended + out_bias
        second_all = seq_gather(norm_rows(resid, mlp_gain, mlp_shift).astype(jnp.bfloat16))
        hidden = jnp.dot(second_all, weight_up, preferred_element_type=jnp.float32) + fc1_bias
        act = exact_gelu(hidden).astype(jnp.bfloat16)
        branch = part_sum(contract(act, weight_down, 1, 1))
        result = resid + branch + fc2_bias
        kept = (
            first_all,
            query,
            key_all,
            value_all,
            log_total,
            heads_out,
            heads_out,
            resid,
            second_all,
            hidden,
            act,
        )
        return (result, kept)

    def backward(inputs, grad_low, kept, weights):
        (weight_qkv, weight_out, weight_up, weight_down), (
            whole_qkv,
            whole_out,
            whole_up,
            whole_down,
        ) = weights
        (
            first_all,
            query,
            key_all,
            value_all,
            log_total,
            heads_out,
            heads_rows,
            resid,
            second_all,
            hidden,
            act,
        ) = kept
        grad_top = grad_low.astype(jnp.float32)
        grad_fc2_bias = jnp.sum(grad_top, axis=0)
        grad_all = grad_gather(grad_low)
        grad_fc2_weight = contract(grad_all, act, 0, 0)
        grad_act = jnp.dot(grad_all, weight_down, preferred_element_type=jnp.float32)
        gelu_pull = jax.vjp(exact_gelu, hidden)[1]
        grad_hidden = gelu_pull(grad_act)[0].astype(jnp.bfloat16)
        grad_fc1_bias = jnp.sum(grad_hidden, axis=0, dtype=jnp.float32)
        grad_fc1_weight = contract(second_all, grad_hidden, 0, 0)
        grad_second = grad_sum(contract(grad_hidden, weight_up, 1, 1))
        second_pull = jax.vjp(norm_rows, resid, mlp_gain, mlp_shift)[1]
        grad_resid_norm, grad_mlp_gain, grad_mlp_shift = second_pull(grad_second)
        grad_resid = grad_top + grad_resid_norm
        grad_out_bias = jnp.sum(grad_resid, axis=0)
        resid_low = grad_resid.astype(jnp.bfloat16)
        resid_all = grad_gather(resid_low)
        grad_out_weight = contract(resid_all, heads_out, 0, 0)
        grad_heads = jnp.dot(resid_all, weight_out, preferred_element_type=jnp.float32).astype(
            jnp.bfloat16
        )
        grad_heads = grad_heads.reshape(length, local_heads, HD)
        grad_key = jnp.zeros((length, local_heads, HD), jnp.float32)
        grad_value = jnp.zeros((length, local_heads, HD), jnp.float32)
        query_grads = []
        for block in range(block_count):
            lower = block * block_rows
            upper = lower + block_rows
            query_block = query[lower:upper]
            grad_block = grad_heads[lower:upper]
            scores = (
                jnp.einsum("qhd,khd->hqk", query_block, key_all, preferred_element_type=jnp.float32)
                * factor
            )
            probs = jnp.exp(scores - log_total[:, lower:upper])
            grad_value = grad_value + jnp.einsum(
                "hqk,qhd->khd",
                probs.astype(jnp.bfloat16),
                grad_block,
                preferred_element_type=jnp.float32,
            )
            grad_probs = jnp.einsum(
                "qhd,khd->hqk", grad_block, value_all, preferred_element_type=jnp.float32
            )
            grad_scores = (
                probs * (grad_probs - jnp.sum(probs * grad_probs, axis=-1, keepdims=True))
            ).astype(jnp.bfloat16)
            query_grads.append(
                jnp.einsum("hqk,khd->qhd", grad_scores, key_all, preferred_element_type=jnp.float32)
                * factor
            )
            grad_key = (
                grad_key
                + jnp.einsum(
                    "hqk,qhd->khd", grad_scores, query_block, preferred_element_type=jnp.float32
                )
                * factor
            )
        grad_query = jnp.concatenate(query_grads, axis=0)
        grad_packed = jnp.stack(
            [rotate_back(grad_query), rotate_back(grad_key), grad_value], axis=2
        )
        grad_packed = grad_packed.reshape(length, packed_cols).astype(jnp.bfloat16)
        grad_qkv_bias = jnp.sum(grad_packed, axis=0, dtype=jnp.float32)
        grad_qkv_weight = contract(first_all, grad_packed, 0, 0)
        grad_first = grad_sum(contract(grad_packed, weight_qkv, 1, 1))
        first_pull = jax.vjp(norm_rows, inputs, attn_gain, attn_shift)[1]
        grad_input_norm, grad_attn_gain, grad_attn_shift = first_pull(grad_first)
        input_grad = grad_resid + grad_input_norm
        grads = (
            grad_attn_gain,
            grad_attn_shift,
            grad_qkv_weight,
            grad_qkv_bias,
            grad_out_weight,
            grad_out_bias,
            grad_mlp_gain,
            grad_mlp_shift,
            grad_fc1_weight,
            grad_fc1_bias,
            grad_fc2_weight,
            grad_fc2_bias,
        )
        return (input_grad, grads)

    def per_clip(totals, inputs_pair):
        clip_in, clip_grad = inputs_pair
        forward_weights = fetch()
        result, kept = forward(clip_in.astype(jnp.float32), forward_weights)
        backward_weights = fetch()
        input_grad, grads = backward(clip_in.astype(jnp.float32), clip_grad, kept, backward_weights)
        totals = tuple((left + right for left, right in zip(totals, grads)))
        return (totals, (result.astype(jnp.bfloat16), input_grad))

    out_cols = local_heads * HD
    start_totals = (
        jnp.zeros((width,), jnp.float32),
        jnp.zeros((width,), jnp.float32),
        jnp.zeros((width, packed_cols), jnp.float32),
        jnp.zeros((packed_cols,), jnp.float32),
        jnp.zeros((width, out_cols), jnp.float32),
        jnp.zeros((width,), jnp.float32),
        jnp.zeros((width,), jnp.float32),
        jnp.zeros((width,), jnp.float32),
        jnp.zeros((width, unit_cols), jnp.float32),
        jnp.zeros((unit_cols,), jnp.float32),
        jnp.zeros((width, unit_cols), jnp.float32),
        jnp.zeros((width,), jnp.float32),
    )
    totals, (output, input_grad) = lax.scan(per_clip, start_totals, (activations, cotangent))
    out_grad = totals[4]
    weight_sums = (
        lax.psum_scatter(
            totals[2].astype(jnp.bfloat16), "dp", scatter_dimension=0, tiled=True
        ).astype(jnp.float32),
        lax.psum_scatter(
            out_grad.astype(jnp.bfloat16), "dp", scatter_dimension=0, tiled=True
        ).astype(jnp.float32),
        lax.psum_scatter(
            totals[8].astype(jnp.bfloat16), "dp", scatter_dimension=0, tiled=True
        ).astype(jnp.float32),
        lax.psum_scatter(
            totals[10].astype(jnp.bfloat16), "dp", scatter_dimension=0, tiled=True
        ).astype(jnp.float32),
    )
    qkv_place = lax.dynamic_update_slice_in_dim(
        jnp.zeros((packed_cols * tensor_size,), jnp.float32),
        totals[3],
        tensor_rank * packed_cols,
        0,
    )
    unit_place = lax.dynamic_update_slice_in_dim(
        jnp.zeros((unit_cols * tensor_size,), jnp.float32), totals[9], tensor_rank * unit_cols, 0
    )
    summed = lax.psum(
        (totals[0], totals[1], qkv_place, totals[5], totals[6], totals[7], unit_place, totals[11]),
        ("dp", "tensor"),
    )
    grad_qkv_bias = lax.dynamic_slice_in_dim(summed[2], tensor_rank * packed_cols, packed_cols, 0)
    grad_fc1_bias = lax.dynamic_slice_in_dim(summed[6], tensor_rank * unit_cols, unit_cols, 0)
    return (
        output,
        input_grad,
        summed[0],
        summed[1],
        weight_sums[0],
        grad_qkv_bias,
        weight_sums[1],
        summed[3],
        summed[4],
        summed[5],
        weight_sums[2],
        grad_fc1_bias,
        weight_sums[3],
        summed[7],
    )


def lane_swap(values):
    even = lax.broadcasted_iota(jnp.int32, values.shape, 1) % 2 == 0
    return jnp.where(even, pltpu.roll(values, 127, 1), pltpu.roll(values, 1, 1))


def attend_kernel(first_ref, weight_ref, bias_ref, cos_ref, sin_ref, qkv_ref, heads_ref, turned_ref, log_ref):
    low = jnp.bfloat16
    packed = jnp.dot(first_ref[...], weight_ref[...], preferred_element_type=jnp.float32) + bias_ref[...]
    cosine, sine = cos_ref[...], sin_ref[...]

    def rotate(values):
        return values * cosine + lane_swap(values) * sine

    query = (rotate(packed[:, :128]).astype(low).astype(jnp.float32) * 0.125).astype(low)
    key = rotate(packed[:, 128:256]).astype(low)
    value = packed[:, 256:]
    qkv_ref[:, :128] = query
    qkv_ref[:, 128:256] = key
    qkv_ref[:, 256:] = value.astype(low)
    value = jnp.transpose(value).astype(low)
    first_head = lax.broadcasted_iota(jnp.int32, key.shape, 1) < HD
    for head in range(2):
        mine = slice(head * HD, (head + 1) * HD)
        key_here = jnp.where(first_head == (head == 0), key, jnp.zeros_like(key))
        scores = contract(key_here, query, 1, 1)
        top = jnp.max(scores, axis=0, keepdims=True)
        expo = jnp.exp(scores - top)
        total = jnp.sum(expo, axis=0, keepdims=True)
        summed = jnp.dot(value[mine], expo.astype(low), preferred_element_type=jnp.float32)
        turned_ref[0, mine] = summed / total
        log_ref[0, head : head + 1] = top + jnp.log(total)
    heads_ref[...] = jnp.transpose(turned_ref[0]).astype(low)


def attend(first, weight, bias, cosine, sine):
    length, width = first.shape
    pairs = weight.shape[1] // 384
    return pl.pallas_call(
        attend_kernel,
        grid=(pairs,),
        in_specs=[
            pl.BlockSpec((length, width), lambda i: (0, 0)),
            pl.BlockSpec((width, 384), lambda i: (0, i)),
            pl.BlockSpec((1, 384), lambda i: (0, i)),
            pl.BlockSpec((length, 128), lambda i: (0, 0)),
            pl.BlockSpec((length, 128), lambda i: (0, 0)),
        ],
        out_specs=[
            pl.BlockSpec((length, 384), lambda i: (0, i)),
            pl.BlockSpec((length, 128), lambda i: (0, i)),
            pl.BlockSpec((1, 128, length), lambda i: (i, 0, 0)),
            pl.BlockSpec((1, 2, length), lambda i: (i, 0, 0)),
        ],
        out_shape=[
            jax.ShapeDtypeStruct((length, 384 * pairs), jnp.bfloat16),
            jax.ShapeDtypeStruct((length, 128 * pairs), jnp.bfloat16),
            jax.ShapeDtypeStruct((pairs, 128, length), jnp.float32),
            jax.ShapeDtypeStruct((pairs, 2, length), jnp.float32),
        ],
        name="attend",
    )(first, weight, bias.reshape(1, -1), cosine, sine)


def attend_back_kernel(qkv_ref, grad_ref, turned_ref, log_ref, cos_ref, sin_ref, out_ref, bias_ref):
    low = jnp.bfloat16
    query = qkv_ref[:, :128]
    key = qkv_ref[:, 128:256]
    value = qkv_ref[:, 256:]
    grad = grad_ref[...]
    key_turned = jnp.transpose(key.astype(jnp.float32)).astype(low)
    product = jnp.transpose(grad.astype(jnp.float32)) * turned_ref[0]
    first_head = lax.broadcasted_iota(jnp.int32, key.shape, 1) < HD
    zero = jnp.zeros_like(key)
    query_grads, key_grads, value_grads = [], [], []
    for head in range(2):
        mine = slice(head * HD, (head + 1) * HD)
        here = first_head == (head == 0)
        delta = jnp.sum(product[mine], axis=0, keepdims=True)
        scores = contract(jnp.where(here, key, zero), query, 1, 1)
        probs = jnp.exp(scores - log_ref[0, head : head + 1])
        grad_probs = contract(jnp.where(here, value, zero), grad, 1, 1)
        grad_scores = (probs * (grad_probs - delta)).astype(low)
        value_grads.append(jnp.dot(probs.astype(low), grad, preferred_element_type=jnp.float32))
        key_grads.append(jnp.dot(grad_scores, query, preferred_element_type=jnp.float32))
        query_grads.append(jnp.dot(key_turned[mine], grad_scores, preferred_element_type=jnp.float32))
    cosine, sine = cos_ref[...], sin_ref[...]

    def rotate_back(values):
        return values * cosine + lane_swap(values * sine)

    parts = [
        rotate_back(jnp.transpose(jnp.concatenate(query_grads, axis=0)) * 0.125),
        rotate_back(jnp.where(first_head, key_grads[0], key_grads[1])),
        jnp.where(first_head, value_grads[0], value_grads[1]),
    ]
    for at, part in enumerate(parts):
        part = part.astype(low)
        out_ref[:, at * 128 : (at + 1) * 128] = part
        bias_ref[:, at * 128 : (at + 1) * 128] = jnp.sum(part.astype(jnp.float32), axis=0, keepdims=True)


def attend_back(qkv, grad, turned, logs, cosine, sine):
    length = qkv.shape[0]
    pairs = qkv.shape[1] // 384
    return pl.pallas_call(
        attend_back_kernel,
        grid=(pairs,),
        in_specs=[
            pl.BlockSpec((length, 384), lambda i: (0, i)),
            pl.BlockSpec((length, 128), lambda i: (0, i)),
            pl.BlockSpec((1, 128, length), lambda i: (i, 0, 0)),
            pl.BlockSpec((1, 2, length), lambda i: (i, 0, 0)),
            pl.BlockSpec((length, 128), lambda i: (0, 0)),
            pl.BlockSpec((length, 128), lambda i: (0, 0)),
        ],
        out_specs=[
            pl.BlockSpec((length, 384), lambda i: (0, i)),
            pl.BlockSpec((1, 384), lambda i: (0, i)),
        ],
        out_shape=[
            jax.ShapeDtypeStruct((length, 384 * pairs), jnp.bfloat16),
            jax.ShapeDtypeStruct((1, 384 * pairs), jnp.float32),
        ],
        name="attend_back",
    )(qkv, grad, turned, logs, cosine, sine)


def assemble_kernel(place_ref, own_ref, x_ref, y_ref, even_ref, odd_ref, *out_refs):
    rows = even_ref.shape[0]
    start = 0
    for out_ref in out_refs:
        cols = slice(start, start + out_ref.shape[1])
        start += out_ref.shape[1]
        for at, ref in enumerate((own_ref, x_ref, y_ref)):
            out_ref[pl.ds(pl.multiple_of((at ^ place_ref[0]) * 2 * rows, 2 * rows), 2 * rows)] = ref[:, cols]
        last = (3 ^ place_ref[0]) * 2 * rows
        out_ref[pl.ds(pl.multiple_of(last, rows), rows)] = even_ref[:, cols]
        out_ref[pl.ds(pl.multiple_of(last + rows, rows), rows)] = odd_ref[:, cols]


def assemble(place, pieces, widths):
    rows = pieces[3].shape[0]
    total = sum(widths)
    return pl.pallas_call(
        assemble_kernel,
        grid_spec=pltpu.PrefetchScalarGridSpec(
            num_scalar_prefetch=1,
            grid=(4,),
            in_specs=[pl.BlockSpec((item.shape[0], total), lambda i, place: (0, i)) for item in pieces],
            out_specs=[pl.BlockSpec((8 * rows, cols), lambda i, place: (0, i)) for cols in widths],
        ),
        out_shape=[jax.ShapeDtypeStruct((8 * rows, 4 * cols), jnp.bfloat16) for cols in widths],
        name="assemble",
    )(place, *pieces)


def deal_kernel(place_ref, *refs):
    in_refs, out_refs = refs[:-4], refs[-4:]
    rows = out_refs[0].shape[1]
    start = 0
    for ref in in_refs:
        cols = slice(start, start + ref.shape[1])
        start += ref.shape[1]
        for half, kept_ref, sent_ref, bit in ((0, out_refs[0], out_refs[1], 2), (1, out_refs[2], out_refs[3], 1)):
            for out_ref, from_bit in ((kept_ref, 0), (sent_ref, bit)):
                for at in range(2):
                    block = (at * (3 - bit) + from_bit) ^ place_ref[0]
                    first_row = pl.multiple_of((2 * block + half) * rows, rows)
                    out_ref[at, :, cols] = ref[pl.ds(first_row, rows)]


def deal(place, grads):
    rows = grads[0].shape[0] // 8
    widths = [item.shape[1] // 4 for item in grads]
    total = sum(widths)
    return pl.pallas_call(
        deal_kernel,
        grid_spec=pltpu.PrefetchScalarGridSpec(
            num_scalar_prefetch=1,
            grid=(4,),
            in_specs=[pl.BlockSpec((8 * rows, cols), lambda i, place: (0, i)) for cols in widths],
            out_specs=[pl.BlockSpec((2, rows, total), lambda i, place: (0, 0, i))] * 4,
        ),
        out_shape=[jax.ShapeDtypeStruct((2, rows, 4 * total), jnp.bfloat16)] * 4,
        name="deal",
    )(place, *grads)


def after(values, earlier):
    return lax.optimization_barrier((values, earlier))[0]


EVERY = ("y", "x", "core", "tensor")


def one_clip_per_chip(mesh):
    return mesh.shape["dp"] == 8 and mesh.shape["tensor"] == 4


def swap(values, axis, bit=1):
    return lax.ppermute(values, axis, [(i, i ^ bit) for i in range(4 if axis == "tensor" else 2)])


def clip_routes(back):
    routes = []
    for turn in range(2):
        pairs = []
        for column in range(4):
            for core in range(2):
                for place in range(4):
                    source = (2 * column + core) * 4 + place
                    target = (2 * column + place // 2) * 4 + 2 * core + (turn ^ (place % 2))
                    pairs.append((target, source) if back else (source, target))
        routes.append(pairs)
    return routes


def pick(flag, first, second):
    return jnp.where(flag, second, first)


def to_clips(values):
    odd = lax.axis_index("tensor") % 2 == 1
    arrived = []
    for turn, pairs in enumerate(clip_routes(False)):
        sent = pick(odd, values[turn], values[1 - turn])
        arrived.append(lax.ppermute(sent, EVERY, pairs))
    return jnp.concatenate(
        [pick(odd, arrived[0], arrived[1]), pick(odd, arrived[1], arrived[0])], axis=0
    )


def from_clips(values):
    odd = lax.axis_index("tensor") % 2 == 1
    rows = values.shape[0] // 2
    arrived = []
    for turn, pairs in enumerate(clip_routes(True)):
        sent = pick(odd, values[turn * rows : (turn + 1) * rows], values[(1 - turn) * rows : (2 - turn) * rows])
        arrived.append(lax.ppermute(sent, EVERY, pairs))
    return jnp.stack([pick(odd, arrived[0], arrived[1]), pick(odd, arrived[1], arrived[0])])


def three_parts(values):
    high = lax.reduce_precision(values, 8, 7)
    rest = values - high
    middle = lax.reduce_precision(rest, 8, 7)
    low = rest - middle
    return jnp.stack([high, middle, low]).astype(jnp.bfloat16)


def clip_body(
    activations,
    cotangent,
    attn_gain,
    attn_shift,
    qkv_weight,
    qkv_bias,
    out_weight,
    out_bias,
    mlp_gain,
    mlp_shift,
    fc1_weight,
    fc1_bias,
    fc2_weight,
    fc2_bias,
):
    core, at_x, at_y, at_z = (lax.axis_index(name) for name in ("core", "x", "y", "tensor"))
    place = (2 * at_y + at_x).astype(jnp.int32).reshape(1)
    width = activations.shape[2]
    length = activations.shape[1] * 4
    half_rows = length // 2
    own_rows = qkv_weight.shape[0]
    half_heads = qkv_weight.shape[1] // (6 * HD)
    qkv_cols = half_heads * 3 * HD
    out_cols = out_weight.shape[1] // 2
    unit_cols = fc1_weight.shape[1] // 2
    low = jnp.bfloat16

    def first_half(values):
        return lax.slice_in_dim(values, 0, values.shape[-1] // 2, axis=values.ndim - 1)

    def second_half(values):
        return lax.slice_in_dim(values, values.shape[-1] // 2, values.shape[-1], axis=values.ndim - 1)

    def own_half(values):
        return pick(core == 1, first_half(values), second_half(values))

    def other_half(values):
        return pick(core == 1, second_half(values), first_half(values))

    def by_kind(values):
        lead = values.shape[:-1]
        split = values.reshape(lead + (2, half_heads, 3, HD))
        return jnp.swapaxes(split, -3, -2).reshape(values.shape)

    def by_head(values):
        lead = values.shape[:-1]
        split = values.reshape(lead + (2, 3, half_heads, HD))
        return jnp.swapaxes(split, -3, -2).reshape(values.shape)

    columns = (by_kind(qkv_weight), out_weight, fc1_weight, fc2_weight)
    mine = jnp.concatenate([own_half(item) for item in columns], axis=1)
    theirs = swap(jnp.concatenate([other_half(item) for item in columns], axis=1), "core")
    held = jnp.concatenate([pick(core == 1, mine, theirs), pick(core == 1, theirs, mine)], axis=0)

    def along_z(own):
        one = swap(own, "tensor", 1)
        two = swap(own, "tensor", 2)
        return [own, one, two, swap(two, "tensor", 1)]

    def over_plane(blocks):
        own = jnp.concatenate(blocks, axis=1)
        from_x, from_y = swap(own, "x"), swap(own, "y")
        return own, from_x, from_y, swap(from_y[:own_rows], "x"), swap(from_x[own_rows:], "y")

    lines = jnp.concatenate([own_half(by_kind(qkv_bias)), own_half(fc1_bias)])
    lines = jnp.pad(three_parts(lines), ((0, 0), (0, 3 * qkv_cols - lines.shape[0]))).reshape(9, qkv_cols)
    blocks = along_z(jnp.concatenate([held[:, :qkv_cols], lines, jnp.zeros((7, qkv_cols), low)], axis=0))
    tokens = to_clips(activations).astype(jnp.float32)
    lines = jnp.stack([item[2 * own_rows : 2 * own_rows + 9] for item in blocks])
    lines = lines.astype(jnp.float32).reshape(4, 3, 3 * qkv_cols).sum(axis=1)
    bias_qkv = lines[:, :qkv_cols].reshape(-1)
    bias_up = lines[:, qkv_cols : qkv_cols + unit_cols].reshape(-1)
    pieces = over_plane([item[: 2 * own_rows] for item in blocks])
    (weight_qkv,) = assemble(place, pieces, [qkv_cols])

    blocks = along_z(after(held[:, qkv_cols : qkv_cols + out_cols + unit_cols], blocks[3]))
    blocks[0] = after(blocks[0], pieces[2])
    pieces = over_plane(blocks)
    weight_out, weight_up = assemble(place, pieces, [out_cols, unit_cols])

    blocks = along_z(after(held[:, qkv_cols + out_cols + unit_cols :], blocks[3]))
    blocks[0] = after(blocks[0], pieces[2])
    grad_own = to_clips(after(cotangent, blocks[3]))
    (weight_down,) = assemble(place, over_plane(blocks), [unit_cols])

    def both_halves(values):
        other = swap(values, "core")
        return jnp.concatenate([pick(core == 1, values, other), pick(core == 1, other, values)], axis=0)

    def part_sum(values):
        halves = values.reshape((2, half_rows) + values.shape[1:])
        sent = pick(core == 1, halves[1], halves[0]).astype(low)
        return pick(core == 1, halves[0], halves[1]) + swap(sent, "core").astype(jnp.float32)

    cosine, sine = (jnp.concatenate([item, item], axis=1) for item in rotary_tables(length))

    first_all = both_halves(norm_rows(tokens, attn_gain, attn_shift).astype(low))
    qkv, heads_out, turned, log_total = attend(first_all, weight_qkv, bias_qkv, cosine, sine)
    resid = tokens + part_sum(contract(heads_out, weight_out, 1, 1)) + out_bias
    second_all = both_halves(norm_rows(resid, mlp_gain, mlp_shift).astype(low))
    hidden = jnp.dot(second_all, weight_up, preferred_element_type=jnp.float32) + bias_up
    act = exact_gelu(hidden).astype(low)
    result = resid + part_sum(contract(act, weight_down, 1, 1)) + fc2_bias
    output = from_clips(result.astype(low))

    def to_core(total):
        kept = pick(core == 1, total[0], total[1])
        came = swap(pick(core == 1, total[1], total[0]), "core")
        return jnp.concatenate(
            [pick(core == 1, kept, came), pick(core == 1, came, kept)], axis=-1
        ).astype(jnp.float32)

    def over_plane_back(grads, waits):
        kept_even, sent_even, kept_odd, sent_odd = deal(place, [item.astype(low) for item in grads])
        even = kept_even + after(swap(sent_even, "y"), waits[0])
        odd = kept_odd + after(swap(sent_odd, "x"), waits[0])
        even = even[0] + after(swap(even[1], "x"), waits[1])
        odd = odd[0] + after(swap(odd[1], "y"), waits[1])
        return jnp.concatenate([even, odd])

    def along_z_back(total, wait):
        cols = total.shape[1] // 4
        own, one, two, three = (total[:, at * cols : (at + 1) * cols] for at in range(4))
        one = swap(one, "tensor", 1)
        two = swap(two + after(swap(three, "tensor", 1), wait), "tensor", 2)
        return to_core((own + one + two).reshape(2, own_rows, cols))

    grad_top = grad_own.astype(jnp.float32)
    grad_all = both_halves(grad_own)
    sum_fc2_bias = jnp.sum(grad_top, axis=0)
    grad_fc2 = contract(grad_all, act, 0, 0)
    grad_act = jnp.dot(grad_all, weight_down, preferred_element_type=jnp.float32)
    grad_hidden = jax.vjp(exact_gelu, hidden)[1](grad_act)[0].astype(low)
    sum_fc1_bias = jnp.sum(grad_hidden, axis=0, dtype=jnp.float32)
    grad_fc1 = contract(second_all, grad_hidden, 0, 0)
    grad_second_part = contract(grad_hidden, weight_up, 1, 1)
    grad_second = part_sum(grad_second_part)
    second_pull = jax.vjp(norm_rows, resid, mlp_gain, mlp_shift)[1]
    grad_resid_norm, sum_mlp_gain, sum_mlp_shift = second_pull(grad_second)
    grad_resid = grad_top + grad_resid_norm
    sum_out_bias = jnp.sum(grad_resid, axis=0)
    resid_all = both_halves(grad_resid.astype(low))
    grad_out = contract(resid_all, heads_out, 0, 0)
    grad_heads = jnp.dot(resid_all, weight_out, preferred_element_type=jnp.float32).astype(low)
    grad_packed, sum_qkv_bias = attend_back(qkv, grad_heads, turned, log_total, cosine, sine)
    grad_qkv = contract(first_all, grad_packed, 0, 0)
    grad_first_part = contract(grad_packed, weight_qkv, 1, 1)
    grad_first = part_sum(grad_first_part)
    first_pull = jax.vjp(norm_rows, tokens, attn_gain, attn_shift)[1]
    grad_input_norm, sum_attn_gain, sum_attn_shift = first_pull(grad_first)
    input_grad = from_clips((grad_resid + grad_input_norm).astype(low)).astype(jnp.float32)

    total = over_plane_back([grad_fc2], [grad_second_part, grad_packed])
    grad_fc2_weight = along_z_back(total, grad_first_part)
    total = over_plane_back([grad_out, grad_fc1], [grad_packed, grad_first_part])
    both_weights = along_z_back(total, grad_first)
    cuts = both_weights.shape[1] // 2
    both_weights = [both_weights[:, :cuts], both_weights[:, cuts:]]
    grad_out_weight = jnp.concatenate([item[:, :out_cols] for item in both_weights], axis=1)
    grad_fc1_weight = jnp.concatenate([item[:, out_cols:] for item in both_weights], axis=1)
    total = over_plane_back([grad_qkv], [grad_first_part, grad_first])
    grad_qkv_weight = by_head(along_z_back(total, grad_first))

    def by_core(values):
        none = jnp.zeros_like(values)
        return [pick(core == 1, values, none), pick(core == 1, none, values)]

    def by_owner(values, cols):
        first, second, third, fourth = (values.reshape(-1)[at * cols : (at + 1) * cols] for at in range(4))
        odd = at_z % 2 == 1
        first, second = pick(odd, first, second), pick(odd, second, first)
        third, fourth = pick(odd, third, fourth), pick(odd, fourth, third)
        lower, upper = jnp.concatenate([first, second]), jnp.concatenate([third, fourth])
        far = at_z // 2 == 1
        return jnp.concatenate([pick(far, lower, upper), pick(far, upper, lower)])

    sums = [sum_attn_gain, sum_attn_shift, sum_out_bias, sum_mlp_gain, sum_mlp_shift, sum_fc2_bias]
    sums = jnp.concatenate(sums + by_core(by_owner(sum_qkv_bias, qkv_cols)) + by_core(by_owner(sum_fc1_bias, unit_cols)))
    for axis, bit in (("core", 1), ("x", 1), ("y", 1), ("tensor", 1), ("tensor", 2)):
        sums = sums + swap(sums, axis, bit)
    vectors = sums[: 6 * width].reshape(6, width)
    qkv_sums = sums[6 * width : 6 * width + 8 * qkv_cols].reshape(2, 4, qkv_cols)
    unit_sums = sums[6 * width + 8 * qkv_cols :].reshape(2, 4, unit_cols)

    def own_place(values):
        return lax.dynamic_index_in_dim(values, at_z, 1, keepdims=False).reshape(-1)

    return (
        output,
        input_grad,
        vectors[0],
        vectors[1],
        grad_qkv_weight,
        by_head(own_place(qkv_sums)),
        grad_out_weight,
        vectors[2],
        vectors[3],
        vectors[4],
        grad_fc1_weight,
        own_place(unit_sums),
        grad_fc2_weight,
        vectors[5],
    )


def solution(mesh):
    if one_clip_per_chip(mesh):
        plan, rows = clip_body, ("y", "x", "core")
        mesh = jax.sharding.Mesh(mesh.devices.reshape(2, 2, 2, 4), EVERY)
    else:
        plan, rows = body, "dp"
    tokens, matrix, columns = P(rows, "tensor", None), P(rows, "tensor"), P("tensor")
    params = (P(), P(), matrix, columns, matrix, P(), P(), P(), matrix, columns, matrix, P())
    both = (tokens, tokens) + params
    return jax.shard_map(plan, mesh=mesh, in_specs=both, out_specs=both, check_vma=False)
```

```python
import math

import jax
import jax.numpy as jnp
from jax import lax
from jax.experimental import pallas as pl
from jax.experimental.pallas import tpu as pltpu
from jax.sharding import PartitionSpec as P

HD = 64
GRID = 16


def norm_rows(values, gain_vec, shift_vec):
    row_mean = jnp.mean(values, axis=-1, keepdims=True)
    centred = values - row_mean
    variance = jnp.mean(centred * centred, axis=-1, keepdims=True)
    return centred * lax.rsqrt(variance + 1e-06) * gain_vec + shift_vec


def rotary_tables(length):
    section = 2 * (HD // 3 // 2)
    half = section // 2
    position = jnp.arange(length)
    frame = (position // (GRID * GRID)).astype(jnp.float32)
    row_pos = (position // GRID % GRID).astype(jnp.float32)
    col_pos = (position % GRID).astype(jnp.float32)
    omega = 1.0 / 10000.0 ** (jnp.arange(half).astype(jnp.float32) / half)
    pieces = [
        jnp.repeat(coordinate[:, None] * omega[None, :], 2, axis=1)
        for coordinate in (frame, row_pos, col_pos)
    ]
    pieces.append(jnp.zeros((length, HD - 3 * section), jnp.float32))
    angles = jnp.concatenate(pieces, axis=1)
    parity = jnp.where(jnp.arange(HD) % 2 == 0, -1.0, 1.0).astype(jnp.float32)
    return (jnp.cos(angles), jnp.sin(angles) * parity)


def pair_swap(values):
    shape = values.shape
    paired = values.reshape(shape[:-1] + (shape[-1] // 2, 2))
    return paired[..., ::-1].reshape(shape)


def contract(left, right, left_dim, right_dim):
    return lax.dot_general(
        left, right, (((left_dim,), (right_dim,)), ((), ())), preferred_element_type=jnp.float32
    )


def exact_gelu(values):
    return jax.nn.gelu(values, approximate=False)


def body(
    activations,
    cotangent,
    attn_gain,
    attn_shift,
    qkv_weight,
    qkv_bias,
    out_weight,
    out_bias,
    mlp_gain,
    mlp_shift,
    fc1_weight,
    fc1_bias,
    fc2_weight,
    fc2_bias,
):
    tensor_size = lax.axis_size("tensor")
    tensor_rank = lax.axis_index("tensor")
    row_count = activations.shape[1]
    width = activations.shape[2]
    length = row_count * tensor_size
    block_rows = min(512, length)
    block_count = length // block_rows
    local_heads = qkv_weight.shape[1] // (3 * HD)
    packed_cols = qkv_weight.shape[1]
    unit_cols = fc1_weight.shape[1]
    factor = 1.0 / math.sqrt(HD)
    cosine, sine = rotary_tables(length)
    cosine = cosine[:, None, :]
    sine = sine[:, None, :]

    def rotate(values):
        return values * cosine + pair_swap(values) * sine

    def rotate_back(values):
        return values * cosine + pair_swap(values * sine)

    def fetch():
        gathered = (
            lax.all_gather(qkv_weight, "dp", axis=0, tiled=True),
            lax.all_gather(out_weight, "dp", axis=0, tiled=True),
            lax.all_gather(fc1_weight, "dp", axis=0, tiled=True),
            lax.all_gather(fc2_weight, "dp", axis=0, tiled=True),
        )
        return (gathered, gathered)

    def seq_gather(values):
        return lax.all_gather(values, "tensor", axis=0, tiled=True)

    def part_sum(values):
        return lax.psum_scatter(
            values.astype(jnp.bfloat16), "tensor", scatter_dimension=0, tiled=True
        ).astype(jnp.float32)

    def grad_gather(values):
        return lax.all_gather(values, "tensor", axis=0, tiled=True)

    def grad_sum(values):
        return lax.psum_scatter(
            values.astype(jnp.bfloat16), "tensor", scatter_dimension=0, tiled=True
        ).astype(jnp.float32)

    def forward(inputs, weights):
        (weight_qkv, weight_out, weight_up, weight_down), (
            whole_qkv,
            whole_out,
            whole_up,
            whole_down,
        ) = weights
        first_all = seq_gather(norm_rows(inputs, attn_gain, attn_shift).astype(jnp.bfloat16))
        packed = (
            jnp.dot(first_all, weight_qkv, preferred_element_type=jnp.float32) + qkv_bias
        ).reshape(length, local_heads, 3, HD)
        query = rotate(packed[:, :, 0]).astype(jnp.bfloat16)
        key_all = rotate(packed[:, :, 1]).astype(jnp.bfloat16)
        value_all = packed[:, :, 2].astype(jnp.bfloat16)
        outputs = []
        log_sums = []
        for block in range(block_count):
            query_block = query[block * block_rows : (block + 1) * block_rows]
            scores = (
                jnp.einsum("qhd,khd->hqk", query_block, key_all, preferred_element_type=jnp.float32)
                * factor
            )
            row_max = jnp.max(scores, axis=-1, keepdims=True)
            expo = jnp.exp(scores - row_max)
            row_total = jnp.sum(expo, axis=-1, keepdims=True)
            weights_low = (expo / row_total).astype(jnp.bfloat16)
            outputs.append(
                jnp.einsum(
                    "hqk,khd->qhd", weights_low, value_all, preferred_element_type=jnp.float32
                )
            )
            log_sums.append(row_max + jnp.log(row_total))
        heads_out = (
            jnp.concatenate(outputs, axis=0).reshape(length, local_heads * HD).astype(jnp.bfloat16)
        )
        log_total = jnp.concatenate(log_sums, axis=1)
        attended = part_sum(contract(heads_out, weight_out, 1, 1))
        resid = inputs + attended + out_bias
        second_all = seq_gather(norm_rows(resid, mlp_gain, mlp_shift).astype(jnp.bfloat16))
        hidden = jnp.dot(second_all, weight_up, preferred_element_type=jnp.float32) + fc1_bias
        act = exact_gelu(hidden).astype(jnp.bfloat16)
        branch = part_sum(contract(act, weight_down, 1, 1))
        result = resid + branch + fc2_bias
        kept = (
            first_all,
            query,
            key_all,
            value_all,
            log_total,
            heads_out,
            heads_out,
            resid,
            second_all,
            hidden,
            act,
        )
        return (result, kept)

    def backward(inputs, grad_low, kept, weights):
        (weight_qkv, weight_out, weight_up, weight_down), (
            whole_qkv,
            whole_out,
            whole_up,
            whole_down,
        ) = weights
        (
            first_all,
            query,
            key_all,
            value_all,
            log_total,
            heads_out,
            heads_rows,
            resid,
            second_all,
            hidden,
            act,
        ) = kept
        grad_top = grad_low.astype(jnp.float32)
        grad_fc2_bias = jnp.sum(grad_top, axis=0)
        grad_all = grad_gather(grad_low)
        grad_fc2_weight = contract(grad_all, act, 0, 0)
        grad_act = jnp.dot(grad_all, weight_down, preferred_element_type=jnp.float32)
        gelu_pull = jax.vjp(exact_gelu, hidden)[1]
        grad_hidden = gelu_pull(grad_act)[0].astype(jnp.bfloat16)
        grad_fc1_bias = jnp.sum(grad_hidden, axis=0, dtype=jnp.float32)
        grad_fc1_weight = contract(second_all, grad_hidden, 0, 0)
        grad_second = grad_sum(contract(grad_hidden, weight_up, 1, 1))
        second_pull = jax.vjp(norm_rows, resid, mlp_gain, mlp_shift)[1]
        grad_resid_norm, grad_mlp_gain, grad_mlp_shift = second_pull(grad_second)
        grad_resid = grad_top + grad_resid_norm
        grad_out_bias = jnp.sum(grad_resid, axis=0)
        resid_low = grad_resid.astype(jnp.bfloat16)
        resid_all = grad_gather(resid_low)
        grad_out_weight = contract(resid_all, heads_out, 0, 0)
        grad_heads = jnp.dot(resid_all, weight_out, preferred_element_type=jnp.float32).astype(
            jnp.bfloat16
        )
        grad_heads = grad_heads.reshape(length, local_heads, HD)
        grad_key = jnp.zeros((length, local_heads, HD), jnp.float32)
        grad_value = jnp.zeros((length, local_heads, HD), jnp.float32)
        query_grads = []
        for block in range(block_count):
            lower = block * block_rows
            upper = lower + block_rows
            query_block = query[lower:upper]
            grad_block = grad_heads[lower:upper]
            scores = (
                jnp.einsum("qhd,khd->hqk", query_block, key_all, preferred_element_type=jnp.float32)
                * factor
            )
            probs = jnp.exp(scores - log_total[:, lower:upper])
            grad_value = grad_value + jnp.einsum(
                "hqk,qhd->khd",
                probs.astype(jnp.bfloat16),
                grad_block,
                preferred_element_type=jnp.float32,
            )
            grad_probs = jnp.einsum(
                "qhd,khd->hqk", grad_block, value_all, preferred_element_type=jnp.float32
            )
            grad_scores = (
                probs * (grad_probs - jnp.sum(probs * grad_probs, axis=-1, keepdims=True))
            ).astype(jnp.bfloat16)
            query_grads.append(
                jnp.einsum("hqk,khd->qhd", grad_scores, key_all, preferred_element_type=jnp.float32)
                * factor
            )
            grad_key = (
                grad_key
                + jnp.einsum(
                    "hqk,qhd->khd", grad_scores, query_block, preferred_element_type=jnp.float32
                )
                * factor
            )
        grad_query = jnp.concatenate(query_grads, axis=0)
        grad_packed = jnp.stack(
            [rotate_back(grad_query), rotate_back(grad_key), grad_value], axis=2
        )
        grad_packed = grad_packed.reshape(length, packed_cols).astype(jnp.bfloat16)
        grad_qkv_bias = jnp.sum(grad_packed, axis=0, dtype=jnp.float32)
        grad_qkv_weight = contract(first_all, grad_packed, 0, 0)
        grad_first = grad_sum(contract(grad_packed, weight_qkv, 1, 1))
        first_pull = jax.vjp(norm_rows, inputs, attn_gain, attn_shift)[1]
        grad_input_norm, grad_attn_gain, grad_attn_shift = first_pull(grad_first)
        input_grad = grad_resid + grad_input_norm
        grads = (
            grad_attn_gain,
            grad_attn_shift,
            grad_qkv_weight,
            grad_qkv_bias,
            grad_out_weight,
            grad_out_bias,
            grad_mlp_gain,
            grad_mlp_shift,
            grad_fc1_weight,
            grad_fc1_bias,
            grad_fc2_weight,
            grad_fc2_bias,
        )
        return (input_grad, grads)

    def per_clip(totals, inputs_pair):
        clip_in, clip_grad = inputs_pair
        forward_weights = fetch()
        result, kept = forward(clip_in.astype(jnp.float32), forward_weights)
        backward_weights = fetch()
        input_grad, grads = backward(clip_in.astype(jnp.float32), clip_grad, kept, backward_weights)
        totals = tuple((left + right for left, right in zip(totals, grads)))
        return (totals, (result.astype(jnp.bfloat16), input_grad))

    out_cols = local_heads * HD
    start_totals = (
        jnp.zeros((width,), jnp.float32),
        jnp.zeros((width,), jnp.float32),
        jnp.zeros((width, packed_cols), jnp.float32),
        jnp.zeros((packed_cols,), jnp.float32),
        jnp.zeros((width, out_cols), jnp.float32),
        jnp.zeros((width,), jnp.float32),
        jnp.zeros((width,), jnp.float32),
        jnp.zeros((width,), jnp.float32),
        jnp.zeros((width, unit_cols), jnp.float32),
        jnp.zeros((unit_cols,), jnp.float32),
        jnp.zeros((width, unit_cols), jnp.float32),
        jnp.zeros((width,), jnp.float32),
    )
    totals, (output, input_grad) = lax.scan(per_clip, start_totals, (activations, cotangent))
    out_grad = totals[4]
    weight_sums = (
        lax.psum_scatter(
            totals[2].astype(jnp.bfloat16), "dp", scatter_dimension=0, tiled=True
        ).astype(jnp.float32),
        lax.psum_scatter(
            out_grad.astype(jnp.bfloat16), "dp", scatter_dimension=0, tiled=True
        ).astype(jnp.float32),
        lax.psum_scatter(
            totals[8].astype(jnp.bfloat16), "dp", scatter_dimension=0, tiled=True
        ).astype(jnp.float32),
        lax.psum_scatter(
            totals[10].astype(jnp.bfloat16), "dp", scatter_dimension=0, tiled=True
        ).astype(jnp.float32),
    )
    qkv_place = lax.dynamic_update_slice_in_dim(
        jnp.zeros((packed_cols * tensor_size,), jnp.float32),
        totals[3],
        tensor_rank * packed_cols,
        0,
    )
    unit_place = lax.dynamic_update_slice_in_dim(
        jnp.zeros((unit_cols * tensor_size,), jnp.float32), totals[9], tensor_rank * unit_cols, 0
    )
    summed = lax.psum(
        (totals[0], totals[1], qkv_place, totals[5], totals[6], totals[7], unit_place, totals[11]),
        ("dp", "tensor"),
    )
    grad_qkv_bias = lax.dynamic_slice_in_dim(summed[2], tensor_rank * packed_cols, packed_cols, 0)
    grad_fc1_bias = lax.dynamic_slice_in_dim(summed[6], tensor_rank * unit_cols, unit_cols, 0)
    return (
        output,
        input_grad,
        summed[0],
        summed[1],
        weight_sums[0],
        grad_qkv_bias,
        weight_sums[1],
        summed[3],
        summed[4],
        summed[5],
        weight_sums[2],
        grad_fc1_bias,
        weight_sums[3],
        summed[7],
    )


def lane_swap(values):
    even = lax.broadcasted_iota(jnp.int32, values.shape, 1) % 2 == 0
    return jnp.where(even, pltpu.roll(values, 127, 1), pltpu.roll(values, 1, 1))


def attend_kernel(first_ref, weight_ref, bias_ref, cos_ref, sin_ref, qkv_ref, heads_ref, turned_ref, log_ref):
    low = jnp.bfloat16
    packed = jnp.dot(first_ref[...], weight_ref[...], preferred_element_type=jnp.float32) + bias_ref[...]
    cosine, sine = cos_ref[...], sin_ref[...]

    def rotate(values):
        return values * cosine + lane_swap(values) * sine

    query = (rotate(packed[:, :128]).astype(low).astype(jnp.float32) * 0.125).astype(low)
    key = rotate(packed[:, 128:256]).astype(low)
    value = packed[:, 256:]
    qkv_ref[:, :128] = query
    qkv_ref[:, 128:256] = key
    qkv_ref[:, 256:] = value.astype(low)
    value = jnp.transpose(value).astype(low)
    first_head = lax.broadcasted_iota(jnp.int32, key.shape, 1) < HD
    for head in range(2):
        mine = slice(head * HD, (head + 1) * HD)
        key_here = jnp.where(first_head == (head == 0), key, jnp.zeros_like(key))
        scores = contract(key_here, query, 1, 1)
        top = jnp.max(scores, axis=0, keepdims=True)
        expo = jnp.exp(scores - top)
        total = jnp.sum(expo, axis=0, keepdims=True)
        summed = jnp.dot(value[mine], expo.astype(low), preferred_element_type=jnp.float32)
        turned_ref[0, mine] = summed / total
        log_ref[0, head : head + 1] = top + jnp.log(total)
    heads_ref[...] = jnp.transpose(turned_ref[0]).astype(low)


def attend(first, weight, bias, cosine, sine):
    length, width = first.shape
    pairs = weight.shape[1] // 384
    return pl.pallas_call(
        attend_kernel,
        grid=(pairs,),
        in_specs=[
            pl.BlockSpec((length, width), lambda i: (0, 0)),
            pl.BlockSpec((width, 384), lambda i: (0, i)),
            pl.BlockSpec((1, 384), lambda i: (0, i)),
            pl.BlockSpec((length, 128), lambda i: (0, 0)),
            pl.BlockSpec((length, 128), lambda i: (0, 0)),
        ],
        out_specs=[
            pl.BlockSpec((length, 384), lambda i: (0, i)),
            pl.BlockSpec((length, 128), lambda i: (0, i)),
            pl.BlockSpec((1, 128, length), lambda i: (i, 0, 0)),
            pl.BlockSpec((1, 2, length), lambda i: (i, 0, 0)),
        ],
        out_shape=[
            jax.ShapeDtypeStruct((length, 384 * pairs), jnp.bfloat16),
            jax.ShapeDtypeStruct((length, 128 * pairs), jnp.bfloat16),
            jax.ShapeDtypeStruct((pairs, 128, length), jnp.float32),
            jax.ShapeDtypeStruct((pairs, 2, length), jnp.float32),
        ],
        cost_estimate=pl.CostEstimate(flops=2 * 10**10, transcendentals=0, bytes_accessed=16 * 2**20),
        name="attend",
    )(first, weight, bias.reshape(1, -1), cosine, sine)


def attend_back_kernel(qkv_ref, grad_ref, turned_ref, log_ref, cos_ref, sin_ref, out_ref, bias_ref):
    low = jnp.bfloat16
    query = qkv_ref[:, :128]
    key = qkv_ref[:, 128:256]
    value = qkv_ref[:, 256:]
    grad = grad_ref[...]
    key_turned = jnp.transpose(key.astype(jnp.float32)).astype(low)
    product = jnp.transpose(grad.astype(jnp.float32)) * turned_ref[0]
    first_head = lax.broadcasted_iota(jnp.int32, key.shape, 1) < HD
    zero = jnp.zeros_like(key)
    query_grads, key_grads, value_grads = [], [], []
    for head in range(2):
        mine = slice(head * HD, (head + 1) * HD)
        here = first_head == (head == 0)
        delta = jnp.sum(product[mine], axis=0, keepdims=True)
        scores = contract(jnp.where(here, key, zero), query, 1, 1)
        probs = jnp.exp(scores - log_ref[0, head : head + 1])
        grad_probs = contract(jnp.where(here, value, zero), grad, 1, 1)
        grad_scores = (probs * (grad_probs - delta)).astype(low)
        value_grads.append(jnp.dot(probs.astype(low), grad, preferred_element_type=jnp.float32))
        key_grads.append(jnp.dot(grad_scores, query, preferred_element_type=jnp.float32))
        query_grads.append(jnp.dot(key_turned[mine], grad_scores, preferred_element_type=jnp.float32))
    cosine, sine = cos_ref[...], sin_ref[...]

    def rotate_back(values):
        return values * cosine + lane_swap(values * sine)

    parts = [
        rotate_back(jnp.transpose(jnp.concatenate(query_grads, axis=0)) * 0.125),
        rotate_back(jnp.where(first_head, key_grads[0], key_grads[1])),
        jnp.where(first_head, value_grads[0], value_grads[1]),
    ]
    for at, part in enumerate(parts):
        part = part.astype(low)
        out_ref[:, at * 128 : (at + 1) * 128] = part
        bias_ref[:, at * 128 : (at + 1) * 128] = jnp.sum(part.astype(jnp.float32), axis=0, keepdims=True)


def attend_back(qkv, grad, turned, logs, cosine, sine):
    length = qkv.shape[0]
    pairs = qkv.shape[1] // 384
    return pl.pallas_call(
        attend_back_kernel,
        grid=(pairs,),
        in_specs=[
            pl.BlockSpec((length, 384), lambda i: (0, i)),
            pl.BlockSpec((length, 128), lambda i: (0, i)),
            pl.BlockSpec((1, 128, length), lambda i: (i, 0, 0)),
            pl.BlockSpec((1, 2, length), lambda i: (i, 0, 0)),
            pl.BlockSpec((length, 128), lambda i: (0, 0)),
            pl.BlockSpec((length, 128), lambda i: (0, 0)),
        ],
        out_specs=[
            pl.BlockSpec((length, 384), lambda i: (0, i)),
            pl.BlockSpec((1, 384), lambda i: (0, i)),
        ],
        out_shape=[
            jax.ShapeDtypeStruct((length, 384 * pairs), jnp.bfloat16),
            jax.ShapeDtypeStruct((1, 384 * pairs), jnp.float32),
        ],
        cost_estimate=pl.CostEstimate(flops=27 * 10**9, transcendentals=0, bytes_accessed=16 * 2**20),
        name="attend_back",
    )(qkv, grad, turned, logs, cosine, sine)


def assemble_kernel(place_ref, own_ref, x_ref, y_ref, even_ref, odd_ref, *out_refs):
    rows = even_ref.shape[0]
    start = 0
    for out_ref in out_refs:
        cols = slice(start, start + out_ref.shape[1])
        start += out_ref.shape[1]
        for at, ref in enumerate((own_ref, x_ref, y_ref)):
            out_ref[pl.ds(pl.multiple_of((at ^ place_ref[0]) * 2 * rows, 2 * rows), 2 * rows)] = ref[:, cols]
        last = (3 ^ place_ref[0]) * 2 * rows
        out_ref[pl.ds(pl.multiple_of(last, rows), rows)] = even_ref[:, cols]
        out_ref[pl.ds(pl.multiple_of(last + rows, rows), rows)] = odd_ref[:, cols]


def assemble(place, pieces, widths):
    rows = pieces[3].shape[0]
    total = sum(widths)
    return pl.pallas_call(
        assemble_kernel,
        grid_spec=pltpu.PrefetchScalarGridSpec(
            num_scalar_prefetch=1,
            grid=(4,),
            in_specs=[pl.BlockSpec((item.shape[0], total), lambda i, place: (0, i)) for item in pieces],
            out_specs=[pl.BlockSpec((8 * rows, cols), lambda i, place: (0, i)) for cols in widths],
        ),
        out_shape=[jax.ShapeDtypeStruct((8 * rows, 4 * cols), jnp.bfloat16) for cols in widths],
        cost_estimate=pl.CostEstimate(flops=0, transcendentals=0, bytes_accessed=16 * 2**20),
        name="assemble",
    )(place, *pieces)


def deal_kernel(place_ref, *refs):
    in_refs, out_refs = refs[:-4], refs[-4:]
    rows = out_refs[0].shape[1]
    start = 0
    for ref in in_refs:
        cols = slice(start, start + ref.shape[1])
        start += ref.shape[1]
        for half, kept_ref, sent_ref, bit in ((0, out_refs[0], out_refs[1], 2), (1, out_refs[2], out_refs[3], 1)):
            for out_ref, from_bit in ((kept_ref, 0), (sent_ref, bit)):
                for at in range(2):
                    block = (at * (3 - bit) + from_bit) ^ place_ref[0]
                    first_row = pl.multiple_of((2 * block + half) * rows, rows)
                    out_ref[at, :, cols] = ref[pl.ds(first_row, rows)]


def deal(place, grads):
    rows = grads[0].shape[0] // 8
    widths = [item.shape[1] // 4 for item in grads]
    total = sum(widths)
    return pl.pallas_call(
        deal_kernel,
        grid_spec=pltpu.PrefetchScalarGridSpec(
            num_scalar_prefetch=1,
            grid=(4,),
            in_specs=[pl.BlockSpec((8 * rows, cols), lambda i, place: (0, i)) for cols in widths],
            out_specs=[pl.BlockSpec((2, rows, total), lambda i, place: (0, 0, i))] * 4,
        ),
        out_shape=[jax.ShapeDtypeStruct((2, rows, 4 * total), jnp.bfloat16)] * 4,
        cost_estimate=pl.CostEstimate(flops=0, transcendentals=0, bytes_accessed=16 * 2**20),
        name="deal",
    )(place, *grads)


def after(values, earlier):
    return lax.optimization_barrier((values, earlier))[0]


EVERY = ("y", "x", "core", "tensor")


def one_clip_per_chip(mesh):
    return mesh.shape["dp"] == 8 and mesh.shape["tensor"] == 4


def swap(values, axis, bit=1):
    return lax.ppermute(values, axis, [(i, i ^ bit) for i in range(4 if axis == "tensor" else 2)])


def clip_routes(back):
    routes = []
    for turn in range(2):
        pairs = []
        for column in range(4):
            for core in range(2):
                for place in range(4):
                    source = (2 * column + core) * 4 + place
                    target = (2 * column + place // 2) * 4 + 2 * core + (turn ^ (place % 2))
                    pairs.append((target, source) if back else (source, target))
        routes.append(pairs)
    return routes


def pick(flag, first, second):
    return jnp.where(flag, second, first)


def to_clips(values):
    odd = lax.axis_index("tensor") % 2 == 1
    arrived = []
    for turn, pairs in enumerate(clip_routes(False)):
        sent = pick(odd, values[turn], values[1 - turn])
        arrived.append(lax.ppermute(sent, EVERY, pairs))
    return jnp.concatenate(
        [pick(odd, arrived[0], arrived[1]), pick(odd, arrived[1], arrived[0])], axis=0
    )


def from_clips(values):
    odd = lax.axis_index("tensor") % 2 == 1
    rows = values.shape[0] // 2
    arrived = []
    for turn, pairs in enumerate(clip_routes(True)):
        sent = pick(odd, values[turn * rows : (turn + 1) * rows], values[(1 - turn) * rows : (2 - turn) * rows])
        arrived.append(lax.ppermute(sent, EVERY, pairs))
    return jnp.stack([pick(odd, arrived[0], arrived[1]), pick(odd, arrived[1], arrived[0])])


def three_parts(values):
    high = lax.reduce_precision(values, 8, 7)
    rest = values - high
    middle = lax.reduce_precision(rest, 8, 7)
    low = rest - middle
    return jnp.stack([high, middle, low]).astype(jnp.bfloat16)


def clip_body(
    activations,
    cotangent,
    attn_gain,
    attn_shift,
    qkv_weight,
    qkv_bias,
    out_weight,
    out_bias,
    mlp_gain,
    mlp_shift,
    fc1_weight,
    fc1_bias,
    fc2_weight,
    fc2_bias,
):
    core, at_x, at_y, at_z = (lax.axis_index(name) for name in ("core", "x", "y", "tensor"))
    place = (2 * at_y + at_x).astype(jnp.int32).reshape(1)
    width = activations.shape[2]
    length = activations.shape[1] * 4
    half_rows = length // 2
    own_rows = qkv_weight.shape[0]
    half_heads = qkv_weight.shape[1] // (6 * HD)
    qkv_cols = half_heads * 3 * HD
    out_cols = out_weight.shape[1] // 2
    unit_cols = fc1_weight.shape[1] // 2
    low = jnp.bfloat16

    def first_half(values):
        return lax.slice_in_dim(values, 0, values.shape[-1] // 2, axis=values.ndim - 1)

    def second_half(values):
        return lax.slice_in_dim(values, values.shape[-1] // 2, values.shape[-1], axis=values.ndim - 1)

    def own_half(values):
        return pick(core == 1, first_half(values), second_half(values))

    def other_half(values):
        return pick(core == 1, second_half(values), first_half(values))

    def by_kind(values):
        lead = values.shape[:-1]
        split = values.reshape(lead + (2, half_heads, 3, HD))
        return jnp.swapaxes(split, -3, -2).reshape(values.shape)

    def by_head(values):
        lead = values.shape[:-1]
        split = values.reshape(lead + (2, 3, half_heads, HD))
        return jnp.swapaxes(split, -3, -2).reshape(values.shape)

    columns = (by_kind(qkv_weight), out_weight, fc1_weight, fc2_weight)
    mine = jnp.concatenate([own_half(item) for item in columns], axis=1)
    theirs = swap(jnp.concatenate([other_half(item) for item in columns], axis=1), "core")
    held = jnp.concatenate([pick(core == 1, mine, theirs), pick(core == 1, theirs, mine)], axis=0)

    def along_z(own, wait=None):
        one = swap(own, "tensor", 1)
        two = swap(own, "tensor", 2)
        two = two if wait is None else after(two, wait)
        return [own, one, two, swap(two, "tensor", 1)]

    def over_plane(blocks, wait=None):
        own = jnp.concatenate(blocks, axis=1)
        from_x, from_y = swap(own, "x"), swap(own, "y")
        if wait is not None:
            from_x, from_y = after((from_x, from_y), wait)
        return own, from_x, from_y, swap(from_y[:own_rows], "x"), swap(from_x[own_rows:], "y")

    lines = jnp.concatenate([own_half(by_kind(qkv_bias)), own_half(fc1_bias)])
    lines = jnp.pad(three_parts(lines), ((0, 0), (0, 3 * qkv_cols - lines.shape[0]))).reshape(9, qkv_cols)
    blocks = along_z(jnp.concatenate([held[:, :qkv_cols], lines, jnp.zeros((7, qkv_cols), low)], axis=0))
    tokens = to_clips(after(activations, blocks[2])).astype(jnp.float32)
    lines = jnp.stack([item[2 * own_rows : 2 * own_rows + 9] for item in blocks])
    lines = lines.astype(jnp.float32).reshape(4, 3, 3 * qkv_cols).sum(axis=1)
    bias_qkv = lines[:, :qkv_cols].reshape(-1)
    bias_up = lines[:, qkv_cols : qkv_cols + unit_cols].reshape(-1)
    pieces = over_plane([item[: 2 * own_rows] for item in blocks])
    (weight_qkv,) = assemble(place, pieces, [qkv_cols])

    def both_halves(values):
        other = swap(values, "core")
        return jnp.concatenate([pick(core == 1, values, other), pick(core == 1, other, values)], axis=0)

    def part_sum(values):
        halves = values.reshape((2, half_rows) + values.shape[1:])
        sent = pick(core == 1, halves[1], halves[0]).astype(low)
        return pick(core == 1, halves[0], halves[1]) + swap(sent, "core").astype(jnp.float32)

    cosine, sine = (jnp.concatenate([item, item], axis=1) for item in rotary_tables(length))

    first_all = both_halves(norm_rows(tokens, attn_gain, attn_shift).astype(low))
    qkv, heads_out, turned, log_total = attend(first_all, weight_qkv, bias_qkv, cosine, sine)

    own = after(held[:, qkv_cols : qkv_cols + out_cols + unit_cols], (blocks[3], tokens))
    blocks = along_z(own, pieces[1:3])
    blocks[0] = after(blocks[0], pieces[3:])
    pieces = over_plane(blocks, heads_out)
    weight_out, weight_up = assemble(place, pieces, [out_cols, unit_cols])
    resid = tokens + part_sum(contract(heads_out, weight_out, 1, 1)) + out_bias
    second_all = both_halves(norm_rows(resid, mlp_gain, mlp_shift).astype(low))

    own = after(held[:, qkv_cols + out_cols + unit_cols :], blocks[3])
    blocks = along_z(own, heads_out)
    blocks[0] = after(blocks[0], pieces[3:])
    pieces = over_plane(blocks, second_all)
    grad_own = to_clips(after(cotangent, blocks[3]))

    hidden = jnp.dot(after(second_all, pieces[1:3]), weight_up, preferred_element_type=jnp.float32) + bias_up
    act = exact_gelu(hidden).astype(low)
    pieces = pieces[:3] + after(pieces[3:], act)
    (weight_down,) = assemble(place, pieces, [unit_cols])
    result = resid + part_sum(contract(act, weight_down, 1, 1)) + fc2_bias
    output = from_clips(result.astype(low))

    def to_core(total):
        kept = pick(core == 1, total[0], total[1])
        came = swap(pick(core == 1, total[1], total[0]), "core")
        return jnp.concatenate(
            [pick(core == 1, kept, came), pick(core == 1, came, kept)], axis=-1
        ).astype(jnp.float32)

    def dealt(*grads):
        return deal(place, [item.astype(low) for item in grads])

    def first_back(parts, wait):
        kept_even, sent_even, kept_odd, sent_odd = parts
        came = after((swap(sent_even, "y"), swap(sent_odd, "x")), wait)
        return kept_even + came[0], kept_odd + came[1]

    def second_back(even, odd, wait):
        came = after((swap(even[1], "x"), swap(odd[1], "y")), wait)
        return jnp.concatenate([even[0] + came[0], odd[0] + came[1]])

    def along_z_back(total, wait, later):
        cols = total.shape[1] // 4
        own, one, two, three = (total[:, at * cols : (at + 1) * cols] for at in range(4))
        one = swap(one, "tensor", 1)
        two = swap(two + after(swap(three, "tensor", 1), wait), "tensor", 2)
        one, two = after((one, two), later)
        return to_core((own + one + two).reshape(2, own_rows, cols))

    grad_top = grad_own.astype(jnp.float32)
    grad_all = both_halves(grad_own)
    sum_fc2_bias = jnp.sum(grad_top, axis=0)
    parts_fc2 = dealt(contract(grad_all, act, 0, 0))
    grad_act = jnp.dot(after(grad_all, parts_fc2), weight_down, preferred_element_type=jnp.float32)
    grad_hidden = jax.vjp(exact_gelu, hidden)[1](grad_act)[0].astype(low)
    sum_fc1_bias = jnp.sum(grad_hidden, axis=0, dtype=jnp.float32)
    grad_second_part = contract(grad_hidden, weight_up, 1, 1)
    sent_fc2 = first_back(parts_fc2, grad_second_part)
    grad_second = part_sum(grad_second_part)
    second_pull = jax.vjp(norm_rows, resid, mlp_gain, mlp_shift)[1]
    grad_resid_norm, sum_mlp_gain, sum_mlp_shift = second_pull(grad_second)
    grad_resid = grad_top + grad_resid_norm
    sum_out_bias = jnp.sum(grad_resid, axis=0)
    resid_all = both_halves(grad_resid.astype(low))
    grad_fc1 = contract(after(second_all, sent_fc2[0]), grad_hidden, 0, 0)
    parts_up = dealt(contract(resid_all, heads_out, 0, 0), grad_fc1)
    grad_heads = jnp.dot(resid_all, weight_out, preferred_element_type=jnp.float32).astype(low)
    total_fc2 = second_back(*sent_fc2, grad_heads)
    grad_packed, sum_qkv_bias = attend_back(qkv, after(grad_heads, (parts_up, total_fc2)), turned, log_total, cosine, sine)
    sent_up = first_back(parts_up, grad_packed)
    parts_qkv = dealt(contract(after(first_all, sent_up), grad_packed, 0, 0))
    total_up = second_back(*sent_up, parts_qkv)
    grad_first_part = contract(after(grad_packed, parts_qkv), weight_qkv, 1, 1)
    grad_first = part_sum(after(grad_first_part, total_up))
    first_pull = jax.vjp(norm_rows, tokens, attn_gain, attn_shift)[1]
    grad_input_norm, sum_attn_gain, sum_attn_shift = first_pull(grad_first)
    input_grad = from_clips((grad_resid + grad_input_norm).astype(low)).astype(jnp.float32)

    grad_fc2_weight = along_z_back(total_fc2, grad_packed, parts_qkv)
    both_weights = along_z_back(total_up, grad_first_part, grad_first)
    cuts = both_weights.shape[1] // 2
    both_weights = [both_weights[:, :cuts], both_weights[:, cuts:]]
    grad_out_weight = jnp.concatenate([item[:, :out_cols] for item in both_weights], axis=1)
    grad_fc1_weight = jnp.concatenate([item[:, out_cols:] for item in both_weights], axis=1)
    total = second_back(*first_back(parts_qkv, grad_first_part), grad_first)
    grad_qkv_weight = by_head(along_z_back(total, grad_first, grad_first))

    def by_core(values):
        none = jnp.zeros_like(values)
        return [pick(core == 1, values, none), pick(core == 1, none, values)]

    def by_owner(values, cols):
        first, second, third, fourth = (values.reshape(-1)[at * cols : (at + 1) * cols] for at in range(4))
        odd = at_z % 2 == 1
        first, second = pick(odd, first, second), pick(odd, second, first)
        third, fourth = pick(odd, third, fourth), pick(odd, fourth, third)
        lower, upper = jnp.concatenate([first, second]), jnp.concatenate([third, fourth])
        far = at_z // 2 == 1
        return jnp.concatenate([pick(far, lower, upper), pick(far, upper, lower)])

    sums = [sum_attn_gain, sum_attn_shift, sum_out_bias, sum_mlp_gain, sum_mlp_shift, sum_fc2_bias]
    sums = jnp.concatenate(sums + by_core(by_owner(sum_qkv_bias, qkv_cols)) + by_core(by_owner(sum_fc1_bias, unit_cols)))
    for axis, bit in (("core", 1), ("x", 1), ("y", 1), ("tensor", 1), ("tensor", 2)):
        sums = sums + swap(sums, axis, bit)
    vectors = sums[: 6 * width].reshape(6, width)
    qkv_sums = sums[6 * width : 6 * width + 8 * qkv_cols].reshape(2, 4, qkv_cols)
    unit_sums = sums[6 * width + 8 * qkv_cols :].reshape(2, 4, unit_cols)

    def own_place(values):
        return lax.dynamic_index_in_dim(values, at_z, 1, keepdims=False).reshape(-1)

    return (
        output,
        input_grad,
        vectors[0],
        vectors[1],
        grad_qkv_weight,
        by_head(own_place(qkv_sums)),
        grad_out_weight,
        vectors[2],
        vectors[3],
        vectors[4],
        grad_fc1_weight,
        own_place(unit_sums),
        grad_fc2_weight,
        vectors[5],
    )


def solution(mesh):
    if one_clip_per_chip(mesh):
        plan, rows = clip_body, ("y", "x", "core")
        mesh = jax.sharding.Mesh(mesh.devices.reshape(2, 2, 2, 4), EVERY)
    else:
        plan, rows = body, "dp"
    tokens, matrix, columns = P(rows, "tensor", None), P(rows, "tensor"), P("tensor")
    params = (P(), P(), matrix, columns, matrix, P(), P(), P(), matrix, columns, matrix, P())
    both = (tokens, tokens) + params
    return jax.shard_map(plan, mesh=mesh, in_specs=both, out_specs=both, check_vma=False)
```

```python
import math

import jax
import jax.numpy as jnp
from jax import lax
from jax.experimental import pallas as pl
from jax.experimental.pallas import tpu as pltpu
from jax.sharding import PartitionSpec as P

HD = 64
GRID = 16


def norm_rows(values, gain_vec, shift_vec):
    row_mean = jnp.mean(values, axis=-1, keepdims=True)
    centred = values - row_mean
    variance = jnp.mean(centred * centred, axis=-1, keepdims=True)
    return centred * lax.rsqrt(variance + 1e-06) * gain_vec + shift_vec


def rotary_tables(length):
    section = 2 * (HD // 3 // 2)
    half = section // 2
    position = jnp.arange(length)
    frame = (position // (GRID * GRID)).astype(jnp.float32)
    row_pos = (position // GRID % GRID).astype(jnp.float32)
    col_pos = (position % GRID).astype(jnp.float32)
    omega = 1.0 / 10000.0 ** (jnp.arange(half).astype(jnp.float32) / half)
    pieces = [
        jnp.repeat(coordinate[:, None] * omega[None, :], 2, axis=1)
        for coordinate in (frame, row_pos, col_pos)
    ]
    pieces.append(jnp.zeros((length, HD - 3 * section), jnp.float32))
    angles = jnp.concatenate(pieces, axis=1)
    parity = jnp.where(jnp.arange(HD) % 2 == 0, -1.0, 1.0).astype(jnp.float32)
    return (jnp.cos(angles), jnp.sin(angles) * parity)


def pair_swap(values):
    shape = values.shape
    paired = values.reshape(shape[:-1] + (shape[-1] // 2, 2))
    return paired[..., ::-1].reshape(shape)


def contract(left, right, left_dim, right_dim):
    return lax.dot_general(
        left, right, (((left_dim,), (right_dim,)), ((), ())), preferred_element_type=jnp.float32
    )


def exact_gelu(values):
    return jax.nn.gelu(values, approximate=False)


def body(
    activations,
    cotangent,
    attn_gain,
    attn_shift,
    qkv_weight,
    qkv_bias,
    out_weight,
    out_bias,
    mlp_gain,
    mlp_shift,
    fc1_weight,
    fc1_bias,
    fc2_weight,
    fc2_bias,
):
    tensor_size = lax.axis_size("tensor")
    tensor_rank = lax.axis_index("tensor")
    row_count = activations.shape[1]
    width = activations.shape[2]
    length = row_count * tensor_size
    block_rows = min(512, length)
    block_count = length // block_rows
    local_heads = qkv_weight.shape[1] // (3 * HD)
    packed_cols = qkv_weight.shape[1]
    unit_cols = fc1_weight.shape[1]
    factor = 1.0 / math.sqrt(HD)
    cosine, sine = rotary_tables(length)
    cosine = cosine[:, None, :]
    sine = sine[:, None, :]

    def rotate(values):
        return values * cosine + pair_swap(values) * sine

    def rotate_back(values):
        return values * cosine + pair_swap(values * sine)

    def fetch():
        gathered = (
            lax.all_gather(qkv_weight, "dp", axis=0, tiled=True),
            lax.all_gather(out_weight, "dp", axis=0, tiled=True),
            lax.all_gather(fc1_weight, "dp", axis=0, tiled=True),
            lax.all_gather(fc2_weight, "dp", axis=0, tiled=True),
        )
        return (gathered, gathered)

    def seq_gather(values):
        return lax.all_gather(values, "tensor", axis=0, tiled=True)

    def part_sum(values):
        return lax.psum_scatter(
            values.astype(jnp.bfloat16), "tensor", scatter_dimension=0, tiled=True
        ).astype(jnp.float32)

    def grad_gather(values):
        return lax.all_gather(values, "tensor", axis=0, tiled=True)

    def grad_sum(values):
        return lax.psum_scatter(
            values.astype(jnp.bfloat16), "tensor", scatter_dimension=0, tiled=True
        ).astype(jnp.float32)

    def forward(inputs, weights):
        (weight_qkv, weight_out, weight_up, weight_down), (
            whole_qkv,
            whole_out,
            whole_up,
            whole_down,
        ) = weights
        first_all = seq_gather(norm_rows(inputs, attn_gain, attn_shift).astype(jnp.bfloat16))
        packed = (
            jnp.dot(first_all, weight_qkv, preferred_element_type=jnp.float32) + qkv_bias
        ).reshape(length, local_heads, 3, HD)
        query = rotate(packed[:, :, 0]).astype(jnp.bfloat16)
        key_all = rotate(packed[:, :, 1]).astype(jnp.bfloat16)
        value_all = packed[:, :, 2].astype(jnp.bfloat16)
        outputs = []
        log_sums = []
        for block in range(block_count):
            query_block = query[block * block_rows : (block + 1) * block_rows]
            scores = (
                jnp.einsum("qhd,khd->hqk", query_block, key_all, preferred_element_type=jnp.float32)
                * factor
            )
            row_max = jnp.max(scores, axis=-1, keepdims=True)
            expo = jnp.exp(scores - row_max)
            row_total = jnp.sum(expo, axis=-1, keepdims=True)
            weights_low = (expo / row_total).astype(jnp.bfloat16)
            outputs.append(
                jnp.einsum(
                    "hqk,khd->qhd", weights_low, value_all, preferred_element_type=jnp.float32
                )
            )
            log_sums.append(row_max + jnp.log(row_total))
        heads_out = (
            jnp.concatenate(outputs, axis=0).reshape(length, local_heads * HD).astype(jnp.bfloat16)
        )
        log_total = jnp.concatenate(log_sums, axis=1)
        attended = part_sum(contract(heads_out, weight_out, 1, 1))
        resid = inputs + attended + out_bias
        second_all = seq_gather(norm_rows(resid, mlp_gain, mlp_shift).astype(jnp.bfloat16))
        hidden = jnp.dot(second_all, weight_up, preferred_element_type=jnp.float32) + fc1_bias
        act = exact_gelu(hidden).astype(jnp.bfloat16)
        branch = part_sum(contract(act, weight_down, 1, 1))
        result = resid + branch + fc2_bias
        kept = (
            first_all,
            query,
            key_all,
            value_all,
            log_total,
            heads_out,
            heads_out,
            resid,
            second_all,
            hidden,
            act,
        )
        return (result, kept)

    def backward(inputs, grad_low, kept, weights):
        (weight_qkv, weight_out, weight_up, weight_down), (
            whole_qkv,
            whole_out,
            whole_up,
            whole_down,
        ) = weights
        (
            first_all,
            query,
            key_all,
            value_all,
            log_total,
            heads_out,
            heads_rows,
            resid,
            second_all,
            hidden,
            act,
        ) = kept
        grad_top = grad_low.astype(jnp.float32)
        grad_fc2_bias = jnp.sum(grad_top, axis=0)
        grad_all = grad_gather(grad_low)
        grad_fc2_weight = contract(grad_all, act, 0, 0)
        grad_act = jnp.dot(grad_all, weight_down, preferred_element_type=jnp.float32)
        gelu_pull = jax.vjp(exact_gelu, hidden)[1]
        grad_hidden = gelu_pull(grad_act)[0].astype(jnp.bfloat16)
        grad_fc1_bias = jnp.sum(grad_hidden, axis=0, dtype=jnp.float32)
        grad_fc1_weight = contract(second_all, grad_hidden, 0, 0)
        grad_second = grad_sum(contract(grad_hidden, weight_up, 1, 1))
        second_pull = jax.vjp(norm_rows, resid, mlp_gain, mlp_shift)[1]
        grad_resid_norm, grad_mlp_gain, grad_mlp_shift = second_pull(grad_second)
        grad_resid = grad_top + grad_resid_norm
        grad_out_bias = jnp.sum(grad_resid, axis=0)
        resid_low = grad_resid.astype(jnp.bfloat16)
        resid_all = grad_gather(resid_low)
        grad_out_weight = contract(resid_all, heads_out, 0, 0)
        grad_heads = jnp.dot(resid_all, weight_out, preferred_element_type=jnp.float32).astype(
            jnp.bfloat16
        )
        grad_heads = grad_heads.reshape(length, local_heads, HD)
        grad_key = jnp.zeros((length, local_heads, HD), jnp.float32)
        grad_value = jnp.zeros((length, local_heads, HD), jnp.float32)
        query_grads = []
        for block in range(block_count):
            lower = block * block_rows
            upper = lower + block_rows
            query_block = query[lower:upper]
            grad_block = grad_heads[lower:upper]
            scores = (
                jnp.einsum("qhd,khd->hqk", query_block, key_all, preferred_element_type=jnp.float32)
                * factor
            )
            probs = jnp.exp(scores - log_total[:, lower:upper])
            grad_value = grad_value + jnp.einsum(
                "hqk,qhd->khd",
                probs.astype(jnp.bfloat16),
                grad_block,
                preferred_element_type=jnp.float32,
            )
            grad_probs = jnp.einsum(
                "qhd,khd->hqk", grad_block, value_all, preferred_element_type=jnp.float32
            )
            grad_scores = (
                probs * (grad_probs - jnp.sum(probs * grad_probs, axis=-1, keepdims=True))
            ).astype(jnp.bfloat16)
            query_grads.append(
                jnp.einsum("hqk,khd->qhd", grad_scores, key_all, preferred_element_type=jnp.float32)
                * factor
            )
            grad_key = (
                grad_key
                + jnp.einsum(
                    "hqk,qhd->khd", grad_scores, query_block, preferred_element_type=jnp.float32
                )
                * factor
            )
        grad_query = jnp.concatenate(query_grads, axis=0)
        grad_packed = jnp.stack(
            [rotate_back(grad_query), rotate_back(grad_key), grad_value], axis=2
        )
        grad_packed = grad_packed.reshape(length, packed_cols).astype(jnp.bfloat16)
        grad_qkv_bias = jnp.sum(grad_packed, axis=0, dtype=jnp.float32)
        grad_qkv_weight = contract(first_all, grad_packed, 0, 0)
        grad_first = grad_sum(contract(grad_packed, weight_qkv, 1, 1))
        first_pull = jax.vjp(norm_rows, inputs, attn_gain, attn_shift)[1]
        grad_input_norm, grad_attn_gain, grad_attn_shift = first_pull(grad_first)
        input_grad = grad_resid + grad_input_norm
        grads = (
            grad_attn_gain,
            grad_attn_shift,
            grad_qkv_weight,
            grad_qkv_bias,
            grad_out_weight,
            grad_out_bias,
            grad_mlp_gain,
            grad_mlp_shift,
            grad_fc1_weight,
            grad_fc1_bias,
            grad_fc2_weight,
            grad_fc2_bias,
        )
        return (input_grad, grads)

    def per_clip(totals, inputs_pair):
        clip_in, clip_grad = inputs_pair
        forward_weights = fetch()
        result, kept = forward(clip_in.astype(jnp.float32), forward_weights)
        backward_weights = fetch()
        input_grad, grads = backward(clip_in.astype(jnp.float32), clip_grad, kept, backward_weights)
        totals = tuple((left + right for left, right in zip(totals, grads)))
        return (totals, (result.astype(jnp.bfloat16), input_grad))

    out_cols = local_heads * HD
    start_totals = (
        jnp.zeros((width,), jnp.float32),
        jnp.zeros((width,), jnp.float32),
        jnp.zeros((width, packed_cols), jnp.float32),
        jnp.zeros((packed_cols,), jnp.float32),
        jnp.zeros((width, out_cols), jnp.float32),
        jnp.zeros((width,), jnp.float32),
        jnp.zeros((width,), jnp.float32),
        jnp.zeros((width,), jnp.float32),
        jnp.zeros((width, unit_cols), jnp.float32),
        jnp.zeros((unit_cols,), jnp.float32),
        jnp.zeros((width, unit_cols), jnp.float32),
        jnp.zeros((width,), jnp.float32),
    )
    totals, (output, input_grad) = lax.scan(per_clip, start_totals, (activations, cotangent))
    out_grad = totals[4]
    weight_sums = (
        lax.psum_scatter(
            totals[2].astype(jnp.bfloat16), "dp", scatter_dimension=0, tiled=True
        ).astype(jnp.float32),
        lax.psum_scatter(
            out_grad.astype(jnp.bfloat16), "dp", scatter_dimension=0, tiled=True
        ).astype(jnp.float32),
        lax.psum_scatter(
            totals[8].astype(jnp.bfloat16), "dp", scatter_dimension=0, tiled=True
        ).astype(jnp.float32),
        lax.psum_scatter(
            totals[10].astype(jnp.bfloat16), "dp", scatter_dimension=0, tiled=True
        ).astype(jnp.float32),
    )
    qkv_place = lax.dynamic_update_slice_in_dim(
        jnp.zeros((packed_cols * tensor_size,), jnp.float32),
        totals[3],
        tensor_rank * packed_cols,
        0,
    )
    unit_place = lax.dynamic_update_slice_in_dim(
        jnp.zeros((unit_cols * tensor_size,), jnp.float32), totals[9], tensor_rank * unit_cols, 0
    )
    summed = lax.psum(
        (totals[0], totals[1], qkv_place, totals[5], totals[6], totals[7], unit_place, totals[11]),
        ("dp", "tensor"),
    )
    grad_qkv_bias = lax.dynamic_slice_in_dim(summed[2], tensor_rank * packed_cols, packed_cols, 0)
    grad_fc1_bias = lax.dynamic_slice_in_dim(summed[6], tensor_rank * unit_cols, unit_cols, 0)
    return (
        output,
        input_grad,
        summed[0],
        summed[1],
        weight_sums[0],
        grad_qkv_bias,
        weight_sums[1],
        summed[3],
        summed[4],
        summed[5],
        weight_sums[2],
        grad_fc1_bias,
        weight_sums[3],
        summed[7],
    )


def lane_swap(values):
    even = lax.broadcasted_iota(jnp.int32, values.shape, 1) % 2 == 0
    return jnp.where(even, pltpu.roll(values, 127, 1), pltpu.roll(values, 1, 1))


def attend_kernel(first_ref, weight_ref, bias_ref, cos_ref, sin_ref, qkv_ref, heads_ref, turned_ref, log_ref):
    low = jnp.bfloat16
    packed = jnp.dot(first_ref[...], weight_ref[...], preferred_element_type=jnp.float32) + bias_ref[...]
    cosine, sine = cos_ref[...], sin_ref[...]

    def rotate(values):
        return values * cosine + lane_swap(values) * sine

    query = (rotate(packed[:, :128]).astype(low).astype(jnp.float32) * 0.125).astype(low)
    key = rotate(packed[:, 128:256]).astype(low)
    value = packed[:, 256:]
    qkv_ref[:, :128] = query
    qkv_ref[:, 128:256] = key
    qkv_ref[:, 256:] = value.astype(low)
    value = jnp.transpose(value).astype(low)
    first_head = lax.broadcasted_iota(jnp.int32, key.shape, 1) < HD
    for head in range(2):
        mine = slice(head * HD, (head + 1) * HD)
        key_here = jnp.where(first_head == (head == 0), key, jnp.zeros_like(key))
        scores = contract(key_here, query, 1, 1)
        top = jnp.max(scores, axis=0, keepdims=True)
        expo = jnp.exp(scores - top)
        total = jnp.sum(expo, axis=0, keepdims=True)
        summed = jnp.dot(value[mine], expo.astype(low), preferred_element_type=jnp.float32)
        turned_ref[0, mine] = summed / total
        log_ref[0, head : head + 1] = top + jnp.log(total)
    heads_ref[...] = jnp.transpose(turned_ref[0]).astype(low)


def attend(first, weight, bias, cosine, sine):
    length, width = first.shape
    pairs = weight.shape[1] // 384
    return pl.pallas_call(
        attend_kernel,
        grid=(pairs,),
        in_specs=[
            pl.BlockSpec((length, width), lambda i: (0, 0)),
            pl.BlockSpec((width, 384), lambda i: (0, i)),
            pl.BlockSpec((1, 384), lambda i: (0, i)),
            pl.BlockSpec((length, 128), lambda i: (0, 0)),
            pl.BlockSpec((length, 128), lambda i: (0, 0)),
        ],
        out_specs=[
            pl.BlockSpec((length, 384), lambda i: (0, i)),
            pl.BlockSpec((length, 128), lambda i: (0, i)),
            pl.BlockSpec((1, 128, length), lambda i: (i, 0, 0)),
            pl.BlockSpec((1, 2, length), lambda i: (i, 0, 0)),
        ],
        out_shape=[
            jax.ShapeDtypeStruct((length, 384 * pairs), jnp.bfloat16),
            jax.ShapeDtypeStruct((length, 128 * pairs), jnp.bfloat16),
            jax.ShapeDtypeStruct((pairs, 128, length), jnp.float32),
            jax.ShapeDtypeStruct((pairs, 2, length), jnp.float32),
        ],
        cost_estimate=pl.CostEstimate(flops=2 * 10**10, transcendentals=0, bytes_accessed=16 * 2**20),
        name="attend",
    )(first, weight, bias.reshape(1, -1), cosine, sine)


def attend_back_kernel(qkv_ref, grad_ref, turned_ref, log_ref, cos_ref, sin_ref, out_ref, bias_ref):
    low = jnp.bfloat16
    query = qkv_ref[:, :128]
    key = qkv_ref[:, 128:256]
    value = qkv_ref[:, 256:]
    grad = grad_ref[...]
    key_turned = jnp.transpose(key.astype(jnp.float32)).astype(low)
    product = jnp.transpose(grad.astype(jnp.float32)) * turned_ref[0]
    first_head = lax.broadcasted_iota(jnp.int32, key.shape, 1) < HD
    zero = jnp.zeros_like(key)
    query_grads, key_grads, value_grads = [], [], []
    for head in range(2):
        mine = slice(head * HD, (head + 1) * HD)
        here = first_head == (head == 0)
        delta = jnp.sum(product[mine], axis=0, keepdims=True)
        scores = contract(jnp.where(here, key, zero), query, 1, 1)
        probs = jnp.exp(scores - log_ref[0, head : head + 1])
        grad_probs = contract(jnp.where(here, value, zero), grad, 1, 1)
        grad_scores = (probs * (grad_probs - delta)).astype(low)
        value_grads.append(jnp.dot(probs.astype(low), grad, preferred_element_type=jnp.float32))
        key_grads.append(jnp.dot(grad_scores, query, preferred_element_type=jnp.float32))
        query_grads.append(jnp.dot(key_turned[mine], grad_scores, preferred_element_type=jnp.float32))
    cosine, sine = cos_ref[...], sin_ref[...]

    def rotate_back(values):
        return values * cosine + lane_swap(values * sine)

    parts = [
        rotate_back(jnp.transpose(jnp.concatenate(query_grads, axis=0)) * 0.125),
        rotate_back(jnp.where(first_head, key_grads[0], key_grads[1])),
        jnp.where(first_head, value_grads[0], value_grads[1]),
    ]
    for at, part in enumerate(parts):
        part = part.astype(low)
        out_ref[:, at * 128 : (at + 1) * 128] = part
        bias_ref[:, at * 128 : (at + 1) * 128] = jnp.sum(part.astype(jnp.float32), axis=0, keepdims=True)


def attend_back(qkv, grad, turned, logs, cosine, sine):
    length = qkv.shape[0]
    pairs = qkv.shape[1] // 384
    return pl.pallas_call(
        attend_back_kernel,
        grid=(pairs,),
        in_specs=[
            pl.BlockSpec((length, 384), lambda i: (0, i)),
            pl.BlockSpec((length, 128), lambda i: (0, i)),
            pl.BlockSpec((1, 128, length), lambda i: (i, 0, 0)),
            pl.BlockSpec((1, 2, length), lambda i: (i, 0, 0)),
            pl.BlockSpec((length, 128), lambda i: (0, 0)),
            pl.BlockSpec((length, 128), lambda i: (0, 0)),
        ],
        out_specs=[
            pl.BlockSpec((length, 384), lambda i: (0, i)),
            pl.BlockSpec((1, 384), lambda i: (0, i)),
        ],
        out_shape=[
            jax.ShapeDtypeStruct((length, 384 * pairs), jnp.bfloat16),
            jax.ShapeDtypeStruct((1, 384 * pairs), jnp.float32),
        ],
        cost_estimate=pl.CostEstimate(flops=27 * 10**9, transcendentals=0, bytes_accessed=16 * 2**20),
        name="attend_back",
    )(qkv, grad, turned, logs, cosine, sine)


def assemble_kernel(place_ref, own_ref, x_ref, y_ref, even_ref, odd_ref, *out_refs):
    rows = even_ref.shape[0]
    start = 0
    for out_ref in out_refs:
        cols = slice(start, start + out_ref.shape[1])
        start += out_ref.shape[1]
        for at, ref in enumerate((own_ref, x_ref, y_ref)):
            out_ref[pl.ds(pl.multiple_of((at ^ place_ref[0]) * 2 * rows, 2 * rows), 2 * rows)] = ref[:, cols]
        last = (3 ^ place_ref[0]) * 2 * rows
        out_ref[pl.ds(pl.multiple_of(last, rows), rows)] = even_ref[:, cols]
        out_ref[pl.ds(pl.multiple_of(last + rows, rows), rows)] = odd_ref[:, cols]


def assemble(place, pieces, widths):
    rows = pieces[3].shape[0]
    total = sum(widths)
    return pl.pallas_call(
        assemble_kernel,
        grid_spec=pltpu.PrefetchScalarGridSpec(
            num_scalar_prefetch=1,
            grid=(4,),
            in_specs=[pl.BlockSpec((item.shape[0], total), lambda i, place: (0, i)) for item in pieces],
            out_specs=[pl.BlockSpec((8 * rows, cols), lambda i, place: (0, i)) for cols in widths],
        ),
        out_shape=[jax.ShapeDtypeStruct((8 * rows, 4 * cols), jnp.bfloat16) for cols in widths],
        cost_estimate=pl.CostEstimate(flops=0, transcendentals=0, bytes_accessed=16 * 2**20),
        name="assemble",
    )(place, *pieces)


def deal_kernel(place_ref, *refs):
    in_refs, out_refs = refs[:-4], refs[-4:]
    rows = out_refs[0].shape[1]
    start = 0
    for ref in in_refs:
        cols = slice(start, start + ref.shape[1])
        start += ref.shape[1]
        for half, kept_ref, sent_ref, bit in ((0, out_refs[0], out_refs[1], 2), (1, out_refs[2], out_refs[3], 1)):
            for out_ref, from_bit in ((kept_ref, 0), (sent_ref, bit)):
                for at in range(2):
                    block = (at * (3 - bit) + from_bit) ^ place_ref[0]
                    first_row = pl.multiple_of((2 * block + half) * rows, rows)
                    out_ref[at, :, cols] = ref[pl.ds(first_row, rows)]


def deal(place, grads):
    rows = grads[0].shape[0] // 8
    widths = [item.shape[1] // 4 for item in grads]
    total = sum(widths)
    return pl.pallas_call(
        deal_kernel,
        grid_spec=pltpu.PrefetchScalarGridSpec(
            num_scalar_prefetch=1,
            grid=(4,),
            in_specs=[pl.BlockSpec((8 * rows, cols), lambda i, place: (0, i)) for cols in widths],
            out_specs=[pl.BlockSpec((2, rows, total), lambda i, place: (0, 0, i))] * 4,
        ),
        out_shape=[jax.ShapeDtypeStruct((2, rows, 4 * total), jnp.bfloat16)] * 4,
        cost_estimate=pl.CostEstimate(flops=0, transcendentals=0, bytes_accessed=16 * 2**20),
        name="deal",
    )(place, *grads)


def after(values, earlier):
    return lax.optimization_barrier((values, earlier))[0]


EVERY = ("y", "x", "core", "tensor")


def one_clip_per_chip(mesh):
    return mesh.shape["dp"] == 8 and mesh.shape["tensor"] == 4


def swap(values, axis, bit=1):
    return lax.ppermute(values, axis, [(i, i ^ bit) for i in range(4 if axis == "tensor" else 2)])


def clip_routes(back):
    routes = []
    for turn in range(2):
        pairs = []
        for column in range(4):
            for core in range(2):
                for place in range(4):
                    source = (2 * column + core) * 4 + place
                    target = (2 * column + place // 2) * 4 + 2 * core + (turn ^ (place % 2))
                    pairs.append((target, source) if back else (source, target))
        routes.append(pairs)
    return routes


def pick(flag, first, second):
    return jnp.where(flag, second, first)


def to_clips(values):
    odd = lax.axis_index("tensor") % 2 == 1
    arrived = []
    for turn, pairs in enumerate(clip_routes(False)):
        sent = pick(odd, values[turn], values[1 - turn])
        arrived.append(lax.ppermute(sent, EVERY, pairs))
    return jnp.concatenate(
        [pick(odd, arrived[0], arrived[1]), pick(odd, arrived[1], arrived[0])], axis=0
    )


def from_clips(values):
    odd = lax.axis_index("tensor") % 2 == 1
    rows = values.shape[0] // 2
    arrived = []
    for turn, pairs in enumerate(clip_routes(True)):
        sent = pick(odd, values[turn * rows : (turn + 1) * rows], values[(1 - turn) * rows : (2 - turn) * rows])
        arrived.append(lax.ppermute(sent, EVERY, pairs))
    return jnp.stack([pick(odd, arrived[0], arrived[1]), pick(odd, arrived[1], arrived[0])])


def three_parts(values):
    high = lax.reduce_precision(values, 8, 7)
    rest = values - high
    middle = lax.reduce_precision(rest, 8, 7)
    low = rest - middle
    return jnp.stack([high, middle, low]).astype(jnp.bfloat16)


def clip_body(
    activations,
    cotangent,
    attn_gain,
    attn_shift,
    qkv_weight,
    qkv_bias,
    out_weight,
    out_bias,
    mlp_gain,
    mlp_shift,
    fc1_weight,
    fc1_bias,
    fc2_weight,
    fc2_bias,
):
    core, at_x, at_y, at_z = (lax.axis_index(name) for name in ("core", "x", "y", "tensor"))
    place = (2 * at_y + at_x).astype(jnp.int32).reshape(1)
    width = activations.shape[2]
    length = activations.shape[1] * 4
    half_rows = length // 2
    own_rows = qkv_weight.shape[0]
    half_heads = qkv_weight.shape[1] // (6 * HD)
    qkv_cols = half_heads * 3 * HD
    out_cols = out_weight.shape[1] // 2
    unit_cols = fc1_weight.shape[1] // 2
    low = jnp.bfloat16

    def first_half(values):
        return lax.slice_in_dim(values, 0, values.shape[-1] // 2, axis=values.ndim - 1)

    def second_half(values):
        return lax.slice_in_dim(values, values.shape[-1] // 2, values.shape[-1], axis=values.ndim - 1)

    def own_half(values):
        return pick(core == 1, first_half(values), second_half(values))

    def other_half(values):
        return pick(core == 1, second_half(values), first_half(values))

    def by_kind(values):
        lead = values.shape[:-1]
        split = values.reshape(lead + (2, half_heads, 3, HD))
        return jnp.swapaxes(split, -3, -2).reshape(values.shape)

    def by_head(values):
        lead = values.shape[:-1]
        split = values.reshape(lead + (2, 3, half_heads, HD))
        return jnp.swapaxes(split, -3, -2).reshape(values.shape)

    columns = (by_kind(qkv_weight), out_weight, fc1_weight, fc2_weight)
    mine = jnp.concatenate([own_half(item) for item in columns], axis=1)
    theirs = swap(jnp.concatenate([other_half(item) for item in columns], axis=1), "core")
    held = jnp.concatenate([pick(core == 1, mine, theirs), pick(core == 1, theirs, mine)], axis=0)

    def along_z(own, wait=None):
        one = swap(own, "tensor", 1)
        two = swap(own, "tensor", 2)
        two = two if wait is None else after(two, wait)
        return [own, one, two, swap(two, "tensor", 1)]

    def over_plane(blocks, wait=None):
        own = jnp.concatenate(blocks, axis=1)
        from_x, from_y = swap(own, "x"), swap(own, "y")
        if wait is not None:
            from_x, from_y = after((from_x, from_y), wait)
        return own, from_x, from_y, swap(from_y[:own_rows], "x"), swap(from_x[own_rows:], "y")

    lines = jnp.concatenate([own_half(by_kind(qkv_bias)), own_half(fc1_bias)])
    lines = jnp.pad(three_parts(lines), ((0, 0), (0, 3 * qkv_cols - lines.shape[0]))).reshape(9, qkv_cols)
    blocks = along_z(jnp.concatenate([held[:, :qkv_cols], lines, jnp.zeros((7, qkv_cols), low)], axis=0))
    tokens = to_clips(after(activations, (blocks[1], blocks[3]))).astype(jnp.float32)
    lines = jnp.stack([item[2 * own_rows : 2 * own_rows + 9] for item in blocks])
    lines = lines.astype(jnp.float32).reshape(4, 3, 3 * qkv_cols).sum(axis=1)
    bias_qkv = lines[:, :qkv_cols].reshape(-1)
    bias_up = lines[:, qkv_cols : qkv_cols + unit_cols].reshape(-1)
    pieces = over_plane([item[: 2 * own_rows] for item in blocks])
    (weight_qkv,) = assemble(place, pieces, [qkv_cols])

    def both_halves(values):
        other = swap(values, "core")
        return jnp.concatenate([pick(core == 1, values, other), pick(core == 1, other, values)], axis=0)

    def part_sum(values):
        halves = values.reshape((2, half_rows) + values.shape[1:])
        sent = pick(core == 1, halves[1], halves[0]).astype(low)
        return pick(core == 1, halves[0], halves[1]) + swap(sent, "core").astype(jnp.float32)

    cosine, sine = (jnp.concatenate([item, item], axis=1) for item in rotary_tables(length))

    first_all = both_halves(norm_rows(tokens, attn_gain, attn_shift).astype(low))
    qkv, heads_out, turned, log_total = attend(first_all, weight_qkv, bias_qkv, cosine, sine)

    own = after(held[:, qkv_cols : qkv_cols + out_cols + unit_cols], blocks[3])
    blocks = along_z(own, pieces[1:3])
    blocks[0] = after(blocks[0], pieces[3:])
    pieces = over_plane(blocks, heads_out)

    own = after(held[:, qkv_cols + out_cols + unit_cols :], blocks[3])
    blocks = along_z(own)
    pieces = pieces[:3] + after(pieces[3:], blocks[1:])
    weight_out, weight_up = assemble(place, pieces, [out_cols, unit_cols])
    resid = tokens + part_sum(contract(heads_out, weight_out, 1, 1)) + out_bias
    second_all = both_halves(norm_rows(resid, mlp_gain, mlp_shift).astype(low))

    blocks[0] = after(blocks[0], pieces[3:])
    pieces = over_plane(blocks, second_all)
    grad_own = to_clips(after(cotangent, second_all))

    hidden = jnp.dot(after(second_all, pieces[1:3]), weight_up, preferred_element_type=jnp.float32) + bias_up
    share = 0.5 + 0.5 * lax.erf(hidden * math.sqrt(0.5))
    act = (hidden * share).astype(low)
    slope = (share + hidden * jnp.exp(-0.5 * hidden * hidden) * (1.0 / math.sqrt(2.0 * math.pi))).astype(low)
    pieces = pieces[:3] + after(pieces[3:], act)
    (weight_down,) = assemble(place, pieces, [unit_cols])
    result = resid + part_sum(contract(act, weight_down, 1, 1)) + fc2_bias
    output = from_clips(result.astype(low))

    def to_core(total):
        kept = pick(core == 1, total[0], total[1])
        came = swap(pick(core == 1, total[1], total[0]), "core")
        return jnp.concatenate(
            [pick(core == 1, kept, came), pick(core == 1, came, kept)], axis=-1
        ).astype(jnp.float32)

    def dealt(*grads):
        return deal(place, [item.astype(low) for item in grads])

    def first_back(parts, wait):
        kept_even, sent_even, kept_odd, sent_odd = parts
        came = after((swap(sent_even, "y"), swap(sent_odd, "x")), wait)
        return kept_even + came[0], kept_odd + came[1]

    def second_back(even, odd, wait):
        came = after((swap(even[1], "x"), swap(odd[1], "y")), wait)
        return jnp.concatenate([even[0] + came[0], odd[0] + came[1]]), came

    def along_z_back(total, wait, later):
        cols = total.shape[1] // 4
        own, one, two, three = (total[:, at * cols : (at + 1) * cols] for at in range(4))
        one = swap(one, "tensor", 1)
        two = swap(two + after(swap(three, "tensor", 1), wait), "tensor", 2)
        one, two = after((one, two), later)
        return to_core((own + one + two).reshape(2, own_rows, cols))

    grad_top = grad_own.astype(jnp.float32)
    grad_all = both_halves(grad_own)
    sum_fc2_bias = jnp.sum(grad_top, axis=0)
    parts_fc2 = dealt(contract(grad_all, act, 0, 0))
    grad_act = jnp.dot(after(grad_all, parts_fc2), weight_down, preferred_element_type=jnp.float32)
    grad_hidden = (grad_act * slope.astype(jnp.float32)).astype(low)
    sum_fc1_bias = jnp.sum(grad_hidden, axis=0, dtype=jnp.float32)
    grad_second_part = contract(grad_hidden, weight_up, 1, 1)
    sent_fc2 = first_back(parts_fc2, grad_second_part)
    grad_second = part_sum(grad_second_part)
    second_pull = jax.vjp(norm_rows, resid, mlp_gain, mlp_shift)[1]
    grad_resid_norm, sum_mlp_gain, sum_mlp_shift = second_pull(grad_second)
    grad_resid = grad_top + grad_resid_norm
    sum_out_bias = jnp.sum(grad_resid, axis=0)
    resid_all = both_halves(grad_resid.astype(low))
    grad_fc1 = contract(after(second_all, sent_fc2[0]), grad_hidden, 0, 0)
    parts_up = dealt(contract(resid_all, heads_out, 0, 0), grad_fc1)
    grad_heads = jnp.dot(resid_all, weight_out, preferred_element_type=jnp.float32).astype(low)
    total_fc2, came_fc2 = second_back(*sent_fc2, grad_heads)
    grad_packed, sum_qkv_bias = attend_back(qkv, after(grad_heads, (parts_up, came_fc2)), turned, log_total, cosine, sine)
    sent_up = first_back(parts_up, grad_packed)
    parts_qkv = dealt(contract(after(first_all, sent_up), grad_packed, 0, 0))
    total_up, came_up = second_back(*sent_up, parts_qkv)
    grad_first_part = contract(after(grad_packed, came_up), weight_qkv, 1, 1)
    grad_first = part_sum(grad_first_part)
    first_pull = jax.vjp(norm_rows, tokens, attn_gain, attn_shift)[1]
    grad_input_norm, sum_attn_gain, sum_attn_shift = first_pull(grad_first)
    input_low = from_clips((grad_resid + grad_input_norm).astype(low))
    input_grad = input_low.astype(jnp.float32)

    grad_fc2_weight = along_z_back(total_fc2, grad_packed, parts_qkv)
    both_weights = along_z_back(total_up, grad_first, input_low)
    cuts = both_weights.shape[1] // 2
    both_weights = [both_weights[:, :cuts], both_weights[:, cuts:]]
    grad_out_weight = jnp.concatenate([item[:, :out_cols] for item in both_weights], axis=1)
    grad_fc1_weight = jnp.concatenate([item[:, out_cols:] for item in both_weights], axis=1)
    sent_qkv = first_back(parts_qkv, grad_first)
    total, came_qkv = second_back(*sent_qkv, grad_first)
    grad_qkv_weight = by_head(along_z_back(total, grad_first, grad_first))

    def by_core(values):
        none = jnp.zeros_like(values)
        return [pick(core == 1, values, none), pick(core == 1, none, values)]

    def by_owner(values, cols):
        first, second, third, fourth = (values.reshape(-1)[at * cols : (at + 1) * cols] for at in range(4))
        odd = at_z % 2 == 1
        first, second = pick(odd, first, second), pick(odd, second, first)
        third, fourth = pick(odd, third, fourth), pick(odd, fourth, third)
        lower, upper = jnp.concatenate([first, second]), jnp.concatenate([third, fourth])
        far = at_z // 2 == 1
        return jnp.concatenate([pick(far, lower, upper), pick(far, upper, lower)])

    sums = [sum_attn_gain, sum_attn_shift, sum_out_bias, sum_mlp_gain, sum_mlp_shift, sum_fc2_bias]
    sums = jnp.concatenate(sums + by_core(by_owner(sum_qkv_bias, qkv_cols)) + by_core(by_owner(sum_fc1_bias, unit_cols)))
    stages = (("core", 1, sent_qkv), ("x", 1, None), ("y", 1, came_qkv), ("tensor", 1, input_low), ("tensor", 2, None))
    for axis, bit, earlier in stages:
        if earlier is not None:
            sums = after(sums, earlier)
        sums = sums + swap(sums, axis, bit)
    vectors = sums[: 6 * width].reshape(6, width)
    qkv_sums = sums[6 * width : 6 * width + 8 * qkv_cols].reshape(2, 4, qkv_cols)
    unit_sums = sums[6 * width + 8 * qkv_cols :].reshape(2, 4, unit_cols)

    def own_place(values):
        return lax.dynamic_index_in_dim(values, at_z, 1, keepdims=False).reshape(-1)

    return (
        output,
        input_grad,
        vectors[0],
        vectors[1],
        grad_qkv_weight,
        by_head(own_place(qkv_sums)),
        grad_out_weight,
        vectors[2],
        vectors[3],
        vectors[4],
        grad_fc1_weight,
        own_place(unit_sums),
        grad_fc2_weight,
        vectors[5],
    )


def solution(mesh):
    if one_clip_per_chip(mesh):
        plan, rows = clip_body, ("y", "x", "core")
        mesh = jax.sharding.Mesh(mesh.devices.reshape(2, 2, 2, 4), EVERY)
    else:
        plan, rows = body, "dp"
    tokens, matrix, columns = P(rows, "tensor", None), P(rows, "tensor"), P("tensor")
    params = (P(), P(), matrix, columns, matrix, P(), P(), P(), matrix, columns, matrix, P())
    both = (tokens, tokens) + params
    return jax.shard_map(plan, mesh=mesh, in_specs=both, out_specs=both, check_vma=False)
```

```python
import math

import jax
import jax.numpy as jnp
from jax import lax
from jax.experimental import pallas as pl
from jax.experimental.pallas import tpu as pltpu
from jax.sharding import PartitionSpec as P

HD = 64
GRID = 16


def norm_rows(values, gain_vec, shift_vec):
    row_mean = jnp.mean(values, axis=-1, keepdims=True)
    centred = values - row_mean
    variance = jnp.mean(centred * centred, axis=-1, keepdims=True)
    return centred * lax.rsqrt(variance + 1e-06) * gain_vec + shift_vec


def rotary_tables(length):
    section = 2 * (HD // 3 // 2)
    half = section // 2
    position = jnp.arange(length)
    frame = (position // (GRID * GRID)).astype(jnp.float32)
    row_pos = (position // GRID % GRID).astype(jnp.float32)
    col_pos = (position % GRID).astype(jnp.float32)
    omega = 1.0 / 10000.0 ** (jnp.arange(half).astype(jnp.float32) / half)
    pieces = [
        jnp.repeat(coordinate[:, None] * omega[None, :], 2, axis=1)
        for coordinate in (frame, row_pos, col_pos)
    ]
    pieces.append(jnp.zeros((length, HD - 3 * section), jnp.float32))
    angles = jnp.concatenate(pieces, axis=1)
    parity = jnp.where(jnp.arange(HD) % 2 == 0, -1.0, 1.0).astype(jnp.float32)
    return (jnp.cos(angles), jnp.sin(angles) * parity)


def pair_swap(values):
    shape = values.shape
    paired = values.reshape(shape[:-1] + (shape[-1] // 2, 2))
    return paired[..., ::-1].reshape(shape)


def contract(left, right, left_dim, right_dim):
    return lax.dot_general(
        left, right, (((left_dim,), (right_dim,)), ((), ())), preferred_element_type=jnp.float32
    )


def exact_gelu(values):
    return jax.nn.gelu(values, approximate=False)


def body(
    activations,
    cotangent,
    attn_gain,
    attn_shift,
    qkv_weight,
    qkv_bias,
    out_weight,
    out_bias,
    mlp_gain,
    mlp_shift,
    fc1_weight,
    fc1_bias,
    fc2_weight,
    fc2_bias,
):
    tensor_size = lax.axis_size("tensor")
    tensor_rank = lax.axis_index("tensor")
    row_count = activations.shape[1]
    width = activations.shape[2]
    length = row_count * tensor_size
    block_rows = min(512, length)
    block_count = length // block_rows
    local_heads = qkv_weight.shape[1] // (3 * HD)
    packed_cols = qkv_weight.shape[1]
    unit_cols = fc1_weight.shape[1]
    factor = 1.0 / math.sqrt(HD)
    cosine, sine = rotary_tables(length)
    cosine = cosine[:, None, :]
    sine = sine[:, None, :]

    def rotate(values):
        return values * cosine + pair_swap(values) * sine

    def rotate_back(values):
        return values * cosine + pair_swap(values * sine)

    def fetch():
        gathered = (
            lax.all_gather(qkv_weight, "dp", axis=0, tiled=True),
            lax.all_gather(out_weight, "dp", axis=0, tiled=True),
            lax.all_gather(fc1_weight, "dp", axis=0, tiled=True),
            lax.all_gather(fc2_weight, "dp", axis=0, tiled=True),
        )
        return (gathered, gathered)

    def seq_gather(values):
        return lax.all_gather(values, "tensor", axis=0, tiled=True)

    def part_sum(values):
        return lax.psum_scatter(
            values.astype(jnp.bfloat16), "tensor", scatter_dimension=0, tiled=True
        ).astype(jnp.float32)

    def grad_gather(values):
        return lax.all_gather(values, "tensor", axis=0, tiled=True)

    def grad_sum(values):
        return lax.psum_scatter(
            values.astype(jnp.bfloat16), "tensor", scatter_dimension=0, tiled=True
        ).astype(jnp.float32)

    def forward(inputs, weights):
        (weight_qkv, weight_out, weight_up, weight_down), (
            whole_qkv,
            whole_out,
            whole_up,
            whole_down,
        ) = weights
        first_all = seq_gather(norm_rows(inputs, attn_gain, attn_shift).astype(jnp.bfloat16))
        packed = (
            jnp.dot(first_all, weight_qkv, preferred_element_type=jnp.float32) + qkv_bias
        ).reshape(length, local_heads, 3, HD)
        query = rotate(packed[:, :, 0]).astype(jnp.bfloat16)
        key_all = rotate(packed[:, :, 1]).astype(jnp.bfloat16)
        value_all = packed[:, :, 2].astype(jnp.bfloat16)
        outputs = []
        log_sums = []
        for block in range(block_count):
            query_block = query[block * block_rows : (block + 1) * block_rows]
            scores = (
                jnp.einsum("qhd,khd->hqk", query_block, key_all, preferred_element_type=jnp.float32)
                * factor
            )
            row_max = jnp.max(scores, axis=-1, keepdims=True)
            expo = jnp.exp(scores - row_max)
            row_total = jnp.sum(expo, axis=-1, keepdims=True)
            weights_low = (expo / row_total).astype(jnp.bfloat16)
            outputs.append(
                jnp.einsum(
                    "hqk,khd->qhd", weights_low, value_all, preferred_element_type=jnp.float32
                )
            )
            log_sums.append(row_max + jnp.log(row_total))
        heads_out = (
            jnp.concatenate(outputs, axis=0).reshape(length, local_heads * HD).astype(jnp.bfloat16)
        )
        log_total = jnp.concatenate(log_sums, axis=1)
        attended = part_sum(contract(heads_out, weight_out, 1, 1))
        resid = inputs + attended + out_bias
        second_all = seq_gather(norm_rows(resid, mlp_gain, mlp_shift).astype(jnp.bfloat16))
        hidden = jnp.dot(second_all, weight_up, preferred_element_type=jnp.float32) + fc1_bias
        act = exact_gelu(hidden).astype(jnp.bfloat16)
        branch = part_sum(contract(act, weight_down, 1, 1))
        result = resid + branch + fc2_bias
        kept = (
            first_all,
            query,
            key_all,
            value_all,
            log_total,
            heads_out,
            heads_out,
            resid,
            second_all,
            hidden,
            act,
        )
        return (result, kept)

    def backward(inputs, grad_low, kept, weights):
        (weight_qkv, weight_out, weight_up, weight_down), (
            whole_qkv,
            whole_out,
            whole_up,
            whole_down,
        ) = weights
        (
            first_all,
            query,
            key_all,
            value_all,
            log_total,
            heads_out,
            heads_rows,
            resid,
            second_all,
            hidden,
            act,
        ) = kept
        grad_top = grad_low.astype(jnp.float32)
        grad_fc2_bias = jnp.sum(grad_top, axis=0)
        grad_all = grad_gather(grad_low)
        grad_fc2_weight = contract(grad_all, act, 0, 0)
        grad_act = jnp.dot(grad_all, weight_down, preferred_element_type=jnp.float32)
        gelu_pull = jax.vjp(exact_gelu, hidden)[1]
        grad_hidden = gelu_pull(grad_act)[0].astype(jnp.bfloat16)
        grad_fc1_bias = jnp.sum(grad_hidden, axis=0, dtype=jnp.float32)
        grad_fc1_weight = contract(second_all, grad_hidden, 0, 0)
        grad_second = grad_sum(contract(grad_hidden, weight_up, 1, 1))
        second_pull = jax.vjp(norm_rows, resid, mlp_gain, mlp_shift)[1]
        grad_resid_norm, grad_mlp_gain, grad_mlp_shift = second_pull(grad_second)
        grad_resid = grad_top + grad_resid_norm
        grad_out_bias = jnp.sum(grad_resid, axis=0)
        resid_low = grad_resid.astype(jnp.bfloat16)
        resid_all = grad_gather(resid_low)
        grad_out_weight = contract(resid_all, heads_out, 0, 0)
        grad_heads = jnp.dot(resid_all, weight_out, preferred_element_type=jnp.float32).astype(
            jnp.bfloat16
        )
        grad_heads = grad_heads.reshape(length, local_heads, HD)
        grad_key = jnp.zeros((length, local_heads, HD), jnp.float32)
        grad_value = jnp.zeros((length, local_heads, HD), jnp.float32)
        query_grads = []
        for block in range(block_count):
            lower = block * block_rows
            upper = lower + block_rows
            query_block = query[lower:upper]
            grad_block = grad_heads[lower:upper]
            scores = (
                jnp.einsum("qhd,khd->hqk", query_block, key_all, preferred_element_type=jnp.float32)
                * factor
            )
            probs = jnp.exp(scores - log_total[:, lower:upper])
            grad_value = grad_value + jnp.einsum(
                "hqk,qhd->khd",
                probs.astype(jnp.bfloat16),
                grad_block,
                preferred_element_type=jnp.float32,
            )
            grad_probs = jnp.einsum(
                "qhd,khd->hqk", grad_block, value_all, preferred_element_type=jnp.float32
            )
            grad_scores = (
                probs * (grad_probs - jnp.sum(probs * grad_probs, axis=-1, keepdims=True))
            ).astype(jnp.bfloat16)
            query_grads.append(
                jnp.einsum("hqk,khd->qhd", grad_scores, key_all, preferred_element_type=jnp.float32)
                * factor
            )
            grad_key = (
                grad_key
                + jnp.einsum(
                    "hqk,qhd->khd", grad_scores, query_block, preferred_element_type=jnp.float32
                )
                * factor
            )
        grad_query = jnp.concatenate(query_grads, axis=0)
        grad_packed = jnp.stack(
            [rotate_back(grad_query), rotate_back(grad_key), grad_value], axis=2
        )
        grad_packed = grad_packed.reshape(length, packed_cols).astype(jnp.bfloat16)
        grad_qkv_bias = jnp.sum(grad_packed, axis=0, dtype=jnp.float32)
        grad_qkv_weight = contract(first_all, grad_packed, 0, 0)
        grad_first = grad_sum(contract(grad_packed, weight_qkv, 1, 1))
        first_pull = jax.vjp(norm_rows, inputs, attn_gain, attn_shift)[1]
        grad_input_norm, grad_attn_gain, grad_attn_shift = first_pull(grad_first)
        input_grad = grad_resid + grad_input_norm
        grads = (
            grad_attn_gain,
            grad_attn_shift,
            grad_qkv_weight,
            grad_qkv_bias,
            grad_out_weight,
            grad_out_bias,
            grad_mlp_gain,
            grad_mlp_shift,
            grad_fc1_weight,
            grad_fc1_bias,
            grad_fc2_weight,
            grad_fc2_bias,
        )
        return (input_grad, grads)

    def per_clip(totals, inputs_pair):
        clip_in, clip_grad = inputs_pair
        forward_weights = fetch()
        result, kept = forward(clip_in.astype(jnp.float32), forward_weights)
        backward_weights = fetch()
        input_grad, grads = backward(clip_in.astype(jnp.float32), clip_grad, kept, backward_weights)
        totals = tuple((left + right for left, right in zip(totals, grads)))
        return (totals, (result.astype(jnp.bfloat16), input_grad))

    out_cols = local_heads * HD
    start_totals = (
        jnp.zeros((width,), jnp.float32),
        jnp.zeros((width,), jnp.float32),
        jnp.zeros((width, packed_cols), jnp.float32),
        jnp.zeros((packed_cols,), jnp.float32),
        jnp.zeros((width, out_cols), jnp.float32),
        jnp.zeros((width,), jnp.float32),
        jnp.zeros((width,), jnp.float32),
        jnp.zeros((width,), jnp.float32),
        jnp.zeros((width, unit_cols), jnp.float32),
        jnp.zeros((unit_cols,), jnp.float32),
        jnp.zeros((width, unit_cols), jnp.float32),
        jnp.zeros((width,), jnp.float32),
    )
    totals, (output, input_grad) = lax.scan(per_clip, start_totals, (activations, cotangent))
    out_grad = totals[4]
    weight_sums = (
        lax.psum_scatter(
            totals[2].astype(jnp.bfloat16), "dp", scatter_dimension=0, tiled=True
        ).astype(jnp.float32),
        lax.psum_scatter(
            out_grad.astype(jnp.bfloat16), "dp", scatter_dimension=0, tiled=True
        ).astype(jnp.float32),
        lax.psum_scatter(
            totals[8].astype(jnp.bfloat16), "dp", scatter_dimension=0, tiled=True
        ).astype(jnp.float32),
        lax.psum_scatter(
            totals[10].astype(jnp.bfloat16), "dp", scatter_dimension=0, tiled=True
        ).astype(jnp.float32),
    )
    qkv_place = lax.dynamic_update_slice_in_dim(
        jnp.zeros((packed_cols * tensor_size,), jnp.float32),
        totals[3],
        tensor_rank * packed_cols,
        0,
    )
    unit_place = lax.dynamic_update_slice_in_dim(
        jnp.zeros((unit_cols * tensor_size,), jnp.float32), totals[9], tensor_rank * unit_cols, 0
    )
    summed = lax.psum(
        (totals[0], totals[1], qkv_place, totals[5], totals[6], totals[7], unit_place, totals[11]),
        ("dp", "tensor"),
    )
    grad_qkv_bias = lax.dynamic_slice_in_dim(summed[2], tensor_rank * packed_cols, packed_cols, 0)
    grad_fc1_bias = lax.dynamic_slice_in_dim(summed[6], tensor_rank * unit_cols, unit_cols, 0)
    return (
        output,
        input_grad,
        summed[0],
        summed[1],
        weight_sums[0],
        grad_qkv_bias,
        weight_sums[1],
        summed[3],
        summed[4],
        summed[5],
        weight_sums[2],
        grad_fc1_bias,
        weight_sums[3],
        summed[7],
    )


def lane_swap(values):
    even = lax.broadcasted_iota(jnp.int32, values.shape, 1) % 2 == 0
    return jnp.where(even, pltpu.roll(values, 127, 1), pltpu.roll(values, 1, 1))


def attend_kernel(first_ref, weight_ref, bias_ref, cos_ref, sin_ref, qkv_ref, heads_ref, turned_ref, log_ref):
    low = jnp.bfloat16
    packed = jnp.dot(first_ref[...], weight_ref[...], preferred_element_type=jnp.float32) + bias_ref[...]
    cosine, sine = cos_ref[...], sin_ref[...]

    def rotate(values):
        return values * cosine + lane_swap(values) * sine

    query = (rotate(packed[:, :128]).astype(low).astype(jnp.float32) * 0.125).astype(low)
    key = rotate(packed[:, 128:256]).astype(low)
    value = packed[:, 256:]
    qkv_ref[:, :128] = query
    qkv_ref[:, 128:256] = key
    qkv_ref[:, 256:] = value.astype(low)
    value = jnp.transpose(value).astype(low)
    first_head = lax.broadcasted_iota(jnp.int32, key.shape, 1) < HD
    for head in range(2):
        mine = slice(head * HD, (head + 1) * HD)
        key_here = jnp.where(first_head == (head == 0), key, jnp.zeros_like(key))
        scores = contract(key_here, query, 1, 1)
        top = jnp.max(scores, axis=0, keepdims=True)
        expo = jnp.exp(scores - top)
        total = jnp.sum(expo, axis=0, keepdims=True)
        summed = jnp.dot(value[mine], expo.astype(low), preferred_element_type=jnp.float32)
        turned_ref[0, mine] = summed / total
        log_ref[0, head : head + 1] = top + jnp.log(total)
    heads_ref[...] = jnp.transpose(turned_ref[0]).astype(low)


def attend(first, weight, bias, cosine, sine):
    length, width = first.shape
    pairs = weight.shape[1] // 384
    return pl.pallas_call(
        attend_kernel,
        grid=(pairs,),
        in_specs=[
            pl.BlockSpec((length, width), lambda i: (0, 0)),
            pl.BlockSpec((width, 384), lambda i: (0, i)),
            pl.BlockSpec((1, 384), lambda i: (0, i)),
            pl.BlockSpec((length, 128), lambda i: (0, 0)),
            pl.BlockSpec((length, 128), lambda i: (0, 0)),
        ],
        out_specs=[
            pl.BlockSpec((length, 384), lambda i: (0, i)),
            pl.BlockSpec((length, 128), lambda i: (0, i)),
            pl.BlockSpec((1, 128, length), lambda i: (i, 0, 0)),
            pl.BlockSpec((1, 2, length), lambda i: (i, 0, 0)),
        ],
        out_shape=[
            jax.ShapeDtypeStruct((length, 384 * pairs), jnp.bfloat16),
            jax.ShapeDtypeStruct((length, 128 * pairs), jnp.bfloat16),
            jax.ShapeDtypeStruct((pairs, 128, length), jnp.float32),
            jax.ShapeDtypeStruct((pairs, 2, length), jnp.float32),
        ],
        cost_estimate=pl.CostEstimate(flops=2 * 10**10, transcendentals=0, bytes_accessed=16 * 2**20),
        name="attend",
    )(first, weight, bias.reshape(1, -1), cosine, sine)


def attend_back_kernel(qkv_ref, grad_ref, turned_ref, log_ref, cos_ref, sin_ref, out_ref, bias_ref):
    low = jnp.bfloat16
    query = qkv_ref[:, :128]
    key = qkv_ref[:, 128:256]
    value = qkv_ref[:, 256:]
    grad = grad_ref[...]
    key_turned = jnp.transpose(key.astype(jnp.float32)).astype(low)
    product = jnp.transpose(grad.astype(jnp.float32)) * turned_ref[0]
    first_head = lax.broadcasted_iota(jnp.int32, key.shape, 1) < HD
    zero = jnp.zeros_like(key)
    query_grads, key_grads, value_grads = [], [], []
    for head in range(2):
        mine = slice(head * HD, (head + 1) * HD)
        here = first_head == (head == 0)
        delta = jnp.sum(product[mine], axis=0, keepdims=True)
        scores = contract(jnp.where(here, key, zero), query, 1, 1)
        probs = jnp.exp(scores - log_ref[0, head : head + 1])
        grad_probs = contract(jnp.where(here, value, zero), grad, 1, 1)
        grad_scores = (probs * (grad_probs - delta)).astype(low)
        value_grads.append(jnp.dot(probs.astype(low), grad, preferred_element_type=jnp.float32))
        key_grads.append(jnp.dot(grad_scores, query, preferred_element_type=jnp.float32))
        query_grads.append(jnp.dot(key_turned[mine], grad_scores, preferred_element_type=jnp.float32))
    cosine, sine = cos_ref[...], sin_ref[...]

    def rotate_back(values):
        return values * cosine + lane_swap(values * sine)

    parts = [
        rotate_back(jnp.transpose(jnp.concatenate(query_grads, axis=0)) * 0.125),
        rotate_back(jnp.where(first_head, key_grads[0], key_grads[1])),
        jnp.where(first_head, value_grads[0], value_grads[1]),
    ]
    for at, part in enumerate(parts):
        part = part.astype(low)
        out_ref[:, at * 128 : (at + 1) * 128] = part
        bias_ref[:, at * 128 : (at + 1) * 128] = jnp.sum(part.astype(jnp.float32), axis=0, keepdims=True)


def attend_back(qkv, grad, turned, logs, cosine, sine):
    length = qkv.shape[0]
    pairs = qkv.shape[1] // 384
    return pl.pallas_call(
        attend_back_kernel,
        grid=(pairs,),
        in_specs=[
            pl.BlockSpec((length, 384), lambda i: (0, i)),
            pl.BlockSpec((length, 128), lambda i: (0, i)),
            pl.BlockSpec((1, 128, length), lambda i: (i, 0, 0)),
            pl.BlockSpec((1, 2, length), lambda i: (i, 0, 0)),
            pl.BlockSpec((length, 128), lambda i: (0, 0)),
            pl.BlockSpec((length, 128), lambda i: (0, 0)),
        ],
        out_specs=[
            pl.BlockSpec((length, 384), lambda i: (0, i)),
            pl.BlockSpec((1, 384), lambda i: (0, i)),
        ],
        out_shape=[
            jax.ShapeDtypeStruct((length, 384 * pairs), jnp.bfloat16),
            jax.ShapeDtypeStruct((1, 384 * pairs), jnp.float32),
        ],
        cost_estimate=pl.CostEstimate(flops=27 * 10**9, transcendentals=0, bytes_accessed=16 * 2**20),
        name="attend_back",
    )(qkv, grad, turned, logs, cosine, sine)


def assemble_kernel(place_ref, own_ref, x_ref, y_ref, even_ref, odd_ref, *out_refs):
    rows = even_ref.shape[0]
    start = 0
    for out_ref in out_refs:
        cols = slice(start, start + out_ref.shape[1])
        start += out_ref.shape[1]
        for at, ref in enumerate((own_ref, x_ref, y_ref)):
            out_ref[pl.ds(pl.multiple_of((at ^ place_ref[0]) * 2 * rows, 2 * rows), 2 * rows)] = ref[:, cols]
        last = (3 ^ place_ref[0]) * 2 * rows
        out_ref[pl.ds(pl.multiple_of(last, rows), rows)] = even_ref[:, cols]
        out_ref[pl.ds(pl.multiple_of(last + rows, rows), rows)] = odd_ref[:, cols]


def assemble(place, pieces, widths):
    rows = pieces[3].shape[0]
    total = sum(widths)
    return pl.pallas_call(
        assemble_kernel,
        grid_spec=pltpu.PrefetchScalarGridSpec(
            num_scalar_prefetch=1,
            grid=(4,),
            in_specs=[pl.BlockSpec((item.shape[0], total), lambda i, place: (0, i)) for item in pieces],
            out_specs=[pl.BlockSpec((8 * rows, cols), lambda i, place: (0, i)) for cols in widths],
        ),
        out_shape=[jax.ShapeDtypeStruct((8 * rows, 4 * cols), jnp.bfloat16) for cols in widths],
        cost_estimate=pl.CostEstimate(flops=0, transcendentals=0, bytes_accessed=16 * 2**20),
        name="assemble",
    )(place, *pieces)


def deal_kernel(place_ref, *refs):
    in_refs, out_refs = refs[:-4], refs[-4:]
    rows = out_refs[0].shape[1]
    start = 0
    for ref in in_refs:
        cols = slice(start, start + ref.shape[1])
        start += ref.shape[1]
        for half, kept_ref, sent_ref, bit in ((0, out_refs[0], out_refs[1], 2), (1, out_refs[2], out_refs[3], 1)):
            for out_ref, from_bit in ((kept_ref, 0), (sent_ref, bit)):
                for at in range(2):
                    block = (at * (3 - bit) + from_bit) ^ place_ref[0]
                    first_row = pl.multiple_of((2 * block + half) * rows, rows)
                    out_ref[at, :, cols] = ref[pl.ds(first_row, rows)]


def deal(place, grads):
    rows = grads[0].shape[0] // 8
    widths = [item.shape[1] // 4 for item in grads]
    total = sum(widths)
    return pl.pallas_call(
        deal_kernel,
        grid_spec=pltpu.PrefetchScalarGridSpec(
            num_scalar_prefetch=1,
            grid=(4,),
            in_specs=[pl.BlockSpec((8 * rows, cols), lambda i, place: (0, i)) for cols in widths],
            out_specs=[pl.BlockSpec((2, rows, total), lambda i, place: (0, 0, i))] * 4,
        ),
        out_shape=[jax.ShapeDtypeStruct((2, rows, 4 * total), jnp.bfloat16)] * 4,
        cost_estimate=pl.CostEstimate(flops=0, transcendentals=0, bytes_accessed=16 * 2**20),
        name="deal",
    )(place, *grads)


def after(values, earlier):
    return lax.optimization_barrier((values, earlier))[0]


EVERY = ("y", "x", "core", "tensor")


def one_clip_per_chip(mesh):
    return mesh.shape["dp"] == 8 and mesh.shape["tensor"] == 4


def swap(values, axis, bit=1):
    return lax.ppermute(values, axis, [(i, i ^ bit) for i in range(4 if axis == "tensor" else 2)])


def clip_routes(back):
    routes = []
    for turn in range(2):
        pairs = []
        for column in range(4):
            for core in range(2):
                for place in range(4):
                    source = (2 * column + core) * 4 + place
                    target = (2 * column + place // 2) * 4 + 2 * core + (turn ^ (place % 2))
                    pairs.append((target, source) if back else (source, target))
        routes.append(pairs)
    return routes


def pick(flag, first, second):
    return jnp.where(flag, second, first)


def to_clips(values):
    odd = lax.axis_index("tensor") % 2 == 1
    arrived = []
    for turn, pairs in enumerate(clip_routes(False)):
        sent = pick(odd, values[turn], values[1 - turn])
        arrived.append(lax.ppermute(sent, EVERY, pairs))
    return arrived, jnp.concatenate(
        [pick(odd, arrived[0], arrived[1]), pick(odd, arrived[1], arrived[0])], axis=0
    )


def from_clips(values):
    odd = lax.axis_index("tensor") % 2 == 1
    rows = values.shape[0] // 2
    arrived = []
    for turn, pairs in enumerate(clip_routes(True)):
        sent = pick(odd, values[turn * rows : (turn + 1) * rows], values[(1 - turn) * rows : (2 - turn) * rows])
        arrived.append(lax.ppermute(sent, EVERY, pairs))
    return jnp.stack([pick(odd, arrived[0], arrived[1]), pick(odd, arrived[1], arrived[0])])


def three_parts(values):
    high = lax.reduce_precision(values, 8, 7)
    rest = values - high
    middle = lax.reduce_precision(rest, 8, 7)
    low = rest - middle
    return jnp.stack([high, middle, low]).astype(jnp.bfloat16)


def clip_body(
    activations,
    cotangent,
    attn_gain,
    attn_shift,
    qkv_weight,
    qkv_bias,
    out_weight,
    out_bias,
    mlp_gain,
    mlp_shift,
    fc1_weight,
    fc1_bias,
    fc2_weight,
    fc2_bias,
):
    core, at_x, at_y, at_z = (lax.axis_index(name) for name in ("core", "x", "y", "tensor"))
    place = (2 * at_y + at_x).astype(jnp.int32).reshape(1)
    width = activations.shape[2]
    length = activations.shape[1] * 4
    half_rows = length // 2
    own_rows = qkv_weight.shape[0]
    half_heads = qkv_weight.shape[1] // (6 * HD)
    qkv_cols = half_heads * 3 * HD
    out_cols = out_weight.shape[1] // 2
    unit_cols = fc1_weight.shape[1] // 2
    low = jnp.bfloat16

    def first_half(values):
        return lax.slice_in_dim(values, 0, values.shape[-1] // 2, axis=values.ndim - 1)

    def second_half(values):
        return lax.slice_in_dim(values, values.shape[-1] // 2, values.shape[-1], axis=values.ndim - 1)

    def own_half(values):
        return pick(core == 1, first_half(values), second_half(values))

    def other_half(values):
        return pick(core == 1, second_half(values), first_half(values))

    def by_kind(values):
        lead = values.shape[:-1]
        split = values.reshape(lead + (2, half_heads, 3, HD))
        return jnp.swapaxes(split, -3, -2).reshape(values.shape)

    def by_head(values):
        lead = values.shape[:-1]
        split = values.reshape(lead + (2, 3, half_heads, HD))
        return jnp.swapaxes(split, -3, -2).reshape(values.shape)

    columns = (by_kind(qkv_weight), out_weight, fc1_weight, fc2_weight)
    mine = jnp.concatenate([own_half(item) for item in columns], axis=1)
    theirs = swap(jnp.concatenate([other_half(item) for item in columns], axis=1), "core")
    held = jnp.concatenate([pick(core == 1, mine, theirs), pick(core == 1, theirs, mine)], axis=0)

    def along_z(own, wait=None):
        one = swap(own, "tensor", 1)
        two = swap(own, "tensor", 2)
        two = two if wait is None else after(two, wait)
        return [own, one, two, swap(two, "tensor", 1)]

    def over_plane(blocks, wait=None):
        own = jnp.concatenate(blocks, axis=1)
        from_x, from_y = swap(own, "x"), swap(own, "y")
        if wait is not None:
            from_x, from_y = after((from_x, from_y), wait)
        return own, from_x, from_y, swap(from_y[:own_rows], "x"), swap(from_x[own_rows:], "y")

    lines = jnp.concatenate([own_half(by_kind(qkv_bias)), own_half(fc1_bias)])
    lines = jnp.pad(three_parts(lines), ((0, 0), (0, 3 * qkv_cols - lines.shape[0]))).reshape(9, qkv_cols)
    blocks = along_z(jnp.concatenate([held[:, :qkv_cols], lines, jnp.zeros((7, qkv_cols), low)], axis=0))
    tokens = to_clips(after(activations, (blocks[1], blocks[3])))[1].astype(jnp.float32)
    lines = jnp.stack([item[2 * own_rows : 2 * own_rows + 9] for item in blocks])
    lines = lines.astype(jnp.float32).reshape(4, 3, 3 * qkv_cols).sum(axis=1)
    bias_qkv = lines[:, :qkv_cols].reshape(-1)
    bias_up = lines[:, qkv_cols : qkv_cols + unit_cols].reshape(-1)
    blocks_up = along_z(after(held[:, qkv_cols : qkv_cols + out_cols + unit_cols], blocks[3]))
    pieces = over_plane([item[: 2 * own_rows] for item in blocks], blocks_up[1:3])
    (weight_qkv,) = assemble(place, pieces, [qkv_cols])
    blocks_down = along_z(after(held[:, qkv_cols + out_cols + unit_cols :], blocks_up[3]))
    weight_qkv = after(weight_qkv, blocks_down[1:3])

    def both_halves(values):
        other = swap(values, "core")
        return jnp.concatenate([pick(core == 1, values, other), pick(core == 1, other, values)], axis=0)

    def part_sum(values):
        halves = values.reshape((2, half_rows) + values.shape[1:])
        sent = pick(core == 1, halves[1], halves[0]).astype(low)
        return pick(core == 1, halves[0], halves[1]) + swap(sent, "core").astype(jnp.float32)

    cosine, sine = (jnp.concatenate([item, item], axis=1) for item in rotary_tables(length))

    first_all = both_halves(norm_rows(tokens, attn_gain, attn_shift).astype(low))
    qkv, heads_out, turned, log_total = attend(first_all, weight_qkv, bias_qkv, cosine, sine)

    blocks_up[0] = after(blocks_up[0], pieces[3:])
    pieces = over_plane(blocks_up, heads_out)
    pieces = pieces[:3] + after(pieces[3:], blocks_down[3])
    weight_out, weight_up = assemble(place, pieces, [out_cols, unit_cols])
    resid = tokens + part_sum(contract(heads_out, weight_out, 1, 1)) + out_bias
    second_all = both_halves(norm_rows(resid, mlp_gain, mlp_shift).astype(low))

    blocks_down[0] = after(blocks_down[0], pieces[3:])
    arrived, grad_own = to_clips(after(cotangent, blocks_down[3]))
    pieces = over_plane(blocks_down, second_all)

    second_all = after(second_all, (pieces[1:3], arrived))
    hidden = jnp.dot(second_all, weight_up, preferred_element_type=jnp.float32) + bias_up
    share = 0.5 + 0.5 * lax.erf(hidden * math.sqrt(0.5))
    act = (hidden * share).astype(low)
    slope = (share + hidden * jnp.exp(-0.5 * hidden * hidden) * (1.0 / math.sqrt(2.0 * math.pi))).astype(low)
    pieces = pieces[:3] + after(pieces[3:], act)
    (weight_down,) = assemble(place, pieces, [unit_cols])
    result = resid + part_sum(contract(act, weight_down, 1, 1)) + fc2_bias
    output = from_clips(result.astype(low))

    def to_core(total):
        kept = pick(core == 1, total[0], total[1])
        came = swap(pick(core == 1, total[1], total[0]), "core")
        return jnp.concatenate(
            [pick(core == 1, kept, came), pick(core == 1, came, kept)], axis=-1
        ).astype(jnp.float32)

    def dealt(*grads):
        return deal(place, [item.astype(low) for item in grads])

    def first_back(parts, wait):
        kept_even, sent_even, kept_odd, sent_odd = parts
        came = after((swap(sent_even, "y"), swap(sent_odd, "x")), wait)
        return kept_even + came[0], kept_odd + came[1]

    def second_back(even, odd, wait):
        came = after((swap(even[1], "x"), swap(odd[1], "y")), wait)
        return jnp.concatenate([even[0] + came[0], odd[0] + came[1]]), came

    def along_z_back(total, wait, later):
        cols = total.shape[1] // 4
        own, one, two, three = (total[:, at * cols : (at + 1) * cols] for at in range(4))
        one = swap(one, "tensor", 1)
        two = swap(two + after(swap(three, "tensor", 1), wait), "tensor", 2)
        one, two = after((one, two), later)
        return to_core((own + one + two).reshape(2, own_rows, cols))

    grad_top = grad_own.astype(jnp.float32)
    grad_all = both_halves(grad_own)
    sum_fc2_bias = jnp.sum(grad_top, axis=0)
    parts_fc2 = dealt(contract(grad_all, act, 0, 0))
    grad_act = jnp.dot(after(grad_all, parts_fc2), weight_down, preferred_element_type=jnp.float32)
    grad_hidden = (grad_act * slope.astype(jnp.float32)).astype(low)
    sum_fc1_bias = jnp.sum(grad_hidden, axis=0, dtype=jnp.float32)
    grad_second_part = contract(grad_hidden, weight_up, 1, 1)
    sent_fc2 = first_back(parts_fc2, grad_second_part)
    grad_second = part_sum(grad_second_part)
    second_pull = jax.vjp(norm_rows, resid, mlp_gain, mlp_shift)[1]
    grad_resid_norm, sum_mlp_gain, sum_mlp_shift = second_pull(grad_second)
    grad_resid = grad_top + grad_resid_norm
    sum_out_bias = jnp.sum(grad_resid, axis=0)
    resid_all = both_halves(grad_resid.astype(low))
    grad_fc1 = contract(after(second_all, sent_fc2[0]), grad_hidden, 0, 0)
    parts_up = dealt(contract(resid_all, heads_out, 0, 0), grad_fc1)
    grad_heads = jnp.dot(resid_all, weight_out, preferred_element_type=jnp.float32).astype(low)
    total_fc2, came_fc2 = second_back(*sent_fc2, grad_heads)
    grad_packed, sum_qkv_bias = attend_back(qkv, after(grad_heads, (parts_up, came_fc2)), turned, log_total, cosine, sine)
    sent_up = first_back(parts_up, grad_packed)
    parts_qkv = dealt(contract(after(first_all, sent_up), grad_packed, 0, 0))
    total_up, came_up = second_back(*sent_up, parts_qkv)
    grad_first_part = contract(after(grad_packed, came_up), weight_qkv, 1, 1)
    grad_first = part_sum(grad_first_part)
    first_pull = jax.vjp(norm_rows, tokens, attn_gain, attn_shift)[1]
    grad_input_norm, sum_attn_gain, sum_attn_shift = first_pull(grad_first)
    input_low = from_clips((grad_resid + grad_input_norm).astype(low))
    input_grad = input_low.astype(jnp.float32)

    grad_fc2_weight = along_z_back(total_fc2, grad_packed, parts_qkv)
    both_weights = along_z_back(total_up, grad_first, input_low)
    cuts = both_weights.shape[1] // 2
    both_weights = [both_weights[:, :cuts], both_weights[:, cuts:]]
    grad_out_weight = jnp.concatenate([item[:, :out_cols] for item in both_weights], axis=1)
    grad_fc1_weight = jnp.concatenate([item[:, out_cols:] for item in both_weights], axis=1)
    sent_qkv = first_back(parts_qkv, grad_first)
    total, came_qkv = second_back(*sent_qkv, grad_first)
    grad_qkv_weight = by_head(along_z_back(total, grad_first, grad_first))

    def by_core(values):
        none = jnp.zeros_like(values)
        return [pick(core == 1, values, none), pick(core == 1, none, values)]

    def by_owner(values, cols):
        first, second, third, fourth = (values.reshape(-1)[at * cols : (at + 1) * cols] for at in range(4))
        odd = at_z % 2 == 1
        first, second = pick(odd, first, second), pick(odd, second, first)
        third, fourth = pick(odd, third, fourth), pick(odd, fourth, third)
        lower, upper = jnp.concatenate([first, second]), jnp.concatenate([third, fourth])
        far = at_z // 2 == 1
        return jnp.concatenate([pick(far, lower, upper), pick(far, upper, lower)])

    sums = [sum_attn_gain, sum_attn_shift, sum_out_bias, sum_mlp_gain, sum_mlp_shift, sum_fc2_bias]
    sums = jnp.concatenate(sums + by_core(by_owner(sum_qkv_bias, qkv_cols)) + by_core(by_owner(sum_fc1_bias, unit_cols)))
    stages = (("core", 1, sent_qkv), ("x", 1, None), ("y", 1, (came_qkv, input_low)), ("tensor", 1, None), ("tensor", 2, None))
    for axis, bit, earlier in stages:
        if earlier is not None:
            sums = after(sums, earlier)
        sums = sums + swap(sums, axis, bit)
    vectors = sums[: 6 * width].reshape(6, width)
    qkv_sums = sums[6 * width : 6 * width + 8 * qkv_cols].reshape(2, 4, qkv_cols)
    unit_sums = sums[6 * width + 8 * qkv_cols :].reshape(2, 4, unit_cols)

    def own_place(values):
        return lax.dynamic_index_in_dim(values, at_z, 1, keepdims=False).reshape(-1)

    return (
        output,
        input_grad,
        vectors[0],
        vectors[1],
        grad_qkv_weight,
        by_head(own_place(qkv_sums)),
        grad_out_weight,
        vectors[2],
        vectors[3],
        vectors[4],
        grad_fc1_weight,
        own_place(unit_sums),
        grad_fc2_weight,
        vectors[5],
    )


def solution(mesh):
    if one_clip_per_chip(mesh):
        plan, rows = clip_body, ("y", "x", "core")
        mesh = jax.sharding.Mesh(mesh.devices.reshape(2, 2, 2, 4), EVERY)
    else:
        plan, rows = body, "dp"
    tokens, matrix, columns = P(rows, "tensor", None), P(rows, "tensor"), P("tensor")
    params = (P(), P(), matrix, columns, matrix, P(), P(), P(), matrix, columns, matrix, P())
    both = (tokens, tokens) + params
    return jax.shard_map(plan, mesh=mesh, in_specs=both, out_specs=both, check_vma=False)
```

```python
import math

import jax
import jax.numpy as jnp
from jax import lax
from jax.experimental import pallas as pl
from jax.experimental.pallas import tpu as pltpu
from jax.sharding import PartitionSpec as P

HD = 64
GRID = 16


def norm_rows(values, gain_vec, shift_vec):
    row_mean = jnp.mean(values, axis=-1, keepdims=True)
    centred = values - row_mean
    variance = jnp.mean(centred * centred, axis=-1, keepdims=True)
    return centred * lax.rsqrt(variance + 1e-06) * gain_vec + shift_vec


def rotary_tables(length):
    section = 2 * (HD // 3 // 2)
    half = section // 2
    position = jnp.arange(length)
    frame = (position // (GRID * GRID)).astype(jnp.float32)
    row_pos = (position // GRID % GRID).astype(jnp.float32)
    col_pos = (position % GRID).astype(jnp.float32)
    omega = 1.0 / 10000.0 ** (jnp.arange(half).astype(jnp.float32) / half)
    pieces = [
        jnp.repeat(coordinate[:, None] * omega[None, :], 2, axis=1)
        for coordinate in (frame, row_pos, col_pos)
    ]
    pieces.append(jnp.zeros((length, HD - 3 * section), jnp.float32))
    angles = jnp.concatenate(pieces, axis=1)
    parity = jnp.where(jnp.arange(HD) % 2 == 0, -1.0, 1.0).astype(jnp.float32)
    return (jnp.cos(angles), jnp.sin(angles) * parity)


def pair_swap(values):
    shape = values.shape
    paired = values.reshape(shape[:-1] + (shape[-1] // 2, 2))
    return paired[..., ::-1].reshape(shape)


def contract(left, right, left_dim, right_dim):
    return lax.dot_general(
        left, right, (((left_dim,), (right_dim,)), ((), ())), preferred_element_type=jnp.float32
    )


def exact_gelu(values):
    return jax.nn.gelu(values, approximate=False)


def body(
    activations,
    cotangent,
    attn_gain,
    attn_shift,
    qkv_weight,
    qkv_bias,
    out_weight,
    out_bias,
    mlp_gain,
    mlp_shift,
    fc1_weight,
    fc1_bias,
    fc2_weight,
    fc2_bias,
):
    tensor_size = lax.axis_size("tensor")
    tensor_rank = lax.axis_index("tensor")
    row_count = activations.shape[1]
    width = activations.shape[2]
    length = row_count * tensor_size
    block_rows = min(512, length)
    block_count = length // block_rows
    local_heads = qkv_weight.shape[1] // (3 * HD)
    packed_cols = qkv_weight.shape[1]
    unit_cols = fc1_weight.shape[1]
    factor = 1.0 / math.sqrt(HD)
    cosine, sine = rotary_tables(length)
    cosine = cosine[:, None, :]
    sine = sine[:, None, :]

    def rotate(values):
        return values * cosine + pair_swap(values) * sine

    def rotate_back(values):
        return values * cosine + pair_swap(values * sine)

    def fetch():
        gathered = (
            lax.all_gather(qkv_weight, "dp", axis=0, tiled=True),
            lax.all_gather(out_weight, "dp", axis=0, tiled=True),
            lax.all_gather(fc1_weight, "dp", axis=0, tiled=True),
            lax.all_gather(fc2_weight, "dp", axis=0, tiled=True),
        )
        return (gathered, gathered)

    def seq_gather(values):
        return lax.all_gather(values, "tensor", axis=0, tiled=True)

    def part_sum(values):
        return lax.psum_scatter(
            values.astype(jnp.bfloat16), "tensor", scatter_dimension=0, tiled=True
        ).astype(jnp.float32)

    def grad_gather(values):
        return lax.all_gather(values, "tensor", axis=0, tiled=True)

    def grad_sum(values):
        return lax.psum_scatter(
            values.astype(jnp.bfloat16), "tensor", scatter_dimension=0, tiled=True
        ).astype(jnp.float32)

    def forward(inputs, weights):
        (weight_qkv, weight_out, weight_up, weight_down), (
            whole_qkv,
            whole_out,
            whole_up,
            whole_down,
        ) = weights
        first_all = seq_gather(norm_rows(inputs, attn_gain, attn_shift).astype(jnp.bfloat16))
        packed = (
            jnp.dot(first_all, weight_qkv, preferred_element_type=jnp.float32) + qkv_bias
        ).reshape(length, local_heads, 3, HD)
        query = rotate(packed[:, :, 0]).astype(jnp.bfloat16)
        key_all = rotate(packed[:, :, 1]).astype(jnp.bfloat16)
        value_all = packed[:, :, 2].astype(jnp.bfloat16)
        outputs = []
        log_sums = []
        for block in range(block_count):
            query_block = query[block * block_rows : (block + 1) * block_rows]
            scores = (
                jnp.einsum("qhd,khd->hqk", query_block, key_all, preferred_element_type=jnp.float32)
                * factor
            )
            row_max = jnp.max(scores, axis=-1, keepdims=True)
            expo = jnp.exp(scores - row_max)
            row_total = jnp.sum(expo, axis=-1, keepdims=True)
            weights_low = (expo / row_total).astype(jnp.bfloat16)
            outputs.append(
                jnp.einsum(
                    "hqk,khd->qhd", weights_low, value_all, preferred_element_type=jnp.float32
                )
            )
            log_sums.append(row_max + jnp.log(row_total))
        heads_out = (
            jnp.concatenate(outputs, axis=0).reshape(length, local_heads * HD).astype(jnp.bfloat16)
        )
        log_total = jnp.concatenate(log_sums, axis=1)
        attended = part_sum(contract(heads_out, weight_out, 1, 1))
        resid = inputs + attended + out_bias
        second_all = seq_gather(norm_rows(resid, mlp_gain, mlp_shift).astype(jnp.bfloat16))
        hidden = jnp.dot(second_all, weight_up, preferred_element_type=jnp.float32) + fc1_bias
        act = exact_gelu(hidden).astype(jnp.bfloat16)
        branch = part_sum(contract(act, weight_down, 1, 1))
        result = resid + branch + fc2_bias
        kept = (
            first_all,
            query,
            key_all,
            value_all,
            log_total,
            heads_out,
            heads_out,
            resid,
            second_all,
            hidden,
            act,
        )
        return (result, kept)

    def backward(inputs, grad_low, kept, weights):
        (weight_qkv, weight_out, weight_up, weight_down), (
            whole_qkv,
            whole_out,
            whole_up,
            whole_down,
        ) = weights
        (
            first_all,
            query,
            key_all,
            value_all,
            log_total,
            heads_out,
            heads_rows,
            resid,
            second_all,
            hidden,
            act,
        ) = kept
        grad_top = grad_low.astype(jnp.float32)
        grad_fc2_bias = jnp.sum(grad_top, axis=0)
        grad_all = grad_gather(grad_low)
        grad_fc2_weight = contract(grad_all, act, 0, 0)
        grad_act = jnp.dot(grad_all, weight_down, preferred_element_type=jnp.float32)
        gelu_pull = jax.vjp(exact_gelu, hidden)[1]
        grad_hidden = gelu_pull(grad_act)[0].astype(jnp.bfloat16)
        grad_fc1_bias = jnp.sum(grad_hidden, axis=0, dtype=jnp.float32)
        grad_fc1_weight = contract(second_all, grad_hidden, 0, 0)
        grad_second = grad_sum(contract(grad_hidden, weight_up, 1, 1))
        second_pull = jax.vjp(norm_rows, resid, mlp_gain, mlp_shift)[1]
        grad_resid_norm, grad_mlp_gain, grad_mlp_shift = second_pull(grad_second)
        grad_resid = grad_top + grad_resid_norm
        grad_out_bias = jnp.sum(grad_resid, axis=0)
        resid_low = grad_resid.astype(jnp.bfloat16)
        resid_all = grad_gather(resid_low)
        grad_out_weight = contract(resid_all, heads_out, 0, 0)
        grad_heads = jnp.dot(resid_all, weight_out, preferred_element_type=jnp.float32).astype(
            jnp.bfloat16
        )
        grad_heads = grad_heads.reshape(length, local_heads, HD)
        grad_key = jnp.zeros((length, local_heads, HD), jnp.float32)
        grad_value = jnp.zeros((length, local_heads, HD), jnp.float32)
        query_grads = []
        for block in range(block_count):
            lower = block * block_rows
            upper = lower + block_rows
            query_block = query[lower:upper]
            grad_block = grad_heads[lower:upper]
            scores = (
                jnp.einsum("qhd,khd->hqk", query_block, key_all, preferred_element_type=jnp.float32)
                * factor
            )
            probs = jnp.exp(scores - log_total[:, lower:upper])
            grad_value = grad_value + jnp.einsum(
                "hqk,qhd->khd",
                probs.astype(jnp.bfloat16),
                grad_block,
                preferred_element_type=jnp.float32,
            )
            grad_probs = jnp.einsum(
                "qhd,khd->hqk", grad_block, value_all, preferred_element_type=jnp.float32
            )
            grad_scores = (
                probs * (grad_probs - jnp.sum(probs * grad_probs, axis=-1, keepdims=True))
            ).astype(jnp.bfloat16)
            query_grads.append(
                jnp.einsum("hqk,khd->qhd", grad_scores, key_all, preferred_element_type=jnp.float32)
                * factor
            )
            grad_key = (
                grad_key
                + jnp.einsum(
                    "hqk,qhd->khd", grad_scores, query_block, preferred_element_type=jnp.float32
                )
                * factor
            )
        grad_query = jnp.concatenate(query_grads, axis=0)
        grad_packed = jnp.stack(
            [rotate_back(grad_query), rotate_back(grad_key), grad_value], axis=2
        )
        grad_packed = grad_packed.reshape(length, packed_cols).astype(jnp.bfloat16)
        grad_qkv_bias = jnp.sum(grad_packed, axis=0, dtype=jnp.float32)
        grad_qkv_weight = contract(first_all, grad_packed, 0, 0)
        grad_first = grad_sum(contract(grad_packed, weight_qkv, 1, 1))
        first_pull = jax.vjp(norm_rows, inputs, attn_gain, attn_shift)[1]
        grad_input_norm, grad_attn_gain, grad_attn_shift = first_pull(grad_first)
        input_grad = grad_resid + grad_input_norm
        grads = (
            grad_attn_gain,
            grad_attn_shift,
            grad_qkv_weight,
            grad_qkv_bias,
            grad_out_weight,
            grad_out_bias,
            grad_mlp_gain,
            grad_mlp_shift,
            grad_fc1_weight,
            grad_fc1_bias,
            grad_fc2_weight,
            grad_fc2_bias,
        )
        return (input_grad, grads)

    def per_clip(totals, inputs_pair):
        clip_in, clip_grad = inputs_pair
        forward_weights = fetch()
        result, kept = forward(clip_in.astype(jnp.float32), forward_weights)
        backward_weights = fetch()
        input_grad, grads = backward(clip_in.astype(jnp.float32), clip_grad, kept, backward_weights)
        totals = tuple((left + right for left, right in zip(totals, grads)))
        return (totals, (result.astype(jnp.bfloat16), input_grad))

    out_cols = local_heads * HD
    start_totals = (
        jnp.zeros((width,), jnp.float32),
        jnp.zeros((width,), jnp.float32),
        jnp.zeros((width, packed_cols), jnp.float32),
        jnp.zeros((packed_cols,), jnp.float32),
        jnp.zeros((width, out_cols), jnp.float32),
        jnp.zeros((width,), jnp.float32),
        jnp.zeros((width,), jnp.float32),
        jnp.zeros((width,), jnp.float32),
        jnp.zeros((width, unit_cols), jnp.float32),
        jnp.zeros((unit_cols,), jnp.float32),
        jnp.zeros((width, unit_cols), jnp.float32),
        jnp.zeros((width,), jnp.float32),
    )
    totals, (output, input_grad) = lax.scan(per_clip, start_totals, (activations, cotangent))
    out_grad = totals[4]
    weight_sums = (
        lax.psum_scatter(
            totals[2].astype(jnp.bfloat16), "dp", scatter_dimension=0, tiled=True
        ).astype(jnp.float32),
        lax.psum_scatter(
            out_grad.astype(jnp.bfloat16), "dp", scatter_dimension=0, tiled=True
        ).astype(jnp.float32),
        lax.psum_scatter(
            totals[8].astype(jnp.bfloat16), "dp", scatter_dimension=0, tiled=True
        ).astype(jnp.float32),
        lax.psum_scatter(
            totals[10].astype(jnp.bfloat16), "dp", scatter_dimension=0, tiled=True
        ).astype(jnp.float32),
    )
    qkv_place = lax.dynamic_update_slice_in_dim(
        jnp.zeros((packed_cols * tensor_size,), jnp.float32),
        totals[3],
        tensor_rank * packed_cols,
        0,
    )
    unit_place = lax.dynamic_update_slice_in_dim(
        jnp.zeros((unit_cols * tensor_size,), jnp.float32), totals[9], tensor_rank * unit_cols, 0
    )
    summed = lax.psum(
        (totals[0], totals[1], qkv_place, totals[5], totals[6], totals[7], unit_place, totals[11]),
        ("dp", "tensor"),
    )
    grad_qkv_bias = lax.dynamic_slice_in_dim(summed[2], tensor_rank * packed_cols, packed_cols, 0)
    grad_fc1_bias = lax.dynamic_slice_in_dim(summed[6], tensor_rank * unit_cols, unit_cols, 0)
    return (
        output,
        input_grad,
        summed[0],
        summed[1],
        weight_sums[0],
        grad_qkv_bias,
        weight_sums[1],
        summed[3],
        summed[4],
        summed[5],
        weight_sums[2],
        grad_fc1_bias,
        weight_sums[3],
        summed[7],
    )


def lane_swap(values):
    even = lax.broadcasted_iota(jnp.int32, values.shape, 1) % 2 == 0
    return jnp.where(even, pltpu.roll(values, 127, 1), pltpu.roll(values, 1, 1))


def attend_kernel(first_ref, weight_ref, bias_ref, cos_ref, sin_ref, qkv_ref, heads_ref, turned_ref, log_ref):
    low = jnp.bfloat16
    packed = jnp.dot(first_ref[...], weight_ref[...], preferred_element_type=jnp.float32) + bias_ref[...]
    cosine, sine = cos_ref[...], sin_ref[...]

    def rotate(values):
        return values * cosine + lane_swap(values) * sine

    query = (rotate(packed[:, :128]).astype(low).astype(jnp.float32) * 0.125).astype(low)
    key = rotate(packed[:, 128:256]).astype(low)
    value = packed[:, 256:]
    qkv_ref[:, :128] = query
    qkv_ref[:, 128:256] = key
    qkv_ref[:, 256:] = value.astype(low)
    value = jnp.transpose(value).astype(low)
    first_head = lax.broadcasted_iota(jnp.int32, key.shape, 1) < HD
    for head in range(2):
        mine = slice(head * HD, (head + 1) * HD)
        key_here = jnp.where(first_head == (head == 0), key, jnp.zeros_like(key))
        scores = contract(key_here, query, 1, 1)
        top = jnp.max(scores, axis=0, keepdims=True)
        expo = jnp.exp(scores - top)
        total = jnp.sum(expo, axis=0, keepdims=True)
        summed = jnp.dot(value[mine], expo.astype(low), preferred_element_type=jnp.float32)
        turned_ref[0, mine] = summed / total
        log_ref[0, head : head + 1] = top + jnp.log(total)
    heads_ref[...] = jnp.transpose(turned_ref[0]).astype(low)


def attend(first, weight, bias, cosine, sine):
    length, width = first.shape
    pairs = weight.shape[1] // 384
    return pl.pallas_call(
        attend_kernel,
        grid=(pairs,),
        in_specs=[
            pl.BlockSpec((length, width), lambda i: (0, 0)),
            pl.BlockSpec((width, 384), lambda i: (0, i)),
            pl.BlockSpec((1, 384), lambda i: (0, i)),
            pl.BlockSpec((length, 128), lambda i: (0, 0)),
            pl.BlockSpec((length, 128), lambda i: (0, 0)),
        ],
        out_specs=[
            pl.BlockSpec((length, 384), lambda i: (0, i)),
            pl.BlockSpec((length, 128), lambda i: (0, i)),
            pl.BlockSpec((1, 128, length), lambda i: (i, 0, 0)),
            pl.BlockSpec((1, 2, length), lambda i: (i, 0, 0)),
        ],
        out_shape=[
            jax.ShapeDtypeStruct((length, 384 * pairs), jnp.bfloat16),
            jax.ShapeDtypeStruct((length, 128 * pairs), jnp.bfloat16),
            jax.ShapeDtypeStruct((pairs, 128, length), jnp.float32),
            jax.ShapeDtypeStruct((pairs, 2, length), jnp.float32),
        ],
        cost_estimate=pl.CostEstimate(flops=2 * 10**10, transcendentals=0, bytes_accessed=16 * 2**20),
        name="attend",
    )(first, weight, bias.reshape(1, -1), cosine, sine)


def attend_back_kernel(qkv_ref, grad_ref, turned_ref, log_ref, cos_ref, sin_ref, out_ref, bias_ref):
    low = jnp.bfloat16
    query = qkv_ref[:, :128]
    key = qkv_ref[:, 128:256]
    value = qkv_ref[:, 256:]
    grad = grad_ref[...]
    key_turned = jnp.transpose(key.astype(jnp.float32)).astype(low)
    product = jnp.transpose(grad.astype(jnp.float32)) * turned_ref[0]
    first_head = lax.broadcasted_iota(jnp.int32, key.shape, 1) < HD
    zero = jnp.zeros_like(key)
    query_grads, key_grads, value_grads = [], [], []
    for head in range(2):
        mine = slice(head * HD, (head + 1) * HD)
        here = first_head == (head == 0)
        delta = jnp.sum(product[mine], axis=0, keepdims=True)
        scores = contract(jnp.where(here, key, zero), query, 1, 1)
        probs = jnp.exp(scores - log_ref[0, head : head + 1])
        grad_probs = contract(jnp.where(here, value, zero), grad, 1, 1)
        grad_scores = (probs * (grad_probs - delta)).astype(low)
        value_grads.append(jnp.dot(probs.astype(low), grad, preferred_element_type=jnp.float32))
        key_grads.append(jnp.dot(grad_scores, query, preferred_element_type=jnp.float32))
        query_grads.append(jnp.dot(key_turned[mine], grad_scores, preferred_element_type=jnp.float32))
    cosine, sine = cos_ref[...], sin_ref[...]

    def rotate_back(values):
        return values * cosine + lane_swap(values * sine)

    parts = [
        rotate_back(jnp.transpose(jnp.concatenate(query_grads, axis=0)) * 0.125),
        rotate_back(jnp.where(first_head, key_grads[0], key_grads[1])),
        jnp.where(first_head, value_grads[0], value_grads[1]),
    ]
    for at, part in enumerate(parts):
        part = part.astype(low)
        out_ref[:, at * 128 : (at + 1) * 128] = part
        bias_ref[:, at * 128 : (at + 1) * 128] = jnp.sum(part.astype(jnp.float32), axis=0, keepdims=True)


def attend_back(qkv, grad, turned, logs, cosine, sine):
    length = qkv.shape[0]
    pairs = qkv.shape[1] // 384
    return pl.pallas_call(
        attend_back_kernel,
        grid=(pairs,),
        in_specs=[
            pl.BlockSpec((length, 384), lambda i: (0, i)),
            pl.BlockSpec((length, 128), lambda i: (0, i)),
            pl.BlockSpec((1, 128, length), lambda i: (i, 0, 0)),
            pl.BlockSpec((1, 2, length), lambda i: (i, 0, 0)),
            pl.BlockSpec((length, 128), lambda i: (0, 0)),
            pl.BlockSpec((length, 128), lambda i: (0, 0)),
        ],
        out_specs=[
            pl.BlockSpec((length, 384), lambda i: (0, i)),
            pl.BlockSpec((1, 384), lambda i: (0, i)),
        ],
        out_shape=[
            jax.ShapeDtypeStruct((length, 384 * pairs), jnp.bfloat16),
            jax.ShapeDtypeStruct((1, 384 * pairs), jnp.float32),
        ],
        cost_estimate=pl.CostEstimate(flops=27 * 10**9, transcendentals=0, bytes_accessed=16 * 2**20),
        name="attend_back",
    )(qkv, grad, turned, logs, cosine, sine)


def assemble_kernel(place_ref, own_ref, x_ref, y_ref, even_ref, odd_ref, *out_refs):
    rows = even_ref.shape[0]
    start = 0
    for out_ref in out_refs:
        cols = slice(start, start + out_ref.shape[1])
        start += out_ref.shape[1]
        for at, ref in enumerate((own_ref, x_ref, y_ref)):
            out_ref[pl.ds(pl.multiple_of((at ^ place_ref[0]) * 2 * rows, 2 * rows), 2 * rows)] = ref[:, cols]
        last = (3 ^ place_ref[0]) * 2 * rows
        out_ref[pl.ds(pl.multiple_of(last, rows), rows)] = even_ref[:, cols]
        out_ref[pl.ds(pl.multiple_of(last + rows, rows), rows)] = odd_ref[:, cols]


def assemble(place, pieces, widths):
    rows = pieces[3].shape[0]
    total = sum(widths)
    return pl.pallas_call(
        assemble_kernel,
        grid_spec=pltpu.PrefetchScalarGridSpec(
            num_scalar_prefetch=1,
            grid=(4,),
            in_specs=[pl.BlockSpec((item.shape[0], total), lambda i, place: (0, i)) for item in pieces],
            out_specs=[pl.BlockSpec((8 * rows, cols), lambda i, place: (0, i)) for cols in widths],
        ),
        out_shape=[jax.ShapeDtypeStruct((8 * rows, 4 * cols), jnp.bfloat16) for cols in widths],
        cost_estimate=pl.CostEstimate(flops=0, transcendentals=0, bytes_accessed=16 * 2**20),
        name="assemble",
    )(place, *pieces)


def deal_kernel(place_ref, *refs):
    in_refs, out_refs = refs[:-4], refs[-4:]
    rows = out_refs[0].shape[1]
    start = 0
    for ref in in_refs:
        cols = slice(start, start + ref.shape[1])
        start += ref.shape[1]
        for half, kept_ref, sent_ref, bit in ((0, out_refs[0], out_refs[1], 2), (1, out_refs[2], out_refs[3], 1)):
            for out_ref, from_bit in ((kept_ref, 0), (sent_ref, bit)):
                for at in range(2):
                    block = (at * (3 - bit) + from_bit) ^ place_ref[0]
                    first_row = pl.multiple_of((2 * block + half) * rows, rows)
                    out_ref[at, :, cols] = ref[pl.ds(first_row, rows)]


def deal(place, grads):
    rows = grads[0].shape[0] // 8
    widths = [item.shape[1] // 4 for item in grads]
    total = sum(widths)
    return pl.pallas_call(
        deal_kernel,
        grid_spec=pltpu.PrefetchScalarGridSpec(
            num_scalar_prefetch=1,
            grid=(4,),
            in_specs=[pl.BlockSpec((8 * rows, cols), lambda i, place: (0, i)) for cols in widths],
            out_specs=[pl.BlockSpec((2, rows, total), lambda i, place: (0, 0, i))] * 4,
        ),
        out_shape=[jax.ShapeDtypeStruct((2, rows, 4 * total), jnp.bfloat16)] * 4,
        cost_estimate=pl.CostEstimate(flops=0, transcendentals=0, bytes_accessed=16 * 2**20),
        name="deal",
    )(place, *grads)


def after(values, earlier):
    return lax.optimization_barrier((values, earlier))[0]


EVERY = ("y", "x", "core", "tensor")


def one_clip_per_chip(mesh):
    return mesh.shape["dp"] == 8 and mesh.shape["tensor"] == 4


def swap(values, axis, bit=1):
    return lax.ppermute(values, axis, [(i, i ^ bit) for i in range(4 if axis == "tensor" else 2)])


def clip_routes(back):
    routes = []
    for turn in range(2):
        pairs = []
        for column in range(4):
            for core in range(2):
                for place in range(4):
                    source = (2 * column + core) * 4 + place
                    target = (2 * column + place // 2) * 4 + 2 * core + (turn ^ (place % 2))
                    pairs.append((target, source) if back else (source, target))
        routes.append(pairs)
    return routes


def pick(flag, first, second):
    return jnp.where(flag, second, first)


def to_clips(values):
    odd = lax.axis_index("tensor") % 2 == 1
    arrived = []
    for turn, pairs in enumerate(clip_routes(False)):
        sent = pick(odd, values[turn], values[1 - turn])
        arrived.append(lax.ppermute(sent, EVERY, pairs))
    return arrived, jnp.concatenate(
        [pick(odd, arrived[0], arrived[1]), pick(odd, arrived[1], arrived[0])], axis=0
    )


def from_clips(values, wait=None):
    odd = lax.axis_index("tensor") % 2 == 1
    rows = values.shape[0] // 2
    arrived = []
    for turn, pairs in enumerate(clip_routes(True)):
        sent = pick(odd, values[turn * rows : (turn + 1) * rows], values[(1 - turn) * rows : (2 - turn) * rows])
        arrived.append(lax.ppermute(sent, EVERY, pairs))
    if wait is not None:
        arrived = after(arrived, wait)
    return jnp.stack([pick(odd, arrived[0], arrived[1]), pick(odd, arrived[1], arrived[0])])


def three_parts(values):
    high = lax.reduce_precision(values, 8, 7)
    rest = values - high
    middle = lax.reduce_precision(rest, 8, 7)
    low = rest - middle
    return jnp.stack([high, middle, low]).astype(jnp.bfloat16)


def clip_body(
    activations,
    cotangent,
    attn_gain,
    attn_shift,
    qkv_weight,
    qkv_bias,
    out_weight,
    out_bias,
    mlp_gain,
    mlp_shift,
    fc1_weight,
    fc1_bias,
    fc2_weight,
    fc2_bias,
):
    core, at_x, at_y, at_z = (lax.axis_index(name) for name in ("core", "x", "y", "tensor"))
    place = (2 * at_y + at_x).astype(jnp.int32).reshape(1)
    width = activations.shape[2]
    length = activations.shape[1] * 4
    half_rows = length // 2
    own_rows = qkv_weight.shape[0]
    half_heads = qkv_weight.shape[1] // (6 * HD)
    qkv_cols = half_heads * 3 * HD
    out_cols = out_weight.shape[1] // 2
    unit_cols = fc1_weight.shape[1] // 2
    low = jnp.bfloat16

    def first_half(values):
        return lax.slice_in_dim(values, 0, values.shape[-1] // 2, axis=values.ndim - 1)

    def second_half(values):
        return lax.slice_in_dim(values, values.shape[-1] // 2, values.shape[-1], axis=values.ndim - 1)

    def own_half(values):
        return pick(core == 1, first_half(values), second_half(values))

    def other_half(values):
        return pick(core == 1, second_half(values), first_half(values))

    def by_kind(values):
        lead = values.shape[:-1]
        split = values.reshape(lead + (2, half_heads, 3, HD))
        return jnp.swapaxes(split, -3, -2).reshape(values.shape)

    def by_head(values):
        lead = values.shape[:-1]
        split = values.reshape(lead + (2, 3, half_heads, HD))
        return jnp.swapaxes(split, -3, -2).reshape(values.shape)

    columns = (by_kind(qkv_weight), out_weight, fc1_weight, fc2_weight)
    mine = jnp.concatenate([own_half(item) for item in columns], axis=1)
    theirs = swap(jnp.concatenate([other_half(item) for item in columns], axis=1), "core")
    held = jnp.concatenate([pick(core == 1, mine, theirs), pick(core == 1, theirs, mine)], axis=0)

    def along_z(own, wait=None):
        one = swap(own, "tensor", 1)
        two = swap(own, "tensor", 2)
        two = two if wait is None else after(two, wait)
        return [own, one, two, swap(two, "tensor", 1)]

    def over_plane(blocks, wait=None):
        own = jnp.concatenate(blocks, axis=1)
        from_x, from_y = swap(own, "x"), swap(own, "y")
        if wait is not None:
            from_x, from_y = after((from_x, from_y), wait)
        return own, from_x, from_y, swap(from_y[:own_rows], "x"), swap(from_x[own_rows:], "y")

    lines = jnp.concatenate([own_half(by_kind(qkv_bias)), own_half(fc1_bias)])
    lines = jnp.pad(three_parts(lines), ((0, 0), (0, 3 * qkv_cols - lines.shape[0]))).reshape(9, qkv_cols)
    blocks = along_z(jnp.concatenate([held[:, :qkv_cols], lines, jnp.zeros((7, qkv_cols), low)], axis=0))
    tokens = to_clips(after(activations, (blocks[1], blocks[3])))[1].astype(jnp.float32)
    lines = jnp.stack([item[2 * own_rows : 2 * own_rows + 9] for item in blocks])
    lines = lines.astype(jnp.float32).reshape(4, 3, 3 * qkv_cols).sum(axis=1)
    bias_qkv = lines[:, :qkv_cols].reshape(-1)
    bias_up = lines[:, qkv_cols : qkv_cols + unit_cols].reshape(-1)
    blocks_up = along_z(after(held[:, qkv_cols : qkv_cols + out_cols + unit_cols], blocks[3]))
    pieces = over_plane([item[: 2 * own_rows] for item in blocks], blocks_up[1:3])
    (weight_qkv,) = assemble(place, pieces, [qkv_cols])
    blocks_down = along_z(after(held[:, qkv_cols + out_cols + unit_cols :], blocks_up[3]))
    weight_qkv = after(weight_qkv, blocks_down[1:3])

    def both_halves(values):
        other = swap(values, "core")
        return jnp.concatenate([pick(core == 1, values, other), pick(core == 1, other, values)], axis=0)

    def part_sum(values):
        halves = values.reshape((2, half_rows) + values.shape[1:])
        sent = pick(core == 1, halves[1], halves[0]).astype(low)
        return pick(core == 1, halves[0], halves[1]) + swap(sent, "core").astype(jnp.float32)

    cosine, sine = (jnp.concatenate([item, item], axis=1) for item in rotary_tables(length))

    first_all = both_halves(norm_rows(tokens, attn_gain, attn_shift).astype(low))
    qkv, heads_out, turned, log_total = attend(first_all, weight_qkv, bias_qkv, cosine, sine)

    blocks_up[0] = after(blocks_up[0], pieces[3:])
    pieces = over_plane(blocks_up, heads_out)
    pieces = pieces[:3] + after(pieces[3:], blocks_down[3])
    weight_out, weight_up = assemble(place, pieces, [out_cols, unit_cols])
    resid = tokens + part_sum(contract(heads_out, weight_out, 1, 1)) + out_bias
    second_all = both_halves(norm_rows(resid, mlp_gain, mlp_shift).astype(low))

    blocks_down[0] = after(blocks_down[0], pieces[3:])
    arrived, grad_own = to_clips(after(cotangent, blocks_down[3]))
    pieces = over_plane(blocks_down, second_all)

    second_all = after(second_all, (pieces[1:3], arrived))
    hidden = jnp.dot(second_all, weight_up, preferred_element_type=jnp.float32) + bias_up
    share = 0.5 + 0.5 * lax.erf(hidden * math.sqrt(0.5))
    act = (hidden * share).astype(low)
    slope = (share + hidden * jnp.exp(-0.5 * hidden * hidden) * (1.0 / math.sqrt(2.0 * math.pi))).astype(low)
    pieces = pieces[:3] + after(pieces[3:], act)
    (weight_down,) = assemble(place, pieces, [unit_cols])
    result = resid + part_sum(contract(act, weight_down, 1, 1)) + fc2_bias

    def to_core(total):
        kept = pick(core == 1, total[0], total[1])
        came = swap(pick(core == 1, total[1], total[0]), "core")
        return jnp.concatenate(
            [pick(core == 1, kept, came), pick(core == 1, came, kept)], axis=-1
        ).astype(jnp.float32)

    def dealt(*grads):
        return deal(place, [item.astype(low) for item in grads])

    def first_back(parts, wait):
        kept_even, sent_even, kept_odd, sent_odd = parts
        came = after((swap(sent_even, "y"), swap(sent_odd, "x")), wait)
        return kept_even + came[0], kept_odd + came[1]

    def second_back(even, odd, wait):
        came = after((swap(even[1], "x"), swap(odd[1], "y")), wait)
        return jnp.concatenate([even[0] + came[0], odd[0] + came[1]]), came

    def along_z_back(total, wait, later):
        cols = total.shape[1] // 4
        own, one, two, three = (total[:, at * cols : (at + 1) * cols] for at in range(4))
        one = swap(one, "tensor", 1)
        two = swap(two + after(swap(three, "tensor", 1), wait), "tensor", 2)
        one, two = after((one, two), later)
        return to_core((own + one + two).reshape(2, own_rows, cols))

    grad_top = grad_own.astype(jnp.float32)
    grad_all = both_halves(grad_own)
    sum_fc2_bias = jnp.sum(grad_top, axis=0)
    parts_fc2 = dealt(contract(grad_all, act, 0, 0))
    grad_act = jnp.dot(after(grad_all, parts_fc2), weight_down, preferred_element_type=jnp.float32)
    grad_hidden = (grad_act * slope.astype(jnp.float32)).astype(low)
    sum_fc1_bias = jnp.sum(grad_hidden, axis=0, dtype=jnp.float32)
    grad_second_part = contract(grad_hidden, weight_up, 1, 1)
    sent_fc2 = first_back(parts_fc2, grad_second_part)
    grad_second = part_sum(grad_second_part)
    second_pull = jax.vjp(norm_rows, resid, mlp_gain, mlp_shift)[1]
    grad_resid_norm, sum_mlp_gain, sum_mlp_shift = second_pull(grad_second)
    grad_resid = grad_top + grad_resid_norm
    sum_out_bias = jnp.sum(grad_resid, axis=0)
    resid_all = both_halves(grad_resid.astype(low))
    grad_fc1 = contract(after(second_all, sent_fc2[0]), grad_hidden, 0, 0)
    parts_up = dealt(contract(resid_all, heads_out, 0, 0), grad_fc1)
    grad_heads = jnp.dot(resid_all, weight_out, preferred_element_type=jnp.float32).astype(low)
    total_fc2, came_fc2 = second_back(*sent_fc2, grad_heads)
    grad_packed, sum_qkv_bias = attend_back(qkv, after(grad_heads, (parts_up, came_fc2)), turned, log_total, cosine, sine)
    output = from_clips(result.astype(low), grad_packed)
    sent_up = first_back(parts_up, grad_packed)
    parts_qkv = dealt(contract(after(first_all, sent_up), grad_packed, 0, 0))
    total_up, came_up = second_back(*sent_up, parts_qkv)
    grad_first_part = contract(after(grad_packed, came_up), weight_qkv, 1, 1)
    grad_first = part_sum(grad_first_part)
    first_pull = jax.vjp(norm_rows, tokens, attn_gain, attn_shift)[1]
    grad_input_norm, sum_attn_gain, sum_attn_shift = first_pull(grad_first)
    input_low = from_clips((grad_resid + grad_input_norm).astype(low))
    input_grad = input_low.astype(jnp.float32)

    grad_fc2_weight = along_z_back(total_fc2, parts_qkv, grad_first)
    both_weights = along_z_back(total_up, grad_first, input_low)
    cuts = both_weights.shape[1] // 2
    both_weights = [both_weights[:, :cuts], both_weights[:, cuts:]]
    grad_out_weight = jnp.concatenate([item[:, :out_cols] for item in both_weights], axis=1)
    grad_fc1_weight = jnp.concatenate([item[:, out_cols:] for item in both_weights], axis=1)
    sent_qkv = first_back(parts_qkv, grad_first)
    total, came_qkv = second_back(*sent_qkv, grad_first)
    grad_qkv_weight = by_head(along_z_back(total, grad_first, grad_first))

    def by_core(values):
        none = jnp.zeros_like(values)
        return [pick(core == 1, values, none), pick(core == 1, none, values)]

    def by_owner(values, cols):
        first, second, third, fourth = (values.reshape(-1)[at * cols : (at + 1) * cols] for at in range(4))
        odd = at_z % 2 == 1
        first, second = pick(odd, first, second), pick(odd, second, first)
        third, fourth = pick(odd, third, fourth), pick(odd, fourth, third)
        lower, upper = jnp.concatenate([first, second]), jnp.concatenate([third, fourth])
        far = at_z // 2 == 1
        return jnp.concatenate([pick(far, lower, upper), pick(far, upper, lower)])

    sums = [sum_attn_gain, sum_attn_shift, sum_out_bias, sum_mlp_gain, sum_mlp_shift, sum_fc2_bias]
    sums = jnp.concatenate(sums + by_core(by_owner(sum_qkv_bias, qkv_cols)) + by_core(by_owner(sum_fc1_bias, unit_cols)))
    stages = (("core", 1, sent_qkv), ("x", 1, None), ("y", 1, (came_qkv, input_low)), ("tensor", 1, None), ("tensor", 2, None))
    for axis, bit, earlier in stages:
        if earlier is not None:
            sums = after(sums, earlier)
        sums = sums + swap(sums, axis, bit)
    vectors = sums[: 6 * width].reshape(6, width)
    qkv_sums = sums[6 * width : 6 * width + 8 * qkv_cols].reshape(2, 4, qkv_cols)
    unit_sums = sums[6 * width + 8 * qkv_cols :].reshape(2, 4, unit_cols)

    def own_place(values):
        return lax.dynamic_index_in_dim(values, at_z, 1, keepdims=False).reshape(-1)

    return (
        output,
        input_grad,
        vectors[0],
        vectors[1],
        grad_qkv_weight,
        by_head(own_place(qkv_sums)),
        grad_out_weight,
        vectors[2],
        vectors[3],
        vectors[4],
        grad_fc1_weight,
        own_place(unit_sums),
        grad_fc2_weight,
        vectors[5],
    )


def solution(mesh):
    if one_clip_per_chip(mesh):
        plan, rows = clip_body, ("y", "x", "core")
        mesh = jax.sharding.Mesh(mesh.devices.reshape(2, 2, 2, 4), EVERY)
    else:
        plan, rows = body, "dp"
    tokens, matrix, columns = P(rows, "tensor", None), P(rows, "tensor"), P("tensor")
    params = (P(), P(), matrix, columns, matrix, P(), P(), P(), matrix, columns, matrix, P())
    both = (tokens, tokens) + params
    return jax.shard_map(plan, mesh=mesh, in_specs=both, out_specs=both, check_vma=False)
```

```python
import math

import jax
import jax.numpy as jnp
from jax import lax
from jax.experimental import pallas as pl
from jax.experimental.pallas import tpu as pltpu
from jax.sharding import PartitionSpec as P

HD = 64
GRID = 16


def norm_rows(values, gain_vec, shift_vec):
    row_mean = jnp.mean(values, axis=-1, keepdims=True)
    centred = values - row_mean
    variance = jnp.mean(centred * centred, axis=-1, keepdims=True)
    return centred * lax.rsqrt(variance + 1e-06) * gain_vec + shift_vec


def rotary_tables(length):
    section = 2 * (HD // 3 // 2)
    half = section // 2
    position = jnp.arange(length)
    frame = (position // (GRID * GRID)).astype(jnp.float32)
    row_pos = (position // GRID % GRID).astype(jnp.float32)
    col_pos = (position % GRID).astype(jnp.float32)
    omega = 1.0 / 10000.0 ** (jnp.arange(half).astype(jnp.float32) / half)
    pieces = [
        jnp.repeat(coordinate[:, None] * omega[None, :], 2, axis=1)
        for coordinate in (frame, row_pos, col_pos)
    ]
    pieces.append(jnp.zeros((length, HD - 3 * section), jnp.float32))
    angles = jnp.concatenate(pieces, axis=1)
    parity = jnp.where(jnp.arange(HD) % 2 == 0, -1.0, 1.0).astype(jnp.float32)
    return (jnp.cos(angles), jnp.sin(angles) * parity)


def pair_swap(values):
    shape = values.shape
    paired = values.reshape(shape[:-1] + (shape[-1] // 2, 2))
    return paired[..., ::-1].reshape(shape)


def contract(left, right, left_dim, right_dim):
    return lax.dot_general(
        left, right, (((left_dim,), (right_dim,)), ((), ())), preferred_element_type=jnp.float32
    )


def exact_gelu(values):
    return jax.nn.gelu(values, approximate=False)


def body(
    activations,
    cotangent,
    attn_gain,
    attn_shift,
    qkv_weight,
    qkv_bias,
    out_weight,
    out_bias,
    mlp_gain,
    mlp_shift,
    fc1_weight,
    fc1_bias,
    fc2_weight,
    fc2_bias,
):
    tensor_size = lax.axis_size("tensor")
    tensor_rank = lax.axis_index("tensor")
    row_count = activations.shape[1]
    width = activations.shape[2]
    length = row_count * tensor_size
    block_rows = min(512, length)
    block_count = length // block_rows
    local_heads = qkv_weight.shape[1] // (3 * HD)
    packed_cols = qkv_weight.shape[1]
    unit_cols = fc1_weight.shape[1]
    factor = 1.0 / math.sqrt(HD)
    cosine, sine = rotary_tables(length)
    cosine = cosine[:, None, :]
    sine = sine[:, None, :]

    def rotate(values):
        return values * cosine + pair_swap(values) * sine

    def rotate_back(values):
        return values * cosine + pair_swap(values * sine)

    def fetch():
        gathered = (
            lax.all_gather(qkv_weight, "dp", axis=0, tiled=True),
            lax.all_gather(out_weight, "dp", axis=0, tiled=True),
            lax.all_gather(fc1_weight, "dp", axis=0, tiled=True),
            lax.all_gather(fc2_weight, "dp", axis=0, tiled=True),
        )
        return (gathered, gathered)

    def seq_gather(values):
        return lax.all_gather(values, "tensor", axis=0, tiled=True)

    def part_sum(values):
        return lax.psum_scatter(
            values.astype(jnp.bfloat16), "tensor", scatter_dimension=0, tiled=True
        ).astype(jnp.float32)

    def grad_gather(values):
        return lax.all_gather(values, "tensor", axis=0, tiled=True)

    def grad_sum(values):
        return lax.psum_scatter(
            values.astype(jnp.bfloat16), "tensor", scatter_dimension=0, tiled=True
        ).astype(jnp.float32)

    def forward(inputs, weights):
        (weight_qkv, weight_out, weight_up, weight_down), (
            whole_qkv,
            whole_out,
            whole_up,
            whole_down,
        ) = weights
        first_all = seq_gather(norm_rows(inputs, attn_gain, attn_shift).astype(jnp.bfloat16))
        packed = (
            jnp.dot(first_all, weight_qkv, preferred_element_type=jnp.float32) + qkv_bias
        ).reshape(length, local_heads, 3, HD)
        query = rotate(packed[:, :, 0]).astype(jnp.bfloat16)
        key_all = rotate(packed[:, :, 1]).astype(jnp.bfloat16)
        value_all = packed[:, :, 2].astype(jnp.bfloat16)
        outputs = []
        log_sums = []
        for block in range(block_count):
            query_block = query[block * block_rows : (block + 1) * block_rows]
            scores = (
                jnp.einsum("qhd,khd->hqk", query_block, key_all, preferred_element_type=jnp.float32)
                * factor
            )
            row_max = jnp.max(scores, axis=-1, keepdims=True)
            expo = jnp.exp(scores - row_max)
            row_total = jnp.sum(expo, axis=-1, keepdims=True)
            weights_low = (expo / row_total).astype(jnp.bfloat16)
            outputs.append(
                jnp.einsum(
                    "hqk,khd->qhd", weights_low, value_all, preferred_element_type=jnp.float32
                )
            )
            log_sums.append(row_max + jnp.log(row_total))
        heads_out = (
            jnp.concatenate(outputs, axis=0).reshape(length, local_heads * HD).astype(jnp.bfloat16)
        )
        log_total = jnp.concatenate(log_sums, axis=1)
        attended = part_sum(contract(heads_out, weight_out, 1, 1))
        resid = inputs + attended + out_bias
        second_all = seq_gather(norm_rows(resid, mlp_gain, mlp_shift).astype(jnp.bfloat16))
        hidden = jnp.dot(second_all, weight_up, preferred_element_type=jnp.float32) + fc1_bias
        act = exact_gelu(hidden).astype(jnp.bfloat16)
        branch = part_sum(contract(act, weight_down, 1, 1))
        result = resid + branch + fc2_bias
        kept = (
            first_all,
            query,
            key_all,
            value_all,
            log_total,
            heads_out,
            heads_out,
            resid,
            second_all,
            hidden,
            act,
        )
        return (result, kept)

    def backward(inputs, grad_low, kept, weights):
        (weight_qkv, weight_out, weight_up, weight_down), (
            whole_qkv,
            whole_out,
            whole_up,
            whole_down,
        ) = weights
        (
            first_all,
            query,
            key_all,
            value_all,
            log_total,
            heads_out,
            heads_rows,
            resid,
            second_all,
            hidden,
            act,
        ) = kept
        grad_top = grad_low.astype(jnp.float32)
        grad_fc2_bias = jnp.sum(grad_top, axis=0)
        grad_all = grad_gather(grad_low)
        grad_fc2_weight = contract(grad_all, act, 0, 0)
        grad_act = jnp.dot(grad_all, weight_down, preferred_element_type=jnp.float32)
        gelu_pull = jax.vjp(exact_gelu, hidden)[1]
        grad_hidden = gelu_pull(grad_act)[0].astype(jnp.bfloat16)
        grad_fc1_bias = jnp.sum(grad_hidden, axis=0, dtype=jnp.float32)
        grad_fc1_weight = contract(second_all, grad_hidden, 0, 0)
        grad_second = grad_sum(contract(grad_hidden, weight_up, 1, 1))
        second_pull = jax.vjp(norm_rows, resid, mlp_gain, mlp_shift)[1]
        grad_resid_norm, grad_mlp_gain, grad_mlp_shift = second_pull(grad_second)
        grad_resid = grad_top + grad_resid_norm
        grad_out_bias = jnp.sum(grad_resid, axis=0)
        resid_low = grad_resid.astype(jnp.bfloat16)
        resid_all = grad_gather(resid_low)
        grad_out_weight = contract(resid_all, heads_out, 0, 0)
        grad_heads = jnp.dot(resid_all, weight_out, preferred_element_type=jnp.float32).astype(
            jnp.bfloat16
        )
        grad_heads = grad_heads.reshape(length, local_heads, HD)
        grad_key = jnp.zeros((length, local_heads, HD), jnp.float32)
        grad_value = jnp.zeros((length, local_heads, HD), jnp.float32)
        query_grads = []
        for block in range(block_count):
            lower = block * block_rows
            upper = lower + block_rows
            query_block = query[lower:upper]
            grad_block = grad_heads[lower:upper]
            scores = (
                jnp.einsum("qhd,khd->hqk", query_block, key_all, preferred_element_type=jnp.float32)
                * factor
            )
            probs = jnp.exp(scores - log_total[:, lower:upper])
            grad_value = grad_value + jnp.einsum(
                "hqk,qhd->khd",
                probs.astype(jnp.bfloat16),
                grad_block,
                preferred_element_type=jnp.float32,
            )
            grad_probs = jnp.einsum(
                "qhd,khd->hqk", grad_block, value_all, preferred_element_type=jnp.float32
            )
            grad_scores = (
                probs * (grad_probs - jnp.sum(probs * grad_probs, axis=-1, keepdims=True))
            ).astype(jnp.bfloat16)
            query_grads.append(
                jnp.einsum("hqk,khd->qhd", grad_scores, key_all, preferred_element_type=jnp.float32)
                * factor
            )
            grad_key = (
                grad_key
                + jnp.einsum(
                    "hqk,qhd->khd", grad_scores, query_block, preferred_element_type=jnp.float32
                )
                * factor
            )
        grad_query = jnp.concatenate(query_grads, axis=0)
        grad_packed = jnp.stack(
            [rotate_back(grad_query), rotate_back(grad_key), grad_value], axis=2
        )
        grad_packed = grad_packed.reshape(length, packed_cols).astype(jnp.bfloat16)
        grad_qkv_bias = jnp.sum(grad_packed, axis=0, dtype=jnp.float32)
        grad_qkv_weight = contract(first_all, grad_packed, 0, 0)
        grad_first = grad_sum(contract(grad_packed, weight_qkv, 1, 1))
        first_pull = jax.vjp(norm_rows, inputs, attn_gain, attn_shift)[1]
        grad_input_norm, grad_attn_gain, grad_attn_shift = first_pull(grad_first)
        input_grad = grad_resid + grad_input_norm
        grads = (
            grad_attn_gain,
            grad_attn_shift,
            grad_qkv_weight,
            grad_qkv_bias,
            grad_out_weight,
            grad_out_bias,
            grad_mlp_gain,
            grad_mlp_shift,
            grad_fc1_weight,
            grad_fc1_bias,
            grad_fc2_weight,
            grad_fc2_bias,
        )
        return (input_grad, grads)

    def per_clip(totals, inputs_pair):
        clip_in, clip_grad = inputs_pair
        forward_weights = fetch()
        result, kept = forward(clip_in.astype(jnp.float32), forward_weights)
        backward_weights = fetch()
        input_grad, grads = backward(clip_in.astype(jnp.float32), clip_grad, kept, backward_weights)
        totals = tuple((left + right for left, right in zip(totals, grads)))
        return (totals, (result.astype(jnp.bfloat16), input_grad))

    out_cols = local_heads * HD
    start_totals = (
        jnp.zeros((width,), jnp.float32),
        jnp.zeros((width,), jnp.float32),
        jnp.zeros((width, packed_cols), jnp.float32),
        jnp.zeros((packed_cols,), jnp.float32),
        jnp.zeros((width, out_cols), jnp.float32),
        jnp.zeros((width,), jnp.float32),
        jnp.zeros((width,), jnp.float32),
        jnp.zeros((width,), jnp.float32),
        jnp.zeros((width, unit_cols), jnp.float32),
        jnp.zeros((unit_cols,), jnp.float32),
        jnp.zeros((width, unit_cols), jnp.float32),
        jnp.zeros((width,), jnp.float32),
    )
    totals, (output, input_grad) = lax.scan(per_clip, start_totals, (activations, cotangent))
    out_grad = totals[4]
    weight_sums = (
        lax.psum_scatter(
            totals[2].astype(jnp.bfloat16), "dp", scatter_dimension=0, tiled=True
        ).astype(jnp.float32),
        lax.psum_scatter(
            out_grad.astype(jnp.bfloat16), "dp", scatter_dimension=0, tiled=True
        ).astype(jnp.float32),
        lax.psum_scatter(
            totals[8].astype(jnp.bfloat16), "dp", scatter_dimension=0, tiled=True
        ).astype(jnp.float32),
        lax.psum_scatter(
            totals[10].astype(jnp.bfloat16), "dp", scatter_dimension=0, tiled=True
        ).astype(jnp.float32),
    )
    qkv_place = lax.dynamic_update_slice_in_dim(
        jnp.zeros((packed_cols * tensor_size,), jnp.float32),
        totals[3],
        tensor_rank * packed_cols,
        0,
    )
    unit_place = lax.dynamic_update_slice_in_dim(
        jnp.zeros((unit_cols * tensor_size,), jnp.float32), totals[9], tensor_rank * unit_cols, 0
    )
    summed = lax.psum(
        (totals[0], totals[1], qkv_place, totals[5], totals[6], totals[7], unit_place, totals[11]),
        ("dp", "tensor"),
    )
    grad_qkv_bias = lax.dynamic_slice_in_dim(summed[2], tensor_rank * packed_cols, packed_cols, 0)
    grad_fc1_bias = lax.dynamic_slice_in_dim(summed[6], tensor_rank * unit_cols, unit_cols, 0)
    return (
        output,
        input_grad,
        summed[0],
        summed[1],
        weight_sums[0],
        grad_qkv_bias,
        weight_sums[1],
        summed[3],
        summed[4],
        summed[5],
        weight_sums[2],
        grad_fc1_bias,
        weight_sums[3],
        summed[7],
    )


def lane_swap(values):
    even = lax.broadcasted_iota(jnp.int32, values.shape, 1) % 2 == 0
    return jnp.where(even, pltpu.roll(values, 127, 1), pltpu.roll(values, 1, 1))


def attend_kernel(first_ref, weight_ref, bias_ref, cos_ref, sin_ref, qkv_ref, heads_ref, turned_ref, log_ref):
    low = jnp.bfloat16
    packed = jnp.dot(first_ref[...], weight_ref[...], preferred_element_type=jnp.float32) + bias_ref[...]
    cosine, sine = cos_ref[...], sin_ref[...]

    def rotate(values):
        return values * cosine + lane_swap(values) * sine

    query = (rotate(packed[:, :128]).astype(low).astype(jnp.float32) * 0.125).astype(low)
    key = rotate(packed[:, 128:256]).astype(low)
    value = packed[:, 256:]
    qkv_ref[:, :128] = query
    qkv_ref[:, 128:256] = key
    qkv_ref[:, 256:] = value.astype(low)
    value = jnp.transpose(value).astype(low)
    first_head = lax.broadcasted_iota(jnp.int32, key.shape, 1) < HD
    for head in range(2):
        mine = slice(head * HD, (head + 1) * HD)
        key_here = jnp.where(first_head == (head == 0), key, jnp.zeros_like(key))
        scores = contract(key_here, query, 1, 1)
        top = jnp.max(scores, axis=0, keepdims=True)
        expo = jnp.exp(scores - top)
        total = jnp.sum(expo, axis=0, keepdims=True)
        summed = jnp.dot(value[mine], expo.astype(low), preferred_element_type=jnp.float32)
        turned_ref[0, mine] = summed / total
        log_ref[0, head : head + 1] = top + jnp.log(total)
    heads_ref[...] = jnp.transpose(turned_ref[0]).astype(low)


def attend(first, weight, bias, cosine, sine):
    length, width = first.shape
    pairs = weight.shape[1] // 384
    return pl.pallas_call(
        attend_kernel,
        grid=(pairs,),
        in_specs=[
            pl.BlockSpec((length, width), lambda i: (0, 0)),
            pl.BlockSpec((width, 384), lambda i: (0, i)),
            pl.BlockSpec((1, 384), lambda i: (0, i)),
            pl.BlockSpec((length, 128), lambda i: (0, 0)),
            pl.BlockSpec((length, 128), lambda i: (0, 0)),
        ],
        out_specs=[
            pl.BlockSpec((length, 384), lambda i: (0, i)),
            pl.BlockSpec((length, 128), lambda i: (0, i)),
            pl.BlockSpec((1, 128, length), lambda i: (i, 0, 0)),
            pl.BlockSpec((1, 2, length), lambda i: (i, 0, 0)),
        ],
        out_shape=[
            jax.ShapeDtypeStruct((length, 384 * pairs), jnp.bfloat16),
            jax.ShapeDtypeStruct((length, 128 * pairs), jnp.bfloat16),
            jax.ShapeDtypeStruct((pairs, 128, length), jnp.float32),
            jax.ShapeDtypeStruct((pairs, 2, length), jnp.float32),
        ],
        cost_estimate=pl.CostEstimate(flops=2 * 10**10, transcendentals=0, bytes_accessed=16 * 2**20),
        name="attend",
    )(first, weight, bias.reshape(1, -1), cosine, sine)


def attend_back_kernel(qkv_ref, grad_ref, turned_ref, log_ref, cos_ref, sin_ref, out_ref, bias_ref):
    low = jnp.bfloat16
    query = qkv_ref[:, :128]
    key = qkv_ref[:, 128:256]
    value = qkv_ref[:, 256:]
    grad = grad_ref[...]
    key_turned = jnp.transpose(key.astype(jnp.float32)).astype(low)
    product = jnp.transpose(grad.astype(jnp.float32)) * turned_ref[0]
    first_head = lax.broadcasted_iota(jnp.int32, key.shape, 1) < HD
    zero = jnp.zeros_like(key)
    query_grads, key_grads, value_grads = [], [], []
    for head in range(2):
        mine = slice(head * HD, (head + 1) * HD)
        here = first_head == (head == 0)
        delta = jnp.sum(product[mine], axis=0, keepdims=True)
        scores = contract(jnp.where(here, key, zero), query, 1, 1)
        probs = jnp.exp(scores - log_ref[0, head : head + 1])
        grad_probs = contract(jnp.where(here, value, zero), grad, 1, 1)
        grad_scores = (probs * (grad_probs - delta)).astype(low)
        value_grads.append(jnp.dot(probs.astype(low), grad, preferred_element_type=jnp.float32))
        key_grads.append(jnp.dot(grad_scores, query, preferred_element_type=jnp.float32))
        query_grads.append(jnp.dot(key_turned[mine], grad_scores, preferred_element_type=jnp.float32))
    cosine, sine = cos_ref[...], sin_ref[...]

    def rotate_back(values):
        return values * cosine + lane_swap(values * sine)

    parts = [
        rotate_back(jnp.transpose(jnp.concatenate(query_grads, axis=0)) * 0.125),
        rotate_back(jnp.where(first_head, key_grads[0], key_grads[1])),
        jnp.where(first_head, value_grads[0], value_grads[1]),
    ]
    for at, part in enumerate(parts):
        part = part.astype(low)
        out_ref[:, at * 128 : (at + 1) * 128] = part
        bias_ref[:, at * 128 : (at + 1) * 128] = jnp.sum(part.astype(jnp.float32), axis=0, keepdims=True)


def attend_back(qkv, grad, turned, logs, cosine, sine):
    length = qkv.shape[0]
    pairs = qkv.shape[1] // 384
    return pl.pallas_call(
        attend_back_kernel,
        grid=(pairs,),
        in_specs=[
            pl.BlockSpec((length, 384), lambda i: (0, i)),
            pl.BlockSpec((length, 128), lambda i: (0, i)),
            pl.BlockSpec((1, 128, length), lambda i: (i, 0, 0)),
            pl.BlockSpec((1, 2, length), lambda i: (i, 0, 0)),
            pl.BlockSpec((length, 128), lambda i: (0, 0)),
            pl.BlockSpec((length, 128), lambda i: (0, 0)),
        ],
        out_specs=[
            pl.BlockSpec((length, 384), lambda i: (0, i)),
            pl.BlockSpec((1, 384), lambda i: (0, i)),
        ],
        out_shape=[
            jax.ShapeDtypeStruct((length, 384 * pairs), jnp.bfloat16),
            jax.ShapeDtypeStruct((1, 384 * pairs), jnp.float32),
        ],
        cost_estimate=pl.CostEstimate(flops=27 * 10**9, transcendentals=0, bytes_accessed=16 * 2**20),
        name="attend_back",
    )(qkv, grad, turned, logs, cosine, sine)


def assemble_kernel(place_ref, own_ref, x_ref, y_ref, even_ref, odd_ref, *out_refs):
    rows = even_ref.shape[0]
    start = 0
    for out_ref in out_refs:
        cols = slice(start, start + out_ref.shape[1])
        start += out_ref.shape[1]
        for at, ref in enumerate((own_ref, x_ref, y_ref)):
            out_ref[pl.ds(pl.multiple_of((at ^ place_ref[0]) * 2 * rows, 2 * rows), 2 * rows)] = ref[:, cols]
        last = (3 ^ place_ref[0]) * 2 * rows
        out_ref[pl.ds(pl.multiple_of(last, rows), rows)] = even_ref[:, cols]
        out_ref[pl.ds(pl.multiple_of(last + rows, rows), rows)] = odd_ref[:, cols]


def assemble(place, pieces, widths):
    rows = pieces[3].shape[0]
    total = sum(widths)
    return pl.pallas_call(
        assemble_kernel,
        grid_spec=pltpu.PrefetchScalarGridSpec(
            num_scalar_prefetch=1,
            grid=(4,),
            in_specs=[pl.BlockSpec((item.shape[0], total), lambda i, place: (0, i)) for item in pieces],
            out_specs=[pl.BlockSpec((8 * rows, cols), lambda i, place: (0, i)) for cols in widths],
        ),
        out_shape=[jax.ShapeDtypeStruct((8 * rows, 4 * cols), jnp.bfloat16) for cols in widths],
        cost_estimate=pl.CostEstimate(flops=0, transcendentals=0, bytes_accessed=16 * 2**20),
        name="assemble",
    )(place, *pieces)


def deal_kernel(place_ref, *refs):
    in_refs, out_refs = refs[:-4], refs[-4:]
    rows = out_refs[0].shape[1]
    start = 0
    for ref in in_refs:
        cols = slice(start, start + ref.shape[1])
        start += ref.shape[1]
        for half, kept_ref, sent_ref, bit in ((0, out_refs[0], out_refs[1], 2), (1, out_refs[2], out_refs[3], 1)):
            for out_ref, from_bit in ((kept_ref, 0), (sent_ref, bit)):
                for at in range(2):
                    block = (at * (3 - bit) + from_bit) ^ place_ref[0]
                    first_row = pl.multiple_of((2 * block + half) * rows, rows)
                    out_ref[at, :, cols] = ref[pl.ds(first_row, rows)]


def deal(place, grads):
    rows = grads[0].shape[0] // 8
    widths = [item.shape[1] // 4 for item in grads]
    total = sum(widths)
    return pl.pallas_call(
        deal_kernel,
        grid_spec=pltpu.PrefetchScalarGridSpec(
            num_scalar_prefetch=1,
            grid=(4,),
            in_specs=[pl.BlockSpec((8 * rows, cols), lambda i, place: (0, i)) for cols in widths],
            out_specs=[pl.BlockSpec((2, rows, total), lambda i, place: (0, 0, i))] * 4,
        ),
        out_shape=[jax.ShapeDtypeStruct((2, rows, 4 * total), jnp.bfloat16)] * 4,
        cost_estimate=pl.CostEstimate(flops=0, transcendentals=0, bytes_accessed=16 * 2**20),
        name="deal",
    )(place, *grads)


def after(values, earlier):
    return lax.optimization_barrier((values, earlier))[0]


EVERY = ("y", "x", "core", "tensor")


def one_clip_per_chip(mesh):
    return mesh.shape["dp"] == 8 and mesh.shape["tensor"] == 4


def swap(values, axis, bit=1):
    return lax.ppermute(values, axis, [(i, i ^ bit) for i in range(4 if axis == "tensor" else 2)])


def clip_routes(back):
    routes = []
    for turn in range(2):
        pairs = []
        for column in range(4):
            for core in range(2):
                for place in range(4):
                    source = (2 * column + core) * 4 + place
                    target = (2 * column + place // 2) * 4 + 2 * core + (turn ^ (place % 2))
                    pairs.append((target, source) if back else (source, target))
        routes.append(pairs)
    return routes


def pick(flag, first, second):
    return jnp.where(flag, second, first)


def to_clips(values):
    odd = lax.axis_index("tensor") % 2 == 1
    arrived = []
    for turn, pairs in enumerate(clip_routes(False)):
        sent = pick(odd, values[turn], values[1 - turn])
        arrived.append(lax.ppermute(sent, EVERY, pairs))
    return arrived, jnp.concatenate(
        [pick(odd, arrived[0], arrived[1]), pick(odd, arrived[1], arrived[0])], axis=0
    )


def from_clips(values, wait=None):
    odd = lax.axis_index("tensor") % 2 == 1
    rows = values.shape[0] // 2
    arrived = []
    for turn, pairs in enumerate(clip_routes(True)):
        sent = pick(odd, values[turn * rows : (turn + 1) * rows], values[(1 - turn) * rows : (2 - turn) * rows])
        arrived.append(lax.ppermute(sent, EVERY, pairs))
    if wait is not None:
        arrived = after(arrived, wait)
    return jnp.stack([pick(odd, arrived[0], arrived[1]), pick(odd, arrived[1], arrived[0])])


def three_parts(values):
    high = lax.reduce_precision(values, 8, 7)
    rest = values - high
    middle = lax.reduce_precision(rest, 8, 7)
    low = rest - middle
    return jnp.stack([high, middle, low]).astype(jnp.bfloat16)


def clip_body(
    activations,
    cotangent,
    attn_gain,
    attn_shift,
    qkv_weight,
    qkv_bias,
    out_weight,
    out_bias,
    mlp_gain,
    mlp_shift,
    fc1_weight,
    fc1_bias,
    fc2_weight,
    fc2_bias,
):
    core, at_x, at_y, at_z = (lax.axis_index(name) for name in ("core", "x", "y", "tensor"))
    place = (2 * at_y + at_x).astype(jnp.int32).reshape(1)
    width = activations.shape[2]
    length = activations.shape[1] * 4
    half_rows = length // 2
    own_rows = qkv_weight.shape[0]
    half_heads = qkv_weight.shape[1] // (6 * HD)
    qkv_cols = half_heads * 3 * HD
    out_cols = out_weight.shape[1] // 2
    unit_cols = fc1_weight.shape[1] // 2
    low = jnp.bfloat16

    def first_half(values):
        return lax.slice_in_dim(values, 0, values.shape[-1] // 2, axis=values.ndim - 1)

    def second_half(values):
        return lax.slice_in_dim(values, values.shape[-1] // 2, values.shape[-1], axis=values.ndim - 1)

    def own_half(values):
        return pick(core == 1, first_half(values), second_half(values))

    def other_half(values):
        return pick(core == 1, second_half(values), first_half(values))

    def by_kind(values):
        lead = values.shape[:-1]
        split = values.reshape(lead + (2, half_heads, 3, HD))
        return jnp.swapaxes(split, -3, -2).reshape(values.shape)

    def by_head(values):
        lead = values.shape[:-1]
        split = values.reshape(lead + (2, 3, half_heads, HD))
        return jnp.swapaxes(split, -3, -2).reshape(values.shape)

    columns = (by_kind(qkv_weight), out_weight, fc1_weight, fc2_weight)
    mine = jnp.concatenate([own_half(item) for item in columns], axis=1)
    theirs = swap(jnp.concatenate([other_half(item) for item in columns], axis=1), "core")
    held = jnp.concatenate([pick(core == 1, mine, theirs), pick(core == 1, theirs, mine)], axis=0)

    def along_z(own, wait=None):
        one = swap(own, "tensor", 1)
        two = swap(own, "tensor", 2)
        two = two if wait is None else after(two, wait)
        return [own, one, two, swap(two, "tensor", 1)]

    def over_plane(blocks, wait=None):
        own = jnp.concatenate(blocks, axis=1)
        from_x, from_y = swap(own, "x"), swap(own, "y")
        if wait is not None:
            from_x, from_y = after((from_x, from_y), wait)
        return own, from_x, from_y, swap(from_y[:own_rows], "x"), swap(from_x[own_rows:], "y")

    lines = jnp.concatenate([own_half(by_kind(qkv_bias)), own_half(fc1_bias)])
    lines = jnp.pad(three_parts(lines), ((0, 0), (0, 3 * qkv_cols - lines.shape[0]))).reshape(9, qkv_cols)
    blocks = along_z(jnp.concatenate([held[:, :qkv_cols], lines, jnp.zeros((7, qkv_cols), low)], axis=0))
    tokens = to_clips(after(activations, (blocks[1], blocks[3])))[1].astype(jnp.float32)
    lines = jnp.stack([item[2 * own_rows : 2 * own_rows + 9] for item in blocks])
    lines = lines.astype(jnp.float32).reshape(4, 3, 3 * qkv_cols).sum(axis=1)
    bias_qkv = lines[:, :qkv_cols].reshape(-1)
    bias_up = lines[:, qkv_cols : qkv_cols + unit_cols].reshape(-1)
    blocks_up = along_z(after(held[:, qkv_cols : qkv_cols + out_cols + unit_cols], blocks[3]))
    pieces = over_plane([item[: 2 * own_rows] for item in blocks], blocks_up[1:3])
    (weight_qkv,) = assemble(place, pieces, [qkv_cols])
    blocks_down = along_z(after(held[:, qkv_cols + out_cols + unit_cols :], blocks_up[3]))
    weight_qkv = after(weight_qkv, blocks_down[1:3])

    def both_halves(values):
        other = swap(values, "core")
        return jnp.concatenate([pick(core == 1, values, other), pick(core == 1, other, values)], axis=0)

    def part_sum(values):
        halves = values.reshape((2, half_rows) + values.shape[1:])
        sent = pick(core == 1, halves[1], halves[0]).astype(low)
        return pick(core == 1, halves[0], halves[1]) + swap(sent, "core").astype(jnp.float32)

    cosine, sine = (jnp.concatenate([item, item], axis=1) for item in rotary_tables(length))

    first_all = both_halves(norm_rows(tokens, attn_gain, attn_shift).astype(low))
    qkv, heads_out, turned, log_total = attend(first_all, weight_qkv, bias_qkv, cosine, sine)

    blocks_up[0] = after(blocks_up[0], pieces[3:])
    pieces = over_plane(blocks_up, heads_out)
    pieces = pieces[:3] + after(pieces[3:], blocks_down[3])
    weight_out, weight_up = assemble(place, pieces, [out_cols, unit_cols])
    resid = tokens + part_sum(contract(heads_out, weight_out, 1, 1)) + out_bias
    second_all = both_halves(norm_rows(resid, mlp_gain, mlp_shift).astype(low))

    blocks_down[0] = after(blocks_down[0], pieces[3:])
    arrived, grad_own = to_clips(after(cotangent, blocks_down[3]))
    pieces = over_plane(blocks_down, second_all)

    second_all = after(second_all, (pieces[1:3], arrived))
    hidden = jnp.dot(second_all, weight_up, preferred_element_type=jnp.float32) + bias_up
    share = 0.5 + 0.5 * lax.erf(hidden * math.sqrt(0.5))
    act = (hidden * share).astype(low)
    slope = (share + hidden * jnp.exp(-0.5 * hidden * hidden) * (1.0 / math.sqrt(2.0 * math.pi))).astype(low)
    pieces = pieces[:3] + after(pieces[3:], act)
    (weight_down,) = assemble(place, pieces, [unit_cols])
    result = resid + part_sum(contract(act, weight_down, 1, 1)) + fc2_bias

    def to_core(total):
        kept = pick(core == 1, total[0], total[1])
        came = swap(pick(core == 1, total[1], total[0]), "core")
        return jnp.concatenate(
            [pick(core == 1, kept, came), pick(core == 1, came, kept)], axis=-1
        ).astype(jnp.float32)

    def dealt(*grads):
        return deal(place, [item.astype(low) for item in grads])

    def first_back(parts, wait):
        kept_even, sent_even, kept_odd, sent_odd = parts
        came = after((swap(sent_even, "y"), swap(sent_odd, "x")), wait)
        return kept_even + came[0], kept_odd + came[1]

    def second_back(even, odd, wait):
        came = after((swap(even[1], "x"), swap(odd[1], "y")), wait)
        return jnp.concatenate([even[0] + came[0], odd[0] + came[1]]), came

    def along_z_back(total, wait, later):
        cols = total.shape[1] // 4
        own, one, two, three = (total[:, at * cols : (at + 1) * cols] for at in range(4))
        one = swap(one, "tensor", 1)
        two = swap(two + after(swap(three, "tensor", 1), wait), "tensor", 2)
        one, two = after((one, two), later)
        return to_core((own + one + two).reshape(2, own_rows, cols))

    grad_top = grad_own.astype(jnp.float32)
    grad_all = both_halves(grad_own)
    sum_fc2_bias = jnp.sum(grad_top, axis=0)
    parts_fc2 = dealt(contract(grad_all, act, 0, 0))
    grad_act = jnp.dot(after(grad_all, parts_fc2), weight_down, preferred_element_type=jnp.float32)
    grad_hidden = (grad_act * slope.astype(jnp.float32)).astype(low)
    sum_fc1_bias = jnp.sum(grad_hidden, axis=0, dtype=jnp.float32)
    grad_second_part = contract(grad_hidden, weight_up, 1, 1)
    sent_fc2 = first_back(parts_fc2, grad_second_part)
    grad_second = part_sum(grad_second_part)
    second_pull = jax.vjp(norm_rows, resid, mlp_gain, mlp_shift)[1]
    grad_resid_norm, sum_mlp_gain, sum_mlp_shift = second_pull(grad_second)
    grad_resid = grad_top + grad_resid_norm
    sum_out_bias = jnp.sum(grad_resid, axis=0)
    resid_all = both_halves(grad_resid.astype(low))
    grad_fc1 = contract(after(second_all, sent_fc2[0]), grad_hidden, 0, 0)
    parts_up = dealt(contract(resid_all, heads_out, 0, 0), grad_fc1)
    grad_heads = jnp.dot(resid_all, weight_out, preferred_element_type=jnp.float32).astype(low)
    total_fc2, _ = second_back(*sent_fc2, grad_heads)
    grad_packed, sum_qkv_bias = attend_back(qkv, after(grad_heads, parts_up), turned, log_total, cosine, sine)
    output = from_clips(result.astype(low), grad_packed)
    sent_up = first_back(parts_up, grad_packed)
    parts_qkv = dealt(contract(after(first_all, sent_up), grad_packed, 0, 0))
    total_up, came_up = second_back(*sent_up, parts_qkv)
    grad_first_part = contract(after(grad_packed, came_up), weight_qkv, 1, 1)
    grad_first = part_sum(grad_first_part)
    first_pull = jax.vjp(norm_rows, tokens, attn_gain, attn_shift)[1]
    grad_input_norm, sum_attn_gain, sum_attn_shift = first_pull(grad_first)
    input_low = from_clips((grad_resid + grad_input_norm).astype(low))
    input_grad = input_low.astype(jnp.float32)

    grad_fc2_weight = along_z_back(total_fc2, parts_qkv, grad_first)
    both_weights = along_z_back(total_up, grad_first, input_low)
    cuts = both_weights.shape[1] // 2
    both_weights = [both_weights[:, :cuts], both_weights[:, cuts:]]
    grad_out_weight = jnp.concatenate([item[:, :out_cols] for item in both_weights], axis=1)
    grad_fc1_weight = jnp.concatenate([item[:, out_cols:] for item in both_weights], axis=1)
    sent_qkv = first_back(parts_qkv, grad_first)
    total, came_qkv = second_back(*sent_qkv, grad_first)
    grad_qkv_weight = by_head(along_z_back(total, grad_first, grad_first))

    def by_core(values):
        none = jnp.zeros_like(values)
        return [pick(core == 1, values, none), pick(core == 1, none, values)]

    def by_owner(values, cols):
        first, second, third, fourth = (values.reshape(-1)[at * cols : (at + 1) * cols] for at in range(4))
        odd = at_z % 2 == 1
        first, second = pick(odd, first, second), pick(odd, second, first)
        third, fourth = pick(odd, third, fourth), pick(odd, fourth, third)
        lower, upper = jnp.concatenate([first, second]), jnp.concatenate([third, fourth])
        far = at_z // 2 == 1
        return jnp.concatenate([pick(far, lower, upper), pick(far, upper, lower)])

    sums = [sum_attn_gain, sum_attn_shift, sum_out_bias, sum_mlp_gain, sum_mlp_shift, sum_fc2_bias]
    sums = jnp.concatenate(sums + by_core(by_owner(sum_qkv_bias, qkv_cols)) + by_core(by_owner(sum_fc1_bias, unit_cols)))
    stages = (("core", 1, sent_qkv), ("x", 1, None), ("y", 1, (came_qkv, input_low)), ("tensor", 1, None), ("tensor", 2, None))
    for axis, bit, earlier in stages:
        if earlier is not None:
            sums = after(sums, earlier)
        sums = sums + swap(sums, axis, bit)
    vectors = sums[: 6 * width].reshape(6, width)
    qkv_sums = sums[6 * width : 6 * width + 8 * qkv_cols].reshape(2, 4, qkv_cols)
    unit_sums = sums[6 * width + 8 * qkv_cols :].reshape(2, 4, unit_cols)

    def own_place(values):
        return lax.dynamic_index_in_dim(values, at_z, 1, keepdims=False).reshape(-1)

    return (
        output,
        input_grad,
        vectors[0],
        vectors[1],
        grad_qkv_weight,
        by_head(own_place(qkv_sums)),
        grad_out_weight,
        vectors[2],
        vectors[3],
        vectors[4],
        grad_fc1_weight,
        own_place(unit_sums),
        grad_fc2_weight,
        vectors[5],
    )


def solution(mesh):
    if one_clip_per_chip(mesh):
        plan, rows = clip_body, ("y", "x", "core")
        mesh = jax.sharding.Mesh(mesh.devices.reshape(2, 2, 2, 4), EVERY)
    else:
        plan, rows = body, "dp"
    tokens, matrix, columns = P(rows, "tensor", None), P(rows, "tensor"), P("tensor")
    params = (P(), P(), matrix, columns, matrix, P(), P(), P(), matrix, columns, matrix, P())
    both = (tokens, tokens) + params
    return jax.shard_map(plan, mesh=mesh, in_specs=both, out_specs=both, check_vma=False)
```
